512 devices in a mesh: prow: 32 (over x, z), pcol: 16 (over y, core).
Axes of the slice: x: 4, y: 8, z: 8, core: 2. Of those that a mesh axis runs over, the one named last changes fastest.
Arguments:
- matrix: float32 [8192, 12288], P('prow', 'pcol'), may hold values from -6 to 6
- pivots: int32 [512], replicated, may hold values from 128 to 8191, as said below
- lower_inverse: float32 [4, 128, 128], replicated, may hold values from -1 to 1, as said below
- upper_inverse: float32 [4, 128, 128], replicated, may hold values from -1 to 1, as said below
Outputs:
- factored: float32 [8192, 12288], P('prow', 'pcol')
The draws below stay inside these ranges and needn't reach their ends.
Inputs may be any that keep to these rules, and one draw needn't show every extreme that they name: For a column j of panel k (k * 128 <= j < (k + 1) * 128), pivots[j] lies in [(k + 1) * 128, 8192); the 128 pivots of one panel are distinct and include (k + 1) * 128 and 8191. Each lower_inverse[k] is unit lower triangular. Each upper_inverse[k] is upper triangular with a positive diagonal.
All inputs are finite; a program needn't handle non-finite values.
Results may differ from the reference program's by a relative error of at most 0.0003.
Values sent between devices are 32-bit elements; how exact they have to be, the bound alone decides.
No kernel may reach another device: no remote copies, remote signals or barrier semaphores. Data moves between devices by JAX's collectives and lax.ppermute only.
A program may use at most 64 MiB of HBM per device.

```python
import math
from functools import partial
import jax
import jax.numpy as jnp
from jax import lax

NB = 128
RB_DEV = 2
CB_DEV = 6
PANELS = 4
M_ROWS = 8192
N_COLS = 12288
N_PROW = 32
N_PCOL = 16


def draw_pivots(key, part):
    pieces = []
    for panel_index in range(PANELS):
        lowest = (panel_index + 1) * NB
        middle = jax.random.permutation(jax.random.fold_in(key, panel_index), M_ROWS - lowest - 2)[:NB - 2].astype(jnp.int32) + lowest + 1
        chosen = jnp.concatenate([jnp.array([lowest], jnp.int32), middle, jnp.array([M_ROWS - 1], jnp.int32)])
        shuffle = jax.random.permutation(jax.random.fold_in(key, 7919 + panel_index), NB)
        pieces.append(chosen[shuffle])
    return jnp.concatenate(pieces).astype(jnp.int32)


def draw_lower_inverse(key, part):
    samples = jnp.clip(jax.random.normal(key, (PANELS, NB, NB), jnp.float32), -3.0, 3.0)
    row_ids = jnp.arange(NB)[:, None]
    col_ids = jnp.arange(NB)[None, :]
    strict = jnp.where(row_ids > col_ids, samples * (1.0 / math.sqrt(NB)), 0.0)
    return (strict + jnp.where(row_ids == col_ids, 1.0, 0.0)).astype(jnp.float32)


def draw_upper_inverse(key, part):
    first_key = jax.random.fold_in(key, 11)
    second_key = jax.random.fold_in(key, 12)
    samples = jnp.clip(jax.random.normal(first_key, (PANELS, NB, NB), jnp.float32), -3.0, 3.0)
    diagonal = jnp.exp(jax.random.uniform(second_key, (PANELS, 1, NB), jnp.float32, math.log(0.01), math.log(0.03)))
    row_ids = jnp.arange(NB)[:, None]
    col_ids = jnp.arange(NB)[None, :]
    strict = jnp.where(row_ids < col_ids, samples * (0.02 / math.sqrt(NB)), 0.0)
    return (strict + jnp.where(row_ids == col_ids, diagonal, 0.0)).astype(jnp.float32)


def shard_levels(key, dims, cuts, least, largest):
    loudness, own = 1.0, jax.random.fold_in(key, 6)
    for axis_at, shards_of in cuts:
        heights = jnp.exp(jax.random.uniform(jax.random.fold_in(own, axis_at), (shards_of,), jnp.float32, least / len(cuts), largest / len(cuts)))
        loudness = loudness * jnp.repeat(heights, dims[axis_at] // shards_of).reshape([-1 if axis == axis_at else 1 for axis in range(len(dims))])
    return loudness


def normal_values(stream_key, extent, width, bound, shards=(), kind=jnp.bfloat16):
    values = jax.random.normal(stream_key, extent, jnp.float32) * width
    if len(shards) > 0:
        values = shard_levels(stream_key, extent, shards, -0.22, 0.18) * values
    return jnp.clip(values, min=-bound, max=bound).astype(kind)


def setup_inputs(seed: int = 0) -> dict:
    splits = jax.random.split(jax.random.key(seed), 5)
    matrix = normal_values(splits[0], (M_ROWS, N_COLS), 1.0, 6.0, ((0, 32), (1, 16)), jnp.float32)
    pivots = draw_pivots(jax.random.fold_in(splits[4], 71), 0)
    lower_inverse = draw_lower_inverse(jax.random.fold_in(splits[4], 71), 0)
    upper_inverse = draw_upper_inverse(jax.random.fold_in(splits[4], 71), 0)
    return dict(matrix=matrix, pivots=pivots, lower_inverse=lower_inverse, upper_inverse=upper_inverse)


def hdot(left, right):
    return jnp.dot(left, right, precision=lax.Precision.HIGHEST, preferred_element_type=jnp.float32)


def to_grid(matrix):
    shaped = matrix.reshape(N_PROW, RB_DEV, NB, N_PCOL, CB_DEV, NB)
    return shaped.transpose(1, 0, 2, 4, 3, 5).reshape(M_ROWS, N_COLS)


def from_grid(whole):
    shaped = whole.reshape(RB_DEV, N_PROW, NB, CB_DEV, N_PCOL, NB)
    return shaped.transpose(1, 0, 2, 4, 3, 5).reshape(M_ROWS, N_COLS)


def swap_step(first_row, pivots, offset, whole):
    target = (offset + first_row).astype(jnp.int32)
    partner = pivots[target].astype(jnp.int32)
    row_one = lax.dynamic_slice_in_dim(whole, target, 1, 0)
    row_two = lax.dynamic_slice_in_dim(whole, partner, 1, 0)
    whole = lax.dynamic_update_slice_in_dim(whole, row_two, target, 0)
    whole = lax.dynamic_update_slice_in_dim(whole, row_one, partner, 0)
    return whole


def reference(matrix, pivots, lower_inverse, upper_inverse):
    whole = to_grid(matrix)
    for panel_index in range(PANELS):
        first_row = panel_index * NB
        past_end = first_row + NB
        whole = lax.fori_loop(0, NB, partial(swap_step, first_row, pivots), whole)
        multipliers = hdot(whole[past_end:, first_row:past_end], upper_inverse[panel_index])
        upper_rows = hdot(lower_inverse[panel_index], whole[first_row:past_end, past_end:])
        whole = whole.at[past_end:, first_row:past_end].set(multipliers)
        whole = whole.at[first_row:past_end, past_end:].set(upper_rows)
        whole = whole.at[past_end:, past_end:].add(-hdot(multipliers, upper_rows))
    return from_grid(whole)
```

```python
import jax
import jax.numpy as jnp
from jax import lax
from jax.experimental import pallas as pl
from jax.experimental.pallas import tpu as pltpu
from jax.sharding import PartitionSpec as P

NB = 128
PANELS = 4
TOP = NB * PANELS
PROW = 32
PCOL = 16
ROWS = 256
COLS = 768
REST = COLS - NB
BF = jnp.bfloat16
F32 = jnp.float32
X_GROUPS = [[x * 8 + z for x in range(4)] for z in range(8)]
Z_GROUPS = [[x * 8 + z for z in range(8)] for x in range(4)]
VMEM = pl.BlockSpec(memory_space=pltpu.VMEM)
SMEM = pl.BlockSpec(memory_space=pltpu.SMEM)


def mm(left, right):
    return lax.dot_general(left, right, (((1,), (0,)), ((), ())), preferred_element_type=F32)


def split2(value):
    high = value.astype(BF)
    low = (value - high.astype(F32)).astype(BF)
    return high, low


def select_rows(onehot, value):
    first = value.astype(BF)
    rest = value - first.astype(F32)
    second = rest.astype(BF)
    third = (rest - second.astype(F32)).astype(BF)
    return mm(onehot, first) + mm(onehot, second) + mm(onehot, third)


def dot3(left, right):
    lh, ll = split2(left)
    rh, rl = split2(right)
    return mm(jnp.concatenate([lh, ll, lh], axis=1), jnp.concatenate([rh, rh, rl], axis=0))


def chase(rows, piv_row_ref, panels):
    lanes = lax.broadcasted_iota(jnp.int32, (rows.shape[0], NB), 1).astype(F32)
    for m in panels:
        equal = rows == piv_row_ref[m : m + 1, :]
        hit = jnp.sum(jnp.where(equal, lanes + float(m * NB + 1), 0.0), axis=1, keepdims=True)
        hit = hit.astype(jnp.int32)
        rows = jnp.where(hit > 0, hit - 1, rows)
    return rows


def pick_kernel(place_ref, piv_row_ref, piv_col_ref, a_ref, first_ref, rest_ref, origin_ref):
    prow = place_ref[0]
    lane = lax.broadcasted_iota(jnp.int32, (NB, ROWS), 1)
    for k in range(PANELS):
        rows = chase(piv_col_ref[k * NB : (k + 1) * NB, :], piv_row_ref, range(k - 1, -1, -1))
        owner = (rows >> 7) & 31
        slot = ((rows >> 12) << 7) | (rows & 127)
        slot = jnp.where(owner == prow, slot, -1)
        onehot = jnp.where(lane == slot, 1.0, 0.0).astype(BF)
        first_ref[k * NB : (k + 1) * NB, :] = select_rows(onehot, a_ref[:, :NB])
        rest_ref[k * NB : (k + 1) * NB, :] = select_rows(onehot, a_ref[:, NB:])
    local = lax.broadcasted_iota(jnp.int32, (ROWS, 1), 0)
    rows = ((local >> 7) * PROW + prow) * NB + (local & 127)
    rows = chase(rows, piv_row_ref, range(PANELS - 1, -1, -1))
    origin_ref[...] = jnp.broadcast_to(rows, (ROWS, NB))


def place_of(origin):
    unit = (origin >> 2) & 31
    return (unit << 5) + 16 + ((origin >> 7) << 2) + (origin & 3)


def moved_rows(origin, gathered, kept):
    lane = lax.broadcasted_iota(jnp.int32, (ROWS, 1024), 1)
    onehot = jnp.where(lane == jnp.where(origin < TOP, place_of(origin), -1), 1.0, 0.0).astype(BF)
    return jnp.where(origin < TOP, select_rows(onehot, gathered), kept)


def column_kernel(origin_ref, gathered_ref, a_ref, out_ref):
    origin = origin_ref[:, :1]
    for unit in range(PROW):
        out_ref[unit * 16 : unit * 16 + 16, :] = gathered_ref[unit * 32 : unit * 32 + 16, :]
    out_ref[TOP:, :] = moved_rows(origin, gathered_ref[...], a_ref[:, :NB])


def factor_kernel(
    place_ref, origin_ref, gathered_ref, a_ref, own_ref, near_ref, across_ref, pair_ref,
    lower_ref, upper_ref, out_ref, z_ref,
):
    prow = place_ref[0]
    pcol = place_ref[1]
    kind = pcol & 3

    def put(index, value):
        z_ref[:, pl.ds(pl.multiple_of(index * NB, NB), NB)] = value

    put(kind, near_ref[...])
    put(kind ^ 2, across_ref[...])
    put(kind ^ 1, pair_ref[:, :NB])
    put(kind ^ 3, pair_ref[:, NB:])
    z_ref[:, TOP : TOP + NB] = own_ref[...]
    for unit in range(PROW):
        z_ref[unit * 16 : unit * 16 + 16, TOP + NB :] = gathered_ref[unit * 32 : unit * 32 + 16, :]
    origin = origin_ref[:, :1]

    @pl.loop(0, REST // NB)
    def _(c):
        cols = pl.ds(pl.multiple_of(c * NB, NB), NB)
        shifted = pl.ds(pl.multiple_of(c * NB + NB, NB), NB)
        target = pl.ds(pl.multiple_of(c * NB + TOP + NB, NB), NB)
        z_ref[TOP:, target] = moved_rows(origin, gathered_ref[:, cols], a_ref[:, shifted])

    for k in range(PANELS):
        s = k * NB
        e = s + NB
        multipliers = dot3(z_ref[e:, s:e], upper_ref[k])
        z_ref[e:, s:e] = multipliers
        mh, ml = split2(multipliers)
        m3 = jnp.concatenate([mh, ml, mh], axis=1)
        lh, ll = split2(lower_ref[k])
        l3 = jnp.concatenate([lh, ll, lh], axis=1)

        @pl.loop(0, (TOP + COLS - e) // NB)
        def _(c):
            cols = pl.ds(pl.multiple_of(c * NB + e, NB), NB)
            bh, bl = split2(z_ref[s:e, cols])
            upper_rows = mm(l3, jnp.concatenate([bh, bh, bl], axis=0))
            z_ref[s:e, cols] = upper_rows
            uh, ul = split2(upper_rows)
            z_ref[e:, cols] = z_ref[e:, cols] - mm(m3, jnp.concatenate([uh, uh, ul], axis=0))

    out_ref[...] = z_ref[TOP:, TOP:]
    panel_cols = pl.ds(pl.multiple_of(kind * NB, NB), NB)
    top_rows = pl.ds(pl.multiple_of((prow & 3) * NB, NB), NB)

    @pl.when(pcol < PANELS)
    def _():
        out_ref[:, :NB] = z_ref[TOP:, panel_cols]

    @pl.when(prow < PANELS)
    def _():
        out_ref[:NB, :] = z_ref[top_rows, TOP:]

    @pl.when((prow < PANELS) & (pcol < PANELS))
    def _():
        out_ref[:NB, :NB] = z_ref[top_rows, panel_cols]


def exchange_first(picked, top):
    sent = jnp.concatenate([picked.reshape(PROW, 16, NB), top.reshape(PROW, 4, NB)], axis=1)
    got = lax.all_to_all(sent, "prow", 0, 0)
    chunk = jnp.concatenate([jnp.sum(got[:, :16], axis=0), got[:4, 16:].reshape(16, NB)], axis=0)
    sent = jnp.broadcast_to(chunk[None], (PROW, 32, NB))
    return lax.all_to_all(sent, "prow", 0, 0).reshape(PROW * 32, NB)


def exchange_rest(picked, top):
    sent = jnp.concatenate([picked.reshape(4, NB, REST), top.reshape(4, 32, REST)], axis=1)
    got = lax.all_to_all(sent, "prow", 0, 0, axis_index_groups=X_GROUPS)
    sent = jnp.concatenate(
        [jnp.sum(got[:, :NB], axis=0).reshape(8, 16, REST), got[0, NB:].reshape(8, 4, REST)], axis=1
    )
    got = lax.all_to_all(sent, "prow", 0, 0, axis_index_groups=Z_GROUPS)
    chunk = jnp.concatenate([jnp.sum(got[:, :16], axis=0), got[:4, 16:].reshape(16, REST)], axis=0)
    got = lax.all_to_all(
        jnp.broadcast_to(chunk[None], (8, 32, REST)), "prow", 0, 0, axis_index_groups=Z_GROUPS
    )
    got = got.reshape(256, REST)
    got = lax.all_to_all(
        jnp.broadcast_to(got[None], (4, 256, REST)), "prow", 0, 0, axis_index_groups=X_GROUPS
    )
    return got.reshape(PROW * 32, REST)


def spread_columns(own, pcol):
    up = lax.ppermute(own, "pcol", [(q, q + 4) for q in range(4)])
    down = lax.ppermute(own, "pcol", [(q, q + 12) for q in range(4)])
    near = jnp.where(pcol < 4, own, jnp.where(pcol < 8, up, down))
    half = near.shape[0] // 2
    left = lax.ppermute(near[:half], "pcol", [(q + 4, q + 8) for q in range(4)])
    right = lax.ppermute(near[half:], "pcol", [(q + 12, q + 8) for q in range(4)])
    far = (pcol >= 8) & (pcol < 12)
    near = jnp.where(far, jnp.concatenate([left, right], axis=0), near)
    across = lax.ppermute(near, "pcol", [(q, q ^ 2) for q in range(PCOL)])
    both = jnp.concatenate([near, across], axis=1)
    pair = lax.ppermute(both, "pcol", [(q, q ^ 1) for q in range(PCOL)])
    return near, across, pair


def per_device(matrix, pivots, lower_inverse, upper_inverse):
    prow = lax.axis_index("prow")
    pcol = lax.axis_index("pcol")
    place = jnp.stack([prow, pcol]).astype(jnp.int32)
    picked_first, picked_rest, origin = pl.pallas_call(
        pick_kernel,
        in_specs=[SMEM, VMEM, VMEM, VMEM],
        out_specs=[VMEM] * 3,
        out_shape=[
            jax.ShapeDtypeStruct((TOP, NB), F32),
            jax.ShapeDtypeStruct((TOP, REST), F32),
            jax.ShapeDtypeStruct((ROWS, NB), jnp.int32),
        ],
    )(place, pivots.reshape(PANELS, NB), pivots.reshape(TOP, 1), matrix)
    gathered_first = exchange_first(picked_first, matrix[:NB, :NB])
    own = pl.pallas_call(
        column_kernel,
        in_specs=[VMEM] * 3,
        out_specs=VMEM,
        out_shape=jax.ShapeDtypeStruct((TOP + ROWS, NB), F32),
    )(origin, gathered_first, matrix)
    near, across, pair = spread_columns(own, pcol)
    gathered_rest = exchange_rest(picked_rest, matrix[:NB, NB:])
    return pl.pallas_call(
        factor_kernel,
        in_specs=[SMEM] + [VMEM] * 9,
        out_specs=VMEM,
        out_shape=jax.ShapeDtypeStruct((ROWS, COLS), F32),
        scratch_shapes=[pltpu.VMEM((TOP + ROWS, TOP + COLS), F32)],
    )(place, origin, gathered_rest, matrix, own, near, across, pair, lower_inverse, upper_inverse)


def solution(mesh):
    in_specs = (P("prow", "pcol"), P(), P(), P())
    out_specs = P("prow", "pcol")
    return jax.shard_map(
        per_device, mesh=mesh, in_specs=in_specs, out_specs=out_specs, check_vma=False
    )
```

```python
import jax
import jax.numpy as jnp
from jax import lax
from jax.experimental import pallas as pl
from jax.experimental.pallas import tpu as pltpu
from jax.sharding import PartitionSpec as P

NB = 128
PANELS = 4
TOP = NB * PANELS
PROW = 32
PCOL = 16
ROWS = 256
COLS = 768
REST = COLS - NB
BF = jnp.bfloat16
F32 = jnp.float32
X_GROUPS = [[x * 8 + z for x in range(4)] for z in range(8)]
Z_GROUPS = [[x * 8 + z for z in range(8)] for x in range(4)]
VMEM = pl.BlockSpec(memory_space=pltpu.VMEM)
SMEM = pl.BlockSpec(memory_space=pltpu.SMEM)


def mm(left, right):
    return lax.dot_general(left, right, (((1,), (0,)), ((), ())), preferred_element_type=F32)


def split2(value):
    high = value.astype(BF)
    low = (value - high.astype(F32)).astype(BF)
    return high, low


def select_rows(onehot, value):
    first = value.astype(BF)
    rest = value - first.astype(F32)
    second = rest.astype(BF)
    third = (rest - second.astype(F32)).astype(BF)
    return mm(onehot, first) + mm(onehot, second) + mm(onehot, third)


def dot3(left, right):
    lh, ll = split2(left)
    rh, rl = split2(right)
    return mm(jnp.concatenate([lh, ll, lh], axis=1), jnp.concatenate([rh, rh, rl], axis=0))


def chase(rows, piv_row_ref, panels):
    lanes = lax.broadcasted_iota(jnp.int32, (rows.shape[0], NB), 1).astype(F32)
    for m in panels:
        equal = rows == piv_row_ref[m : m + 1, :]
        hit = jnp.sum(jnp.where(equal, lanes + float(m * NB + 1), 0.0), axis=1, keepdims=True)
        hit = hit.astype(jnp.int32)
        rows = jnp.where(hit > 0, hit - 1, rows)
    return rows


def pick_kernel(place_ref, piv_row_ref, piv_col_ref, a_ref, first_ref, rest_ref, origin_ref):
    prow = place_ref[0]
    lane = lax.broadcasted_iota(jnp.int32, (NB, ROWS), 1)
    for k in range(PANELS):
        rows = chase(piv_col_ref[k * NB : (k + 1) * NB, :], piv_row_ref, range(k - 1, -1, -1))
        owner = (rows >> 7) & 31
        slot = ((rows >> 12) << 7) | (rows & 127)
        slot = jnp.where(owner == prow, slot, -1)
        onehot = jnp.where(lane == slot, 1.0, 0.0).astype(BF)
        first_ref[k * NB : (k + 1) * NB, :] = select_rows(onehot, a_ref[:, :NB])
        rest_ref[k * NB : (k + 1) * NB, :] = select_rows(onehot, a_ref[:, NB:])
    local = lax.broadcasted_iota(jnp.int32, (ROWS, 1), 0)
    rows = ((local >> 7) * PROW + prow) * NB + (local & 127)
    rows = chase(rows, piv_row_ref, range(PANELS - 1, -1, -1))
    origin_ref[...] = jnp.broadcast_to(rows, (ROWS, NB))


def place_of(origin):
    unit = (origin >> 2) & 31
    return (unit << 5) + 16 + ((origin >> 7) << 2) + (origin & 3)


def moved_rows(origin, gathered, kept):
    lane = lax.broadcasted_iota(jnp.int32, (ROWS, 1024), 1)
    onehot = jnp.where(lane == jnp.where(origin < TOP, place_of(origin), -1), 1.0, 0.0).astype(BF)
    return jnp.where(origin < TOP, select_rows(onehot, gathered), kept)


def column_kernel(origin_ref, gathered_ref, a_ref, out_ref):
    origin = origin_ref[:, :1]
    for unit in range(PROW):
        out_ref[unit * 16 : unit * 16 + 16, :] = gathered_ref[unit * 32 : unit * 32 + 16, :]
    out_ref[TOP:, :] = moved_rows(origin, gathered_ref[...], a_ref[:, :NB])


def exchange_first(picked, top):
    sent = jnp.concatenate([picked.reshape(PROW, 16, NB), top.reshape(PROW, 4, NB)], axis=1)
    got = lax.all_to_all(sent, "prow", 0, 0)
    chunk = jnp.concatenate([jnp.sum(got[:, :16], axis=0), got[:4, 16:].reshape(16, NB)], axis=0)
    sent = jnp.broadcast_to(chunk[None], (PROW, 32, NB))
    return lax.all_to_all(sent, "prow", 0, 0).reshape(PROW * 32, NB)


def exchange_rest(picked, top):
    sent = jnp.concatenate([picked.reshape(4, NB, REST), top.reshape(4, 32, REST)], axis=1)
    got = lax.all_to_all(sent, "prow", 0, 0, axis_index_groups=X_GROUPS)
    sent = jnp.concatenate(
        [jnp.sum(got[:, :NB], axis=0).reshape(8, 16, REST), got[0, NB:].reshape(8, 4, REST)], axis=1
    )
    got = lax.all_to_all(sent, "prow", 0, 0, axis_index_groups=Z_GROUPS)
    chunk = jnp.concatenate([jnp.sum(got[:, :16], axis=0), got[:4, 16:].reshape(16, REST)], axis=0)
    got = lax.all_to_all(
        jnp.broadcast_to(chunk[None], (8, 32, REST)), "prow", 0, 0, axis_index_groups=Z_GROUPS
    )
    got = got.reshape(256, REST)
    got = lax.all_to_all(
        jnp.broadcast_to(got[None], (4, 256, REST)), "prow", 0, 0, axis_index_groups=X_GROUPS
    )
    return got.reshape(PROW * 32, REST)


def spread_start(own):
    up = lax.ppermute(own, "pcol", [(q, q + 4) for q in range(4)])
    down = lax.ppermute(own, "pcol", [(q, q + 12) for q in range(4)])
    return up, down


def spread_columns(own, pcol):
    return spread_rest(own, *spread_start(own), pcol)


def spread_rest(own, up, down, pcol):
    near = jnp.where(pcol < 4, own, jnp.where(pcol < 8, up, down))
    half = near.shape[0] // 2
    left = lax.ppermute(near[:half], "pcol", [(q + 4, q + 8) for q in range(4)])
    right = lax.ppermute(near[half:], "pcol", [(q + 12, q + 8) for q in range(4)])
    far = (pcol >= 8) & (pcol < 12)
    near = jnp.where(far, jnp.concatenate([left, right], axis=0), near)
    across = lax.ppermute(near, "pcol", [(q, q ^ 2) for q in range(PCOL)])
    both = jnp.concatenate([near, across], axis=1)
    pair = lax.ppermute(both, "pcol", [(q, q ^ 1) for q in range(PCOL)])
    return near, across, pair


def lane_sum(mask, value):
    return jnp.sum(jnp.where(mask, value, 0.0), axis=1, keepdims=True)


def sub_sum(mask, value):
    return jnp.sum(jnp.where(mask, value, 0.0), axis=0, keepdims=True).astype(jnp.int32)


def iota(shape, axis):
    return lax.broadcasted_iota(jnp.int32, shape, axis)


def ranks(masks):
    count = len(masks)
    padded = -(-count // 8) * 8
    rows = [jnp.where(mask, 1.0, 0.0) for mask in masks]
    rows = rows + [jnp.zeros((1, NB), F32)] * (padded - count)
    before = jnp.where(iota((NB, NB), 0) < iota((NB, NB), 1), 1.0, 0.0).astype(BF)
    found = mm(jnp.concatenate(rows, axis=0).astype(BF), before)
    return [found[n : n + 1, :] for n in range(count)]


def slots(mask, rank, value, capacity):
    row = iota((capacity, NB), 0).astype(F32)
    return lane_sum(mask & (rank == row), value + 1.0).astype(jnp.int32) - 1


def onehot_of(column, width):
    return jnp.where(iota((column.shape[0], width), 1) == column, 1.0, 0.0).astype(BF)


def plan_kernel(pivots_ref, a_ref, send_ref, plan_ref, over_ref, source_ref, target_ref):
    prow = lax.axis_index("prow")
    x = prow >> 3
    z = prow & 7
    sub = iota((NB, NB), 0)
    lane = iota((NB, NB), 1)
    subf = sub.astype(F32)
    lane_row = iota((1, NB), 1)
    piv_row = [pivots_ref[m : m + 1, :] for m in range(PANELS)]
    piv_col = []
    for m in range(PANELS):
        piv_col.append(lane_sum(sub == lane, piv_row[m].astype(F32)).astype(jnp.int32))

    def met(m, rows):
        return sub_sum(piv_col[m] == rows, subf + float(m * NB + 1))

    source = []
    target = []
    for k in range(PANELS):
        rows = piv_row[k]
        for m in range(k - 1, -1, -1):
            hit = met(m, rows)
            rows = jnp.where(hit > 0, hit - 1, rows)
        source.append(rows)
        source_ref[k : k + 1, :] = rows
        rows = lane_row + k * NB
        for m in range(PANELS):
            if m == k:
                rows = jnp.where(rows == lane_row + k * NB, piv_row[k], rows)
                continue
            hit = met(m, rows)
            moved = jnp.where(hit > 0, hit - 1, rows)
            if m > k:
                look = sub_sum(sub + m * NB == rows, piv_col[m].astype(F32))
                moved = jnp.where(look > 0, look, moved)
            rows = moved
        target.append(rows)
        target_ref[k : k + 1, :] = rows

    def local_of(rows):
        return ((rows >> 12) << 7) | (rows & 127)

    def owner_of(rows):
        return (rows >> 7) & 31

    masks = [owner_of(source[k]) == prow for k in range(PANELS)]
    order = ranks(masks)
    pieces = [
        slots(masks[k], order[k], local_of(source[k]).astype(F32), 16) for k in range(PANELS)
    ]
    mine = target_ref[pl.ds(prow & 3, 1), :]
    leaves = (mine >= TOP) & (prow < PANELS)
    masks = [leaves & (((mine >> 10) & 3) == n) for n in range(4)]
    order = ranks(masks)
    lanef = lane_row.astype(F32)
    chosen = []
    for n in range(4):
        chosen.append(pieces[n])
        chosen.append(slots(masks[n], order[n], lanef, 48))
    send_ref[...] = select_rows(onehot_of(jnp.concatenate(chosen, axis=0), ROWS), a_ref[...])

    panel = source_ref[pl.ds(x, 1), :]
    panel_z = (panel >> 7) & 7
    panel_x = (panel >> 10) & 3
    here = panel_z == z
    masks = [here & (panel_x == n) for n in range(4)] + [here]
    order = ranks(masks)
    spot = jnp.zeros((1, NB), F32)
    for n in range(4):
        spot = spot + jnp.where(masks[n], order[n] + 64.0 * n, 0.0)
    wide = lambda column: jnp.broadcast_to(column, (column.shape[0], NB))
    plan_ref[0:32, :] = wide(slots(here, order[4], spot, 32))
    other = target_ref[pl.ds(z & 3, 1), :]
    along = (other >= TOP) & (z < PANELS) & (((other >> 10) & 3) == x)
    masks = [along & (((other >> 7) & 7) == n) for n in range(8)] + [along]
    order = ranks(masks)
    for n in range(8):
        plan_ref[32 + 16 * n : 48 + 16 * n, :] = wide(slots(masks[n], order[n], order[8], 16))
    zf = panel_z.astype(F32)
    zcol = lane_sum(sub == lane, zf)
    ahead = lane_sum((zf == zcol) & (lane < sub), 1.0)
    plan_ref[160:288, :] = wide((zcol * 32.0 + ahead).astype(jnp.int32))
    masks = [(target[k] >= TOP) & (owner_of(target[k]) == prow) for k in range(PANELS)]
    order = ranks(masks)
    row = iota((ROWS, NB), 0)
    total = jnp.zeros((ROWS, 1), F32)
    for k in range(PANELS):
        total = total + lane_sum(masks[k] & (local_of(target[k]) == row), order[k] + (16.0 * k + 1.0))
    plan_ref[288:544, :] = wide(total.astype(jnp.int32) - 1)
    unit = iota((PROW, NB), 0)
    over = jnp.zeros((PROW, 1), F32)
    for k in range(PANELS):
        leaves = target[k] >= TOP
        for mask, cap in (
            (owner_of(source[k]) == unit, 16.0),
            (((source[k] >> 7) & 7) == unit, 32.0),
            (leaves & (((target[k] >> 10) & 3) == unit), 48.0),
            (leaves & (owner_of(target[k]) == unit), 16.0),
        ):
            over = jnp.maximum(over, lane_sum(mask, 1.0) - cap)
    over = jnp.max(over, axis=0, keepdims=True)
    over_ref[...] = jnp.broadcast_to(over, (8, NB)).astype(jnp.int32)


def turn_kernel(plan_ref, got_ref, send_ref):
    got = got_ref[...].reshape(256, COLS)
    rows = select_rows(onehot_of(plan_ref[0:32, :1], 256), got)
    moved = plan_ref[32:160, :1]
    moved = jnp.where(moved < 0, -1, moved + 16)
    sent = select_rows(onehot_of(moved, 64), got[:64])
    for n in range(8):
        send_ref[n, 0:32, :] = rows
        send_ref[n, 32:48, :] = sent[n * 16 : n * 16 + 16]


def panel_kernel(plan_ref, got_ref, send_ref, lead_ref):
    got = jnp.concatenate([got_ref[n, 0:32, :] for n in range(8)], axis=0)
    rows = select_rows(onehot_of(plan_ref[160:288, :1], 256), got)
    for n in range(4):
        send_ref[n] = rows
        lead_ref[NB + n * 16 : NB + n * 16 + 16, :] = got_ref[n, 32:48, :NB]
    lead_ref[0:NB, :] = rows[:, :NB]


def put_columns(near_ref, across_ref, pair_ref, rows, store):
    kind = lax.axis_index("pcol") & 3
    store(kind, near_ref[rows, :])
    store(kind ^ 2, across_ref[rows, :])
    store(kind ^ 1, pair_ref[rows, :NB])
    store(kind ^ 3, pair_ref[rows, NB:])


def lane_block(index):
    return pl.ds(pl.multiple_of(index * NB, NB), NB)


def corner_kernel(near_ref, across_ref, pair_ref, send_ref, moved_ref):
    def store_send(index, value):
        for n in range(4):
            send_ref[n, :, lane_block(index)] = value

    def store_moved(index, value):
        moved_ref[:, lane_block(index)] = value

    put_columns(near_ref, across_ref, pair_ref, slice(0, NB), store_send)
    put_columns(near_ref, across_ref, pair_ref, slice(NB, NB + 64), store_moved)


def rows_kernel(plan_ref, got_ref, moved_ref, a_ref, near_ref, across_ref, pair_ref, out_ref):
    slot = plan_ref[288:544, :1]
    onehot = onehot_of(slot, 64)

    def store(index, value):
        out_ref[:, lane_block(index)] = value

    put_columns(near_ref, across_ref, pair_ref, slice(0, ROWS), store)
    out_ref[:, TOP:] = a_ref[...]
    moved = jnp.concatenate([got_ref[n, 32:48, :] for n in range(4)], axis=0)
    moved = jnp.concatenate([moved_ref[...], moved], axis=1)
    out_ref[...] = jnp.where(slot >= 0, select_rows(onehot, moved), out_ref[...])


def factor_kernel(corner_ref, own_ref, rows_ref, lower_ref, upper_ref, out_ref, z_ref, y_ref, m_ref, u_ref):
    prow = lax.axis_index("prow")
    pcol = lax.axis_index("pcol")
    z_ref[:TOP, :] = corner_ref[...]
    z_ref[TOP:, :] = rows_ref[:, :TOP]
    for k in range(PANELS):
        s = k * NB
        e = s + NB
        before = own_ref if k == 0 else y_ref
        multipliers = dot3(z_ref[e:, s:e], upper_ref[k])
        z_ref[e:, s:e] = multipliers
        mh, ml = split2(multipliers)
        m3 = jnp.concatenate([mh, ml, mh], axis=1)
        m_ref[:, 3 * s : 3 * e] = m3[TOP - e :]
        lh, ll = split2(lower_ref[k])
        l3 = jnp.concatenate([lh, ll, lh], axis=1)
        if e < TOP:
            bh, bl = split2(z_ref[s:e, e:])
            corner = mm(l3, jnp.concatenate([bh, bh, bl], axis=0))
            z_ref[s:e, e:] = corner
            uh, ul = split2(corner)
            z_ref[e:, e:] = z_ref[e:, e:] - mm(m3, jnp.concatenate([uh, uh, ul], axis=0))
        bh, bl = split2(before[s:e, :])
        upper_rows = mm(l3, jnp.concatenate([bh, bh, bl], axis=0))
        y_ref[s:e, :] = upper_rows
        uh, ul = split2(upper_rows)
        u3 = jnp.concatenate([uh, uh, ul], axis=0)
        u_ref[3 * s : 3 * e, :] = u3
        if e < TOP:
            y_ref[e:TOP, :] = before[e:TOP, :] - mm(m3[: TOP - e], u3)
    out_ref[...] = rows_ref[:, TOP:] - mm(m_ref[...], u_ref[...])
    panel_cols = lane_block(pcol & 3)
    top_rows = pl.ds(pl.multiple_of((prow & 3) * NB, NB), NB)

    @pl.when(pcol < PANELS)
    def _():
        out_ref[:, :NB] = z_ref[TOP:, panel_cols]

    @pl.when(prow < PANELS)
    def _():
        out_ref[:NB, :] = y_ref[top_rows, :]

    @pl.when((prow < PANELS) & (pcol < PANELS))
    def _():
        out_ref[:NB, :NB] = z_ref[top_rows, panel_cols]


def kernel_call(body, shapes, scratch=()):
    def call(*args):
        return pl.pallas_call(
            body,
            in_specs=[VMEM] * len(args),
            out_specs=[VMEM] * len(shapes),
            out_shape=[jax.ShapeDtypeStruct(shape, kind) for shape, kind in shapes],
            scratch_shapes=list(scratch),
        )(*args)

    return call


def factor(corner, own, rows, lower_inverse, upper_inverse):
    return pl.pallas_call(
        factor_kernel,
        in_specs=[VMEM] * 5,
        out_specs=VMEM,
        out_shape=jax.ShapeDtypeStruct((ROWS, COLS), F32),
        scratch_shapes=[
            pltpu.VMEM((TOP + ROWS, TOP), F32),
            pltpu.VMEM((TOP, COLS), F32),
            pltpu.VMEM((ROWS, 3 * TOP), BF),
            pltpu.VMEM((3 * TOP, COLS), BF),
        ],
    )(corner, own, rows, lower_inverse, upper_inverse)


def along(value, groups):
    return lax.all_to_all(value, "prow", 0, 0, axis_index_groups=groups)


def slotted(send, plan, matrix, lower_inverse, upper_inverse):
    pcol = lax.axis_index("pcol")
    block = matrix[:, :NB]
    ends = spread_start(block)
    got = along(send.reshape(4, 64, COLS), X_GROUPS)
    got, ends = lax.optimization_barrier((got, ends))
    (send,) = kernel_call(turn_kernel, [((8, 48, COLS), F32)])(plan, got)
    raw = spread_rest(block, *ends, pcol)
    got = along(send, Z_GROUPS)
    got, raw = lax.optimization_barrier((got, raw))
    send, lead = kernel_call(panel_kernel, [((4, NB, COLS), F32), ((NB + 64, NB), F32)])(plan, got)
    own = along(send, X_GROUPS).reshape(TOP, COLS)
    near, across, pair = spread_columns(lead, pcol)
    send, moved = kernel_call(corner_kernel, [((4, NB, TOP), F32), ((64, TOP), F32)])(
        near, across, pair
    )
    corner = along(send, X_GROUPS).reshape(TOP, TOP)
    (rows,) = kernel_call(rows_kernel, [((ROWS, TOP + COLS), F32)])(
        plan, got, moved, matrix, *raw
    )
    return factor(corner, own, rows, lower_inverse, upper_inverse)


def dense_rows_kernel(
    origin_ref, gathered_ref, a_ref, own_ref, near_ref, across_ref, pair_ref, corner_ref, top_ref, out_ref
):
    def store_corner(index, value):
        corner_ref[:, lane_block(index)] = value

    def store_rows(index, value):
        out_ref[:, lane_block(index)] = value

    put_columns(near_ref, across_ref, pair_ref, slice(0, TOP), store_corner)
    put_columns(near_ref, across_ref, pair_ref, slice(TOP, TOP + ROWS), store_rows)
    top_ref[:, :NB] = own_ref[:TOP, :]
    out_ref[:, TOP : TOP + NB] = own_ref[TOP:, :]
    for unit in range(PROW):
        top_ref[unit * 16 : unit * 16 + 16, NB:] = gathered_ref[unit * 32 : unit * 32 + 16, :]
    origin = origin_ref[:, :1]

    @pl.loop(0, REST // NB)
    def _(c):
        out_ref[:, lane_block(c + PANELS + 1)] = moved_rows(
            origin, gathered_ref[:, lane_block(c)], a_ref[:, lane_block(c + 1)]
        )


def dense(pivots, matrix, lower_inverse, upper_inverse):
    prow = lax.axis_index("prow")
    pcol = lax.axis_index("pcol")
    place = jnp.stack([prow, pcol]).astype(jnp.int32)
    picked_first, picked_rest, origin = pl.pallas_call(
        pick_kernel,
        in_specs=[SMEM, VMEM, VMEM, VMEM],
        out_specs=[VMEM] * 3,
        out_shape=[
            jax.ShapeDtypeStruct((TOP, NB), F32),
            jax.ShapeDtypeStruct((TOP, REST), F32),
            jax.ShapeDtypeStruct((ROWS, NB), jnp.int32),
        ],
    )(place, pivots.reshape(PANELS, NB), pivots.reshape(TOP, 1), matrix)
    gathered_first = exchange_first(picked_first, matrix[:NB, :NB])
    (own,) = kernel_call(column_kernel, [((TOP + ROWS, NB), F32)])(origin, gathered_first, matrix)
    near, across, pair = spread_columns(own, pcol)
    gathered_rest = exchange_rest(picked_rest, matrix[:NB, NB:])
    corner, top, rows = kernel_call(
        dense_rows_kernel,
        [((TOP, TOP), F32), ((TOP, COLS), F32), ((ROWS, TOP + COLS), F32)],
    )(origin, gathered_rest, matrix, own, near, across, pair)
    return factor(corner, top, rows, lower_inverse, upper_inverse)


def per_device(matrix, pivots, lower_inverse, upper_inverse):
    send, plan, over = kernel_call(
        plan_kernel,
        [((256, COLS), F32), ((544, NB), jnp.int32), ((8, NB), jnp.int32)],
        [pltpu.VMEM((8, NB), jnp.int32), pltpu.VMEM((8, NB), jnp.int32)],
    )(pivots.reshape(PANELS, NB), matrix)
    return lax.cond(
        over[0, 0] <= 0,
        lambda: slotted(send, plan, matrix, lower_inverse, upper_inverse),
        lambda: dense(pivots, matrix, lower_inverse, upper_inverse),
    )


def solution(mesh):
    in_specs = (P("prow", "pcol"), P(), P(), P())
    out_specs = P("prow", "pcol")
    return jax.shard_map(
        per_device, mesh=mesh, in_specs=in_specs, out_specs=out_specs, check_vma=False
    )
```

```python
import jax
import jax.numpy as jnp
from jax import lax
from jax.experimental import pallas as pl
from jax.experimental.pallas import tpu as pltpu
from jax.sharding import PartitionSpec as P

NB = 128
PANELS = 4
TOP = NB * PANELS
PROW = 32
PCOL = 16
ROWS = 256
COLS = 768
REST = COLS - NB
WIDE = TOP + COLS
KERNEL_VMEM = 20 << 20
FACTOR_VMEM = 28 << 20
BF = jnp.bfloat16
F32 = jnp.float32
X_GROUPS = [[x * 8 + z for x in range(4)] for z in range(8)]
Z_GROUPS = [[x * 8 + z for z in range(8)] for x in range(4)]
VMEM = pl.BlockSpec(memory_space=pltpu.VMEM)
SMEM = pl.BlockSpec(memory_space=pltpu.SMEM)


def mm(left, right):
    return lax.dot_general(left, right, (((1,), (0,)), ((), ())), preferred_element_type=F32)


def split2(value):
    high = value.astype(BF)
    low = (value - high.astype(F32)).astype(BF)
    return high, low


def select_rows(onehot, value):
    first = value.astype(BF)
    rest = value - first.astype(F32)
    second = rest.astype(BF)
    third = (rest - second.astype(F32)).astype(BF)
    return mm(onehot, first) + mm(onehot, second) + mm(onehot, third)


def dot3(left, right):
    lh, ll = split2(left)
    rh, rl = split2(right)
    return mm(jnp.concatenate([lh, ll, lh], axis=1), jnp.concatenate([rh, rh, rl], axis=0))


def chase(rows, piv_row_ref, panels):
    lanes = lax.broadcasted_iota(jnp.int32, (rows.shape[0], NB), 1).astype(F32)
    for m in panels:
        equal = rows == piv_row_ref[m : m + 1, :]
        hit = jnp.sum(jnp.where(equal, lanes + float(m * NB + 1), 0.0), axis=1, keepdims=True)
        hit = hit.astype(jnp.int32)
        rows = jnp.where(hit > 0, hit - 1, rows)
    return rows


def pick_kernel(place_ref, piv_row_ref, piv_col_ref, a_ref, first_ref, rest_ref, origin_ref):
    prow = place_ref[0]
    lane = lax.broadcasted_iota(jnp.int32, (NB, ROWS), 1)
    for k in range(PANELS):
        rows = chase(piv_col_ref[k * NB : (k + 1) * NB, :], piv_row_ref, range(k - 1, -1, -1))
        owner = (rows >> 7) & 31
        slot = ((rows >> 12) << 7) | (rows & 127)
        slot = jnp.where(owner == prow, slot, -1)
        onehot = jnp.where(lane == slot, 1.0, 0.0).astype(BF)
        first_ref[k * NB : (k + 1) * NB, :] = select_rows(onehot, a_ref[:, :NB])
        rest_ref[k * NB : (k + 1) * NB, :] = select_rows(onehot, a_ref[:, NB:])
    local = lax.broadcasted_iota(jnp.int32, (ROWS, 1), 0)
    rows = ((local >> 7) * PROW + prow) * NB + (local & 127)
    rows = chase(rows, piv_row_ref, range(PANELS - 1, -1, -1))
    origin_ref[...] = jnp.broadcast_to(rows, (ROWS, NB))


def place_of(origin):
    unit = (origin >> 2) & 31
    return (unit << 5) + 16 + ((origin >> 7) << 2) + (origin & 3)


def moved_rows(origin, gathered, kept):
    lane = lax.broadcasted_iota(jnp.int32, (ROWS, 1024), 1)
    onehot = jnp.where(lane == jnp.where(origin < TOP, place_of(origin), -1), 1.0, 0.0).astype(BF)
    return jnp.where(origin < TOP, select_rows(onehot, gathered), kept)


def column_kernel(origin_ref, gathered_ref, a_ref, out_ref):
    origin = origin_ref[:, :1]
    for unit in range(PROW):
        out_ref[unit * 16 : unit * 16 + 16, :] = gathered_ref[unit * 32 : unit * 32 + 16, :]
    out_ref[TOP:, :] = moved_rows(origin, gathered_ref[...], a_ref[:, :NB])


def exchange_first(picked, top):
    sent = jnp.concatenate([picked.reshape(PROW, 16, NB), top.reshape(PROW, 4, NB)], axis=1)
    got = lax.all_to_all(sent, "prow", 0, 0)
    chunk = jnp.concatenate([jnp.sum(got[:, :16], axis=0), got[:4, 16:].reshape(16, NB)], axis=0)
    sent = jnp.broadcast_to(chunk[None], (PROW, 32, NB))
    return lax.all_to_all(sent, "prow", 0, 0).reshape(PROW * 32, NB)


def exchange_rest(picked, top):
    sent = jnp.concatenate([picked.reshape(4, NB, REST), top.reshape(4, 32, REST)], axis=1)
    got = lax.all_to_all(sent, "prow", 0, 0, axis_index_groups=X_GROUPS)
    sent = jnp.concatenate(
        [jnp.sum(got[:, :NB], axis=0).reshape(8, 16, REST), got[0, NB:].reshape(8, 4, REST)], axis=1
    )
    got = lax.all_to_all(sent, "prow", 0, 0, axis_index_groups=Z_GROUPS)
    chunk = jnp.concatenate([jnp.sum(got[:, :16], axis=0), got[:4, 16:].reshape(16, REST)], axis=0)
    got = lax.all_to_all(
        jnp.broadcast_to(chunk[None], (8, 32, REST)), "prow", 0, 0, axis_index_groups=Z_GROUPS
    )
    got = got.reshape(256, REST)
    got = lax.all_to_all(
        jnp.broadcast_to(got[None], (4, 256, REST)), "prow", 0, 0, axis_index_groups=X_GROUPS
    )
    return got.reshape(PROW * 32, REST)


def spread_start(own):
    up = lax.ppermute(own, "pcol", [(q, q + 4) for q in range(4)])
    down = lax.ppermute(own, "pcol", [(q, q + 12) for q in range(4)])
    return up, down


def spread_columns(own, pcol):
    return spread_rest(own, *spread_start(own), pcol)


def spread_rest(own, up, down, pcol):
    near = jnp.where(pcol < 4, own, jnp.where(pcol < 8, up, down))
    half = near.shape[0] // 2
    left = lax.ppermute(near[:half], "pcol", [(q + 4, q + 8) for q in range(4)])
    right = lax.ppermute(near[half:], "pcol", [(q + 12, q + 8) for q in range(4)])
    far = (pcol >= 8) & (pcol < 12)
    near = jnp.where(far, jnp.concatenate([left, right], axis=0), near)
    across = lax.ppermute(near, "pcol", [(q, q ^ 2) for q in range(PCOL)])
    both = jnp.concatenate([near, across], axis=1)
    pair = lax.ppermute(both, "pcol", [(q, q ^ 1) for q in range(PCOL)])
    return near, across, pair


def lane_sum(mask, value):
    return jnp.sum(jnp.where(mask, value, 0.0), axis=1, keepdims=True)


def sub_sum(mask, value):
    return jnp.sum(jnp.where(mask, value, 0.0), axis=0, keepdims=True).astype(jnp.int32)


def iota(shape, axis):
    return lax.broadcasted_iota(jnp.int32, shape, axis)


def ranks(masks):
    count = len(masks)
    padded = -(-count // 8) * 8
    rows = [jnp.where(mask, 1.0, 0.0) for mask in masks]
    rows = rows + [jnp.zeros((1, NB), F32)] * (padded - count)
    before = jnp.where(iota((NB, NB), 0) < iota((NB, NB), 1), 1.0, 0.0).astype(BF)
    found = mm(jnp.concatenate(rows, axis=0).astype(BF), before)
    return [found[n : n + 1, :] for n in range(count)]


def slots(mask, rank, value, capacity):
    row = iota((capacity, NB), 0).astype(F32)
    return lane_sum(mask & (rank == row), value + 1.0).astype(jnp.int32) - 1


def onehot_of(column, width):
    return jnp.where(iota((column.shape[0], width), 1) == column, 1.0, 0.0).astype(BF)


def plan_kernel(pivots_ref, a_ref, send_ref, plan_ref, over_ref, source_ref, target_ref):
    prow = lax.axis_index("prow")
    x = prow >> 3
    z = prow & 7
    sub = iota((NB, NB), 0)
    lane = iota((NB, NB), 1)
    subf = sub.astype(F32)
    lane_row = iota((1, NB), 1)
    piv_row = [pivots_ref[m : m + 1, :] for m in range(PANELS)]
    piv_col = []
    for m in range(PANELS):
        piv_col.append(lane_sum(sub == lane, piv_row[m].astype(F32)).astype(jnp.int32))

    def met(m, rows):
        return sub_sum(piv_col[m] == rows, subf + float(m * NB + 1))

    source = []
    target = []
    for k in range(PANELS):
        rows = piv_row[k]
        for m in range(k - 1, -1, -1):
            hit = met(m, rows)
            rows = jnp.where(hit > 0, hit - 1, rows)
        source.append(rows)
        source_ref[k : k + 1, :] = rows
        rows = lane_row + k * NB
        for m in range(PANELS):
            if m == k:
                rows = jnp.where(rows == lane_row + k * NB, piv_row[k], rows)
                continue
            hit = met(m, rows)
            moved = jnp.where(hit > 0, hit - 1, rows)
            if m > k:
                look = sub_sum(sub + m * NB == rows, piv_col[m].astype(F32))
                moved = jnp.where(look > 0, look, moved)
            rows = moved
        target.append(rows)
        target_ref[k : k + 1, :] = rows

    def local_of(rows):
        return ((rows >> 12) << 7) | (rows & 127)

    def owner_of(rows):
        return (rows >> 7) & 31

    masks = [owner_of(source[k]) == prow for k in range(PANELS)]
    order = ranks(masks)
    chosen = [
        slots(masks[k], order[k], local_of(source[k]).astype(F32), 16) for k in range(PANELS)
    ]
    send_ref[...] = select_rows(onehot_of(jnp.concatenate(chosen, axis=0), ROWS), a_ref[...])
    wide = lambda column: jnp.broadcast_to(column, (column.shape[0], NB))
    mine = target_ref[pl.ds(prow & 3, 1), :]
    leaves = (mine >= TOP) & (prow < PANELS)
    masks = [leaves & (((mine >> 10) & 3) == n) for n in range(4)]
    order = ranks(masks)
    lanef = lane_row.astype(F32)
    for n in range(4):
        plan_ref[544 + 48 * n : 592 + 48 * n, :] = wide(slots(masks[n], order[n], lanef, 48))

    panel = source_ref[pl.ds(x, 1), :]
    panel_z = (panel >> 7) & 7
    panel_x = (panel >> 10) & 3
    here = panel_z == z
    masks = [here & (panel_x == n) for n in range(4)] + [here]
    order = ranks(masks)
    spot = jnp.zeros((1, NB), F32)
    for n in range(4):
        spot = spot + jnp.where(masks[n], order[n] + 16.0 * n, 0.0)
    plan_ref[0:32, :] = wide(slots(here, order[4], spot, 32))
    other = target_ref[pl.ds(z & 3, 1), :]
    along = (other >= TOP) & (z < PANELS) & (((other >> 10) & 3) == x)
    masks = [along & (((other >> 7) & 7) == n) for n in range(8)] + [along]
    order = ranks(masks)
    for n in range(8):
        plan_ref[32 + 16 * n : 48 + 16 * n, :] = wide(slots(masks[n], order[n], order[8], 16))
    zf = panel_z.astype(F32)
    zcol = lane_sum(sub == lane, zf)
    ahead = lane_sum((zf == zcol) & (lane < sub), 1.0)
    plan_ref[160:288, :] = wide((zcol * 32.0 + ahead).astype(jnp.int32))
    masks = [(target[k] >= TOP) & (owner_of(target[k]) == prow) for k in range(PANELS)]
    order = ranks(masks)
    row = iota((ROWS, NB), 0)
    total = jnp.zeros((ROWS, 1), F32)
    for k in range(PANELS):
        total = total + lane_sum(masks[k] & (local_of(target[k]) == row), order[k] + (16.0 * k + 1.0))
    plan_ref[288:544, :] = wide(total.astype(jnp.int32) - 1)
    unit = iota((PROW, NB), 0)
    over = jnp.zeros((PROW, 1), F32)
    for k in range(PANELS):
        leaves = target[k] >= TOP
        for mask, cap in (
            (owner_of(source[k]) == unit, 16.0),
            (((source[k] >> 7) & 7) == unit, 32.0),
            (leaves & (((target[k] >> 10) & 3) == unit), 48.0),
            (leaves & (owner_of(target[k]) == unit), 16.0),
        ):
            over = jnp.maximum(over, lane_sum(mask, 1.0) - cap)
    over = jnp.max(over, axis=0, keepdims=True)
    over_ref[...] = jnp.broadcast_to(over, (8, NB)).astype(jnp.int32)


def turn_kernel(plan_ref, got_ref, send_ref):
    rows = select_rows(onehot_of(plan_ref[0:32, :1], 64), got_ref[...])
    for n in range(8):
        send_ref[n] = rows


def panel_kernel(plan_ref, got_ref, send_ref, lead_ref):
    rows = select_rows(onehot_of(plan_ref[160:288, :1], 256), got_ref[...])
    for n in range(4):
        send_ref[n] = rows
    lead_ref[...] = rows[:, :NB]


def put_columns(near_ref, across_ref, pair_ref, rows, store):
    kind = lax.axis_index("pcol") & 3
    store(kind, near_ref[rows, :])
    store(kind ^ 2, across_ref[rows, :])
    store(kind ^ 1, pair_ref[rows, :NB])
    store(kind ^ 3, pair_ref[rows, NB:])


def lane_block(index):
    return pl.ds(pl.multiple_of(index * NB, NB), NB)


def corner_kernel(near_ref, across_ref, pair_ref, send_ref):
    panel = lax.axis_index("prow") >> 3

    def store(index, value):
        @pl.when(index != panel)
        def _():
            spot = lane_block(jnp.where(index < panel, index, index - 1))
            for n in range(4):
                send_ref[n, :, spot] = value

    put_columns(near_ref, across_ref, pair_ref, slice(0, NB), store)


def leave_kernel(plan_ref, a_ref, near_ref, across_ref, pair_ref, *refs):
    out_refs, full_ref = refs[:4], refs[4]

    def store(index, value):
        full_ref[:, lane_block(index)] = value

    put_columns(near_ref, across_ref, pair_ref, slice(0, NB), store)
    full_ref[:, TOP:] = a_ref[:NB, :]
    rows = select_rows(onehot_of(plan_ref[544:736, :1], NB), full_ref[...])
    for n in range(4):
        out_refs[n][...] = rows[48 * n : 48 * n + 48]


def spread_kernel(plan_ref, lead_ref, home_ref, one_ref, two_ref, three_ref, lead_out_ref, *out_refs):
    prow = lax.axis_index("prow")
    z = prow & 7
    lead_out_ref[...] = lead_ref[...]
    held = one_ref[...] + two_ref[...] + three_ref[...]
    held = jnp.where(prow < 8, home_ref[...], held)
    spots = [plan_ref[pl.ds(pl.multiple_of(32 + 16 * ((z + n) & 7), 8), 16), :1] for n in range(8)]
    rows = select_rows(onehot_of(jnp.concatenate(spots, axis=0), 48), held)
    for n in range(8):
        out_refs[n][...] = rows[16 * n : 16 * n + 16]


def rows_kernel(plan_ref, a_ref, near_ref, across_ref, pair_ref, *refs):
    moved_refs, out_ref, moved_ref = refs[:8], refs[8], refs[9]
    z = lax.axis_index("prow") & 7
    slot = plan_ref[288:544, :1]
    onehot = onehot_of(slot, 64)

    def store(index, value):
        out_ref[:, lane_block(index)] = value

    put_columns(near_ref, across_ref, pair_ref, slice(0, ROWS), store)
    out_ref[:, TOP:] = a_ref[...]
    for n in range(8):
        moved_ref[(z - n) & 7] = moved_refs[n][...]
    moved = moved_ref[0:4].reshape(64, TOP + COLS)
    out_ref[...] = jnp.where(slot >= 0, select_rows(onehot, moved), out_ref[...])


def factor_kernel(corner_ref, own_ref, rows_ref, lower_ref, upper_ref, out_ref, z_ref, y_ref, m_ref, u_ref, d_ref):
    prow = lax.axis_index("prow")
    pcol = lax.axis_index("pcol")
    for k in range(PANELS):
        for j in range(PANELS):
            if j != k:
                spot = j if j < k else j - 1
                z_ref[k * NB : k * NB + NB, j * NB : j * NB + NB] = corner_ref[
                    k * NB : k * NB + NB, spot * NB : spot * NB + NB
                ]
    z_ref[TOP:, :] = rows_ref[:, :TOP]
    for k in range(PANELS):
        s = k * NB
        e = s + NB
        before = own_ref if k == 0 else y_ref
        multipliers = dot3(z_ref[e:, s:e], upper_ref[k])
        z_ref[e:, s:e] = multipliers
        mh, ml = split2(multipliers)
        m3 = jnp.concatenate([mh, ml, mh], axis=1)
        m_ref[:, 3 * s : 3 * e] = m3[TOP - e :]
        lh, ll = split2(lower_ref[k])
        l3 = jnp.concatenate([lh, ll, lh], axis=1)
        if e < TOP:
            bh, bl = split2(z_ref[s:e, e:])
            corner = mm(l3, jnp.concatenate([bh, bh, bl], axis=0))
            z_ref[s:e, e:] = corner
            uh, ul = split2(corner)
            z_ref[e:, e:] = z_ref[e:, e:] - mm(m3, jnp.concatenate([uh, uh, ul], axis=0))
        d_ref[s:e, :] = before[s:e, :NB]
        bh, bl = split2(before[s:e, :])
        upper_rows = mm(l3, jnp.concatenate([bh, bh, bl], axis=0))
        y_ref[s:e, :] = upper_rows
        uh, ul = split2(upper_rows)
        u3 = jnp.concatenate([uh, uh, ul], axis=0)
        u_ref[3 * s : 3 * e, :] = u3
        if e < TOP:
            y_ref[e:TOP, :] = before[e:TOP, :] - mm(m3[: TOP - e], u3)
    out_ref[...] = rows_ref[:, TOP:] - mm(m_ref[...], u_ref[...])
    panel_cols = lane_block(pcol & 3)
    top_rows = pl.ds(pl.multiple_of((prow & 3) * NB, NB), NB)

    @pl.when(pcol < PANELS)
    def _():
        out_ref[:, :NB] = z_ref[TOP:, panel_cols]

    @pl.when(prow < PANELS)
    def _():
        out_ref[:NB, :] = y_ref[top_rows, :]

    @pl.when((prow < PANELS) & (pcol < PANELS))
    def _():
        out_ref[:NB, :NB] = jnp.where(
            prow == pcol, d_ref[top_rows, :], z_ref[top_rows, panel_cols]
        )


def kernel_call(body, shapes, scratch=()):
    def call(*args):
        return pl.pallas_call(
            body,
            in_specs=[VMEM] * len(args),
            out_specs=[VMEM] * len(shapes),
            out_shape=[jax.ShapeDtypeStruct(shape, kind) for shape, kind in shapes],
            scratch_shapes=list(scratch),
            compiler_params=pltpu.CompilerParams(vmem_limit_bytes=KERNEL_VMEM),
        )(*args)

    return call


def factor(corner, own, rows, lower_inverse, upper_inverse):
    return pl.pallas_call(
        factor_kernel,
        in_specs=[VMEM] * 5,
        out_specs=VMEM,
        out_shape=jax.ShapeDtypeStruct((ROWS, COLS), F32),
        scratch_shapes=[
            pltpu.VMEM((TOP + ROWS, TOP), F32),
            pltpu.VMEM((TOP, COLS), F32),
            pltpu.VMEM((ROWS, 3 * TOP), BF),
            pltpu.VMEM((3 * TOP, COLS), BF),
            pltpu.VMEM((TOP, NB), F32),
        ],
        compiler_params=pltpu.CompilerParams(vmem_limit_bytes=FACTOR_VMEM),
    )(corner, own, rows, lower_inverse, upper_inverse)


def along(value, groups):
    return lax.all_to_all(value, "prow", 0, 0, axis_index_groups=groups)


def hop(value, pairs):
    return lax.ppermute(value, "prow", pairs)


def slotted(send, plan, matrix, lower_inverse, upper_inverse):
    pcol = lax.axis_index("pcol")
    block = matrix[:, :NB]
    ends = spread_start(block)
    got = along(send.reshape(4, 16, COLS), X_GROUPS)
    got, ends = lax.optimization_barrier((got, ends))
    (send,) = kernel_call(turn_kernel, [((8, 32, COLS), F32)])(plan, got.reshape(64, COLS))
    raw = spread_rest(block, *ends, pcol)
    got = along(send, Z_GROUPS)
    leaving = kernel_call(leave_kernel, [((48, WIDE), F32)] * 4, [pltpu.VMEM((NB, WIDE), F32)])(
        plan, matrix, *raw
    )
    held = [hop(leaving[n], [(k, 8 * n + k) for k in range(PANELS)]) for n in range(1, 4)]
    got, raw, held = lax.optimization_barrier((got, raw, held))
    send, lead = kernel_call(panel_kernel, [((4, NB, COLS), F32), ((NB, NB), F32)])(
        plan, got.reshape(256, COLS)
    )
    own = along(send, X_GROUPS).reshape(TOP, COLS)
    lead, *parts = kernel_call(spread_kernel, [((NB, NB), F32)] + [((16, WIDE), F32)] * 8)(
        plan, lead, leaving[0], *held
    )
    near, across, pair = spread_columns(lead, pcol)
    moved = [parts[0]]
    for n in range(1, 8):
        pairs = [(8 * x + k, 8 * x + (k + n) % 8) for x in range(4) for k in range(PANELS)]
        moved.append(hop(parts[n], pairs))
    (send,) = kernel_call(corner_kernel, [((4, NB, TOP - NB), F32)])(near, across, pair)
    send, own, moved = lax.optimization_barrier((send, own, moved))
    corner = along(send, X_GROUPS).reshape(TOP, TOP - NB)
    (rows,) = kernel_call(
        rows_kernel, [((ROWS, WIDE), F32)], [pltpu.VMEM((8, 16, WIDE), F32)]
    )(plan, matrix, *raw, *moved)
    return factor(corner, own, rows, lower_inverse, upper_inverse)


def dense_rows_kernel(
    origin_ref, gathered_ref, a_ref, own_ref, near_ref, across_ref, pair_ref, corner_ref, top_ref, out_ref
):
    def store_corner(index, value):
        for k in range(PANELS):

            @pl.when(index != k)
            def _():
                spot = lane_block(jnp.where(index < k, index, index - 1))
                corner_ref[k * NB : k * NB + NB, spot] = value[k * NB : k * NB + NB]

    def store_rows(index, value):
        out_ref[:, lane_block(index)] = value

    put_columns(near_ref, across_ref, pair_ref, slice(0, TOP), store_corner)
    put_columns(near_ref, across_ref, pair_ref, slice(TOP, TOP + ROWS), store_rows)
    top_ref[:, :NB] = own_ref[:TOP, :]
    out_ref[:, TOP : TOP + NB] = own_ref[TOP:, :]
    for unit in range(PROW):
        top_ref[unit * 16 : unit * 16 + 16, NB:] = gathered_ref[unit * 32 : unit * 32 + 16, :]
    origin = origin_ref[:, :1]

    @pl.loop(0, REST // NB)
    def _(c):
        out_ref[:, lane_block(c + PANELS + 1)] = moved_rows(
            origin, gathered_ref[:, lane_block(c)], a_ref[:, lane_block(c + 1)]
        )


def dense(pivots, matrix, lower_inverse, upper_inverse):
    prow = lax.axis_index("prow")
    pcol = lax.axis_index("pcol")
    place = jnp.stack([prow, pcol]).astype(jnp.int32)
    picked_first, picked_rest, origin = pl.pallas_call(
        pick_kernel,
        in_specs=[SMEM, VMEM, VMEM, VMEM],
        out_specs=[VMEM] * 3,
        out_shape=[
            jax.ShapeDtypeStruct((TOP, NB), F32),
            jax.ShapeDtypeStruct((TOP, REST), F32),
            jax.ShapeDtypeStruct((ROWS, NB), jnp.int32),
        ],
    )(place, pivots.reshape(PANELS, NB), pivots.reshape(TOP, 1), matrix)
    gathered_first = exchange_first(picked_first, matrix[:NB, :NB])
    (own,) = kernel_call(column_kernel, [((TOP + ROWS, NB), F32)])(origin, gathered_first, matrix)
    near, across, pair = spread_columns(own, pcol)
    gathered_rest = exchange_rest(picked_rest, matrix[:NB, NB:])
    corner, top, rows = kernel_call(
        dense_rows_kernel,
        [((TOP, TOP - NB), F32), ((TOP, COLS), F32), ((ROWS, WIDE), F32)],
    )(origin, gathered_rest, matrix, own, near, across, pair)
    return factor(corner, top, rows, lower_inverse, upper_inverse)


def per_device(matrix, pivots, lower_inverse, upper_inverse):
    send, plan, over = kernel_call(
        plan_kernel,
        [((64, COLS), F32), ((736, NB), jnp.int32), ((8, NB), jnp.int32)],
        [pltpu.VMEM((8, NB), jnp.int32), pltpu.VMEM((8, NB), jnp.int32)],
    )(pivots.reshape(PANELS, NB), matrix)
    return lax.cond(
        over[0, 0] <= 0,
        lambda: slotted(send, plan, matrix, lower_inverse, upper_inverse),
        lambda: dense(pivots, matrix, lower_inverse, upper_inverse),
    )


def solution(mesh):
    in_specs = (P("prow", "pcol"), P(), P(), P())
    out_specs = P("prow", "pcol")
    return jax.shard_map(
        per_device, mesh=mesh, in_specs=in_specs, out_specs=out_specs, check_vma=False
    )
```

```python
import jax
import jax.numpy as jnp
from jax import lax
from jax.experimental import pallas as pl
from jax.experimental.pallas import tpu as pltpu
from jax.sharding import PartitionSpec as P

NB = 128
PANELS = 4
TOP = NB * PANELS
PROW = 32
PCOL = 16
ROWS = 256
COLS = 768
REST = COLS - NB
KERNEL_VMEM = 20 << 20
FACTOR_VMEM = 28 << 20
BF = jnp.bfloat16
F32 = jnp.float32
X_GROUPS = [[x * 8 + z for x in range(4)] for z in range(8)]
Z_GROUPS = [[x * 8 + z for z in range(8)] for x in range(4)]
VMEM = pl.BlockSpec(memory_space=pltpu.VMEM)
SMEM = pl.BlockSpec(memory_space=pltpu.SMEM)


def mm(left, right):
    return lax.dot_general(left, right, (((1,), (0,)), ((), ())), preferred_element_type=F32)


def split2(value):
    high = value.astype(BF)
    low = (value - high.astype(F32)).astype(BF)
    return high, low


def select_rows(onehot, value):
    first = value.astype(BF)
    rest = value - first.astype(F32)
    second = rest.astype(BF)
    third = (rest - second.astype(F32)).astype(BF)
    return mm(onehot, first) + mm(onehot, second) + mm(onehot, third)


def dot3(left, right):
    lh, ll = split2(left)
    rh, rl = split2(right)
    return mm(jnp.concatenate([lh, ll, lh], axis=1), jnp.concatenate([rh, rh, rl], axis=0))


def chase(rows, piv_row_ref, panels):
    lanes = lax.broadcasted_iota(jnp.int32, (rows.shape[0], NB), 1).astype(F32)
    for m in panels:
        equal = rows == piv_row_ref[m : m + 1, :]
        hit = jnp.sum(jnp.where(equal, lanes + float(m * NB + 1), 0.0), axis=1, keepdims=True)
        hit = hit.astype(jnp.int32)
        rows = jnp.where(hit > 0, hit - 1, rows)
    return rows


def pick_kernel(place_ref, piv_row_ref, piv_col_ref, a_ref, first_ref, rest_ref, origin_ref):
    prow = place_ref[0]
    lane = lax.broadcasted_iota(jnp.int32, (NB, ROWS), 1)
    for k in range(PANELS):
        rows = chase(piv_col_ref[k * NB : (k + 1) * NB, :], piv_row_ref, range(k - 1, -1, -1))
        owner = (rows >> 7) & 31
        slot = ((rows >> 12) << 7) | (rows & 127)
        slot = jnp.where(owner == prow, slot, -1)
        onehot = jnp.where(lane == slot, 1.0, 0.0).astype(BF)
        first_ref[k * NB : (k + 1) * NB, :] = select_rows(onehot, a_ref[:, :NB])
        rest_ref[k * NB : (k + 1) * NB, :] = select_rows(onehot, a_ref[:, NB:])
    local = lax.broadcasted_iota(jnp.int32, (ROWS, 1), 0)
    rows = ((local >> 7) * PROW + prow) * NB + (local & 127)
    rows = chase(rows, piv_row_ref, range(PANELS - 1, -1, -1))
    origin_ref[...] = jnp.broadcast_to(rows, (ROWS, NB))


def place_of(origin):
    unit = (origin >> 2) & 31
    return (unit << 5) + 16 + ((origin >> 7) << 2) + (origin & 3)


def moved_rows(origin, gathered, kept):
    lane = lax.broadcasted_iota(jnp.int32, (ROWS, 1024), 1)
    onehot = jnp.where(lane == jnp.where(origin < TOP, place_of(origin), -1), 1.0, 0.0).astype(BF)
    return jnp.where(origin < TOP, select_rows(onehot, gathered), kept)


def column_kernel(origin_ref, gathered_ref, a_ref, out_ref):
    origin = origin_ref[:, :1]
    for unit in range(PROW):
        out_ref[unit * 16 : unit * 16 + 16, :] = gathered_ref[unit * 32 : unit * 32 + 16, :]
    out_ref[TOP:, :] = moved_rows(origin, gathered_ref[...], a_ref[:, :NB])


def exchange_first(picked, top):
    sent = jnp.concatenate([picked.reshape(PROW, 16, NB), top.reshape(PROW, 4, NB)], axis=1)
    got = lax.all_to_all(sent, "prow", 0, 0)
    chunk = jnp.concatenate([jnp.sum(got[:, :16], axis=0), got[:4, 16:].reshape(16, NB)], axis=0)
    sent = jnp.broadcast_to(chunk[None], (PROW, 32, NB))
    return lax.all_to_all(sent, "prow", 0, 0).reshape(PROW * 32, NB)


def exchange_rest(picked, top):
    sent = jnp.concatenate([picked.reshape(4, NB, REST), top.reshape(4, 32, REST)], axis=1)
    got = lax.all_to_all(sent, "prow", 0, 0, axis_index_groups=X_GROUPS)
    sent = jnp.concatenate(
        [jnp.sum(got[:, :NB], axis=0).reshape(8, 16, REST), got[0, NB:].reshape(8, 4, REST)], axis=1
    )
    got = lax.all_to_all(sent, "prow", 0, 0, axis_index_groups=Z_GROUPS)
    chunk = jnp.concatenate([jnp.sum(got[:, :16], axis=0), got[:4, 16:].reshape(16, REST)], axis=0)
    got = lax.all_to_all(
        jnp.broadcast_to(chunk[None], (8, 32, REST)), "prow", 0, 0, axis_index_groups=Z_GROUPS
    )
    got = got.reshape(256, REST)
    got = lax.all_to_all(
        jnp.broadcast_to(got[None], (4, 256, REST)), "prow", 0, 0, axis_index_groups=X_GROUPS
    )
    return got.reshape(PROW * 32, REST)


def spread_start(own):
    up = lax.ppermute(own, "pcol", [(q, q + 4) for q in range(4)])
    down = lax.ppermute(own, "pcol", [(q, q + 12) for q in range(4)])
    return up, down


def spread_columns(own, pcol):
    return spread_rest(own, *spread_start(own), pcol)


def spread_rest(own, up, down, pcol):
    near = jnp.where(pcol < 4, own, jnp.where(pcol < 8, up, down))
    half = near.shape[0] // 2
    left = lax.ppermute(near[:half], "pcol", [(q + 4, q + 8) for q in range(4)])
    right = lax.ppermute(near[half:], "pcol", [(q + 12, q + 8) for q in range(4)])
    far = (pcol >= 8) & (pcol < 12)
    near = jnp.where(far, jnp.concatenate([left, right], axis=0), near)
    across = lax.ppermute(near, "pcol", [(q, q ^ 2) for q in range(PCOL)])
    both = jnp.concatenate([near, across], axis=1)
    pair = lax.ppermute(both, "pcol", [(q, q ^ 1) for q in range(PCOL)])
    return near, across, pair


def lane_sum(mask, value):
    return jnp.sum(jnp.where(mask, value, 0.0), axis=1, keepdims=True)


def sub_sum(mask, value):
    return jnp.sum(jnp.where(mask, value, 0.0), axis=0, keepdims=True).astype(jnp.int32)


def iota(shape, axis):
    return lax.broadcasted_iota(jnp.int32, shape, axis)


def ranks(masks):
    count = len(masks)
    padded = -(-count // 8) * 8
    rows = [jnp.where(mask, 1.0, 0.0) for mask in masks]
    rows = rows + [jnp.zeros((1, NB), F32)] * (padded - count)
    before = jnp.where(iota((NB, NB), 0) < iota((NB, NB), 1), 1.0, 0.0).astype(BF)
    found = mm(jnp.concatenate(rows, axis=0).astype(BF), before)
    return [found[n : n + 1, :] for n in range(count)]


def slots(mask, rank, value, capacity):
    row = iota((capacity, NB), 0).astype(F32)
    return lane_sum(mask & (rank == row), value + 1.0).astype(jnp.int32) - 1


def onehot_of(column, width):
    return jnp.where(iota((column.shape[0], width), 1) == column, 1.0, 0.0).astype(BF)


def plan_kernel(pivots_ref, a_ref, send_ref, plan_ref, over_ref, source_ref, target_ref):
    prow = lax.axis_index("prow")
    x = prow >> 3
    z = prow & 7
    sub = iota((NB, NB), 0)
    lane = iota((NB, NB), 1)
    subf = sub.astype(F32)
    lane_row = iota((1, NB), 1)
    piv_row = [pivots_ref[m : m + 1, :] for m in range(PANELS)]
    piv_col = []
    for m in range(PANELS):
        piv_col.append(lane_sum(sub == lane, piv_row[m].astype(F32)).astype(jnp.int32))

    def met(m, rows):
        return sub_sum(piv_col[m] == rows, subf + float(m * NB + 1))

    source = []
    target = []
    for k in range(PANELS):
        rows = piv_row[k]
        for m in range(k - 1, -1, -1):
            hit = met(m, rows)
            rows = jnp.where(hit > 0, hit - 1, rows)
        source.append(rows)
        source_ref[k : k + 1, :] = rows
        rows = lane_row + k * NB
        for m in range(PANELS):
            if m == k:
                rows = jnp.where(rows == lane_row + k * NB, piv_row[k], rows)
                continue
            hit = met(m, rows)
            moved = jnp.where(hit > 0, hit - 1, rows)
            if m > k:
                look = sub_sum(sub + m * NB == rows, piv_col[m].astype(F32))
                moved = jnp.where(look > 0, look, moved)
            rows = moved
        target.append(rows)
        target_ref[k : k + 1, :] = rows

    def local_of(rows):
        return ((rows >> 12) << 7) | (rows & 127)

    def owner_of(rows):
        return (rows >> 7) & 31

    masks = [owner_of(source[k]) == prow for k in range(PANELS)]
    order = ranks(masks)
    pieces = [
        slots(masks[k], order[k], local_of(source[k]).astype(F32), 16) for k in range(PANELS)
    ]
    mine = target_ref[pl.ds(prow & 3, 1), :]
    leaves = (mine >= TOP) & (prow < PANELS)
    masks = [leaves & (((mine >> 10) & 3) == n) for n in range(4)]
    order = ranks(masks)
    lanef = lane_row.astype(F32)
    chosen = []
    for n in range(4):
        chosen.append(pieces[n])
        chosen.append(slots(masks[n], order[n], lanef, 48))
    send_ref[...] = select_rows(onehot_of(jnp.concatenate(chosen, axis=0), ROWS), a_ref[...])

    panel = source_ref[pl.ds(x, 1), :]
    panel_z = (panel >> 7) & 7
    panel_x = (panel >> 10) & 3
    here = panel_z == z
    masks = [here & (panel_x == n) for n in range(4)] + [here]
    order = ranks(masks)
    spot = jnp.zeros((1, NB), F32)
    for n in range(4):
        spot = spot + jnp.where(masks[n], order[n] + 64.0 * n, 0.0)
    wide = lambda column: jnp.broadcast_to(column, (column.shape[0], NB))
    plan_ref[0:32, :] = wide(slots(here, order[4], spot, 32))
    other = target_ref[pl.ds(z & 3, 1), :]
    along = (other >= TOP) & (z < PANELS) & (((other >> 10) & 3) == x)
    masks = [along & (((other >> 7) & 7) == n) for n in range(8)] + [along]
    order = ranks(masks)
    for n in range(8):
        plan_ref[32 + 16 * n : 48 + 16 * n, :] = wide(slots(masks[n], order[n], order[8], 16))
    zf = panel_z.astype(F32)
    zcol = lane_sum(sub == lane, zf)
    ahead = lane_sum((zf == zcol) & (lane < sub), 1.0)
    plan_ref[160:288, :] = wide((zcol * 32.0 + ahead).astype(jnp.int32))
    masks = [(target[k] >= TOP) & (owner_of(target[k]) == prow) for k in range(PANELS)]
    order = ranks(masks)
    row = iota((ROWS, NB), 0)
    total = jnp.zeros((ROWS, 1), F32)
    for k in range(PANELS):
        total = total + lane_sum(masks[k] & (local_of(target[k]) == row), order[k] + (16.0 * k + 1.0))
    plan_ref[288:544, :] = wide(total.astype(jnp.int32) - 1)
    unit = iota((PROW, NB), 0)
    over = jnp.zeros((PROW, 1), F32)
    for k in range(PANELS):
        leaves = target[k] >= TOP
        for mask, cap in (
            (owner_of(source[k]) == unit, 16.0),
            (((source[k] >> 7) & 7) == unit, 32.0),
            (leaves & (((target[k] >> 10) & 3) == unit), 48.0),
            (leaves & (owner_of(target[k]) == unit), 16.0),
        ):
            over = jnp.maximum(over, lane_sum(mask, 1.0) - cap)
    over = jnp.max(over, axis=0, keepdims=True)
    over_ref[...] = jnp.broadcast_to(over, (8, NB)).astype(jnp.int32)


def turn_kernel(plan_ref, got_ref, send_ref):
    got = got_ref[...].reshape(256, COLS)
    rows = select_rows(onehot_of(plan_ref[0:32, :1], 256), got)
    moved = plan_ref[32:160, :1]
    moved = jnp.where(moved < 0, -1, moved + 16)
    sent = select_rows(onehot_of(moved, 64), got[:64])
    for n in range(8):
        send_ref[n, 0:32, :] = rows
        send_ref[n, 32:48, :] = sent[n * 16 : n * 16 + 16]


def panel_kernel(plan_ref, got_ref, send_ref, lead_ref):
    got = jnp.concatenate([got_ref[n, 0:32, :] for n in range(8)], axis=0)
    rows = select_rows(onehot_of(plan_ref[160:288, :1], 256), got)
    for n in range(4):
        send_ref[n] = rows
        lead_ref[NB + n * 16 : NB + n * 16 + 16, :] = got_ref[n, 32:48, :NB]
    lead_ref[0:NB, :] = rows[:, :NB]


def put_columns(near_ref, across_ref, pair_ref, rows, store):
    kind = lax.axis_index("pcol") & 3
    store(kind, near_ref[rows, :])
    store(kind ^ 2, across_ref[rows, :])
    store(kind ^ 1, pair_ref[rows, :NB])
    store(kind ^ 3, pair_ref[rows, NB:])


def lane_block(index):
    return pl.ds(pl.multiple_of(index * NB, NB), NB)


def corner_kernel(near_ref, across_ref, pair_ref, send_ref, moved_ref):
    panel = lax.axis_index("prow") >> 3

    def store_send(index, value):
        @pl.when(index != panel)
        def _():
            send_ref[:, lane_block(jnp.where(index < panel, index, index - 1))] = value

    def store_moved(index, value):
        moved_ref[:, lane_block(index)] = value

    put_columns(near_ref, across_ref, pair_ref, slice(0, NB), store_send)
    put_columns(near_ref, across_ref, pair_ref, slice(NB, NB + 64), store_moved)


def own_rows_kernel(plan_ref, got_ref, a_ref, out_ref):
    slot = plan_ref[288:544, :1]
    moved = jnp.concatenate([got_ref[n, 32:48, :] for n in range(4)], axis=0)
    out_ref[...] = jnp.where(slot >= 0, select_rows(onehot_of(slot, 64), moved), a_ref[...])


def panel_rows_kernel(plan_ref, moved_ref, near_ref, across_ref, pair_ref, out_ref):
    slot = plan_ref[288:544, :1]

    def store(index, value):
        out_ref[:, lane_block(index)] = value

    put_columns(near_ref, across_ref, pair_ref, slice(0, ROWS), store)
    moved = select_rows(onehot_of(slot, 64), moved_ref[...])
    out_ref[...] = jnp.where(slot >= 0, moved, out_ref[...])


def factor_kernel(
    home_ref, one_ref, two_ref, three_ref, own_ref, left_ref, right_ref, lower_ref, upper_ref,
    out_ref, z_ref, y_ref, m_ref, u_ref, d_ref,
):
    prow = lax.axis_index("prow")
    pcol = lax.axis_index("pcol")
    for n, ref in enumerate((home_ref, one_ref, two_ref, three_ref)):
        panel = ((prow >> 3) - n) & 3
        rows = pl.ds(pl.multiple_of(panel * NB, NB), NB)
        for spot in range(PANELS - 1):
            block = jnp.where(spot < panel, spot, spot + 1)
            z_ref[rows, lane_block(block)] = ref[:, spot * NB : spot * NB + NB]
    z_ref[TOP:, :] = left_ref[...]
    for k in range(PANELS):
        s = k * NB
        e = s + NB
        before = own_ref if k == 0 else y_ref
        multipliers = dot3(z_ref[e:, s:e], upper_ref[k])
        z_ref[e:, s:e] = multipliers
        mh, ml = split2(multipliers)
        m3 = jnp.concatenate([mh, ml, mh], axis=1)
        m_ref[:, 3 * s : 3 * e] = m3[TOP - e :]
        lh, ll = split2(lower_ref[k])
        l3 = jnp.concatenate([lh, ll, lh], axis=1)
        if e < TOP:
            bh, bl = split2(z_ref[s:e, e:])
            corner = mm(l3, jnp.concatenate([bh, bh, bl], axis=0))
            z_ref[s:e, e:] = corner
            uh, ul = split2(corner)
            z_ref[e:, e:] = z_ref[e:, e:] - mm(m3, jnp.concatenate([uh, uh, ul], axis=0))
        d_ref[s:e, :] = before[s:e, :NB]
        bh, bl = split2(before[s:e, :])
        upper_rows = mm(l3, jnp.concatenate([bh, bh, bl], axis=0))
        y_ref[s:e, :] = upper_rows
        uh, ul = split2(upper_rows)
        u3 = jnp.concatenate([uh, uh, ul], axis=0)
        u_ref[3 * s : 3 * e, :] = u3
        if e < TOP:
            y_ref[e:TOP, :] = before[e:TOP, :] - mm(m3[: TOP - e], u3)
    out_ref[...] = right_ref[...] - mm(m_ref[...], u_ref[...])
    panel_cols = lane_block(pcol & 3)
    top_rows = pl.ds(pl.multiple_of((prow & 3) * NB, NB), NB)

    @pl.when(pcol < PANELS)
    def _():
        out_ref[:, :NB] = z_ref[TOP:, panel_cols]

    @pl.when(prow < PANELS)
    def _():
        out_ref[:NB, :] = y_ref[top_rows, :]

    @pl.when((prow < PANELS) & (pcol < PANELS))
    def _():
        out_ref[:NB, :NB] = jnp.where(
            prow == pcol, d_ref[top_rows, :], z_ref[top_rows, panel_cols]
        )


def kernel_call(body, shapes, scratch=()):
    def call(*args):
        return pl.pallas_call(
            body,
            in_specs=[VMEM] * len(args),
            out_specs=[VMEM] * len(shapes),
            out_shape=[jax.ShapeDtypeStruct(shape, kind) for shape, kind in shapes],
            scratch_shapes=list(scratch),
            compiler_params=pltpu.CompilerParams(vmem_limit_bytes=KERNEL_VMEM),
        )(*args)

    return call


def factor(*args):
    return pl.pallas_call(
        factor_kernel,
        in_specs=[VMEM] * len(args),
        out_specs=VMEM,
        out_shape=jax.ShapeDtypeStruct((ROWS, COLS), F32),
        scratch_shapes=[
            pltpu.VMEM((TOP + ROWS, TOP), F32),
            pltpu.VMEM((TOP, COLS), F32),
            pltpu.VMEM((ROWS, 3 * TOP), BF),
            pltpu.VMEM((3 * TOP, COLS), BF),
            pltpu.VMEM((TOP, NB), F32),
        ],
        compiler_params=pltpu.CompilerParams(vmem_limit_bytes=FACTOR_VMEM),
    )(*args)


def along(value, groups):
    return lax.all_to_all(value, "prow", 0, 0, axis_index_groups=groups)


def slotted(send, plan, matrix, lower_inverse, upper_inverse):
    pcol = lax.axis_index("pcol")
    block = matrix[:, :NB]
    ends = spread_start(block)
    got = along(send.reshape(4, 64, COLS), X_GROUPS)
    got, ends = lax.optimization_barrier((got, ends))
    (send,) = kernel_call(turn_kernel, [((8, 48, COLS), F32)])(plan, got)
    raw = spread_rest(block, *ends, pcol)
    got = along(send, Z_GROUPS)
    got, raw = lax.optimization_barrier((got, raw))
    send, lead = kernel_call(panel_kernel, [((4, NB, COLS), F32), ((NB + 64, NB), F32)])(plan, got)
    own = along(send, X_GROUPS).reshape(TOP, COLS)
    ends = spread_start(lead)
    near, across, pair = spread_rest(lead, *ends, pcol)
    (right,) = kernel_call(own_rows_kernel, [((ROWS, COLS), F32)])(plan, got, matrix)
    home, moved = kernel_call(corner_kernel, [((NB, TOP - NB), F32), ((64, TOP), F32)])(
        near, across, pair
    )
    others = [
        lax.ppermute(home, "prow", [(p, (p + 8 * n) % PROW) for p in range(PROW)])
        for n in range(1, 4)
    ]
    (left,) = kernel_call(panel_rows_kernel, [((ROWS, TOP), F32)])(plan, moved, *raw)
    return factor(home, *others, own, left, right, lower_inverse, upper_inverse)


def dense_rows_kernel(
    origin_ref, gathered_ref, a_ref, own_ref, near_ref, across_ref, pair_ref,
    home_ref, one_ref, two_ref, three_ref, top_ref, left_ref, right_ref,
):
    x = lax.axis_index("prow") >> 3

    def store_corner(index, value):
        for n, ref in enumerate((home_ref, one_ref, two_ref, three_ref)):
            panel = (x - n) & 3

            @pl.when(index != panel)
            def _():
                spot = lane_block(jnp.where(index < panel, index, index - 1))
                for k in range(PANELS):

                    @pl.when(panel == k)
                    def _():
                        ref[:, spot] = value[k * NB : k * NB + NB]

    def store_left(index, value):
        left_ref[:, lane_block(index)] = value

    put_columns(near_ref, across_ref, pair_ref, slice(0, TOP), store_corner)
    put_columns(near_ref, across_ref, pair_ref, slice(TOP, TOP + ROWS), store_left)
    top_ref[:, :NB] = own_ref[:TOP, :]
    right_ref[:, :NB] = own_ref[TOP:, :]
    for unit in range(PROW):
        top_ref[unit * 16 : unit * 16 + 16, NB:] = gathered_ref[unit * 32 : unit * 32 + 16, :]
    origin = origin_ref[:, :1]

    @pl.loop(0, REST // NB)
    def _(c):
        right_ref[:, lane_block(c + 1)] = moved_rows(
            origin, gathered_ref[:, lane_block(c)], a_ref[:, lane_block(c + 1)]
        )


def dense(pivots, matrix, lower_inverse, upper_inverse):
    prow = lax.axis_index("prow")
    pcol = lax.axis_index("pcol")
    place = jnp.stack([prow, pcol]).astype(jnp.int32)
    picked_first, picked_rest, origin = pl.pallas_call(
        pick_kernel,
        in_specs=[SMEM, VMEM, VMEM, VMEM],
        out_specs=[VMEM] * 3,
        out_shape=[
            jax.ShapeDtypeStruct((TOP, NB), F32),
            jax.ShapeDtypeStruct((TOP, REST), F32),
            jax.ShapeDtypeStruct((ROWS, NB), jnp.int32),
        ],
    )(place, pivots.reshape(PANELS, NB), pivots.reshape(TOP, 1), matrix)
    gathered_first = exchange_first(picked_first, matrix[:NB, :NB])
    (own,) = kernel_call(column_kernel, [((TOP + ROWS, NB), F32)])(origin, gathered_first, matrix)
    near, across, pair = spread_columns(own, pcol)
    gathered_rest = exchange_rest(picked_rest, matrix[:NB, NB:])
    *corners, top, left, right = kernel_call(
        dense_rows_kernel,
        [((NB, TOP - NB), F32)] * 4 + [((TOP, COLS), F32), ((ROWS, TOP), F32), ((ROWS, COLS), F32)],
    )(origin, gathered_rest, matrix, own, near, across, pair)
    return factor(*corners, top, left, right, lower_inverse, upper_inverse)


def per_device(matrix, pivots, lower_inverse, upper_inverse):
    send, plan, over = kernel_call(
        plan_kernel,
        [((256, COLS), F32), ((544, NB), jnp.int32), ((8, NB), jnp.int32)],
        [pltpu.VMEM((8, NB), jnp.int32), pltpu.VMEM((8, NB), jnp.int32)],
    )(pivots.reshape(PANELS, NB), matrix)
    return lax.cond(
        over[0, 0] <= 0,
        lambda: slotted(send, plan, matrix, lower_inverse, upper_inverse),
        lambda: dense(pivots, matrix, lower_inverse, upper_inverse),
    )


def solution(mesh):
    in_specs = (P("prow", "pcol"), P(), P(), P())
    out_specs = P("prow", "pcol")
    return jax.shard_map(
        per_device, mesh=mesh, in_specs=in_specs, out_specs=out_specs, check_vma=False
    )
```

```python
import jax
import jax.numpy as jnp
from jax import lax
from jax.experimental import pallas as pl
from jax.experimental.pallas import tpu as pltpu
from jax.sharding import PartitionSpec as P

NB = 128
PANELS = 4
TOP = NB * PANELS
PROW = 32
PCOL = 16
ROWS = 256
COLS = 768
REST = COLS - NB
WIDE = TOP + COLS
KERNEL_VMEM = 20 << 20
FACTOR_VMEM = 28 << 20
BF = jnp.bfloat16
F32 = jnp.float32
X_GROUPS = [[x * 8 + z for x in range(4)] for z in range(8)]
Z_GROUPS = [[x * 8 + z for z in range(8)] for x in range(4)]
VMEM = pl.BlockSpec(memory_space=pltpu.VMEM)
SMEM = pl.BlockSpec(memory_space=pltpu.SMEM)


def mm(left, right):
    return lax.dot_general(left, right, (((1,), (0,)), ((), ())), preferred_element_type=F32)


def split2(value):
    high = value.astype(BF)
    low = (value - high.astype(F32)).astype(BF)
    return high, low


def select_rows(onehot, value):
    first = value.astype(BF)
    rest = value - first.astype(F32)
    second = rest.astype(BF)
    third = (rest - second.astype(F32)).astype(BF)
    return mm(onehot, first) + mm(onehot, second) + mm(onehot, third)


def dot3(left, right):
    lh, ll = split2(left)
    rh, rl = split2(right)
    return mm(jnp.concatenate([lh, ll, lh], axis=1), jnp.concatenate([rh, rh, rl], axis=0))


def chase(rows, piv_row_ref, panels):
    lanes = lax.broadcasted_iota(jnp.int32, (rows.shape[0], NB), 1).astype(F32)
    for m in panels:
        equal = rows == piv_row_ref[m : m + 1, :]
        hit = jnp.sum(jnp.where(equal, lanes + float(m * NB + 1), 0.0), axis=1, keepdims=True)
        hit = hit.astype(jnp.int32)
        rows = jnp.where(hit > 0, hit - 1, rows)
    return rows


def pick_kernel(place_ref, piv_row_ref, piv_col_ref, a_ref, first_ref, rest_ref, origin_ref):
    prow = place_ref[0]
    lane = lax.broadcasted_iota(jnp.int32, (NB, ROWS), 1)
    for k in range(PANELS):
        rows = chase(piv_col_ref[k * NB : (k + 1) * NB, :], piv_row_ref, range(k - 1, -1, -1))
        owner = (rows >> 7) & 31
        slot = ((rows >> 12) << 7) | (rows & 127)
        slot = jnp.where(owner == prow, slot, -1)
        onehot = jnp.where(lane == slot, 1.0, 0.0).astype(BF)
        first_ref[k * NB : (k + 1) * NB, :] = select_rows(onehot, a_ref[:, :NB])
        rest_ref[k * NB : (k + 1) * NB, :] = select_rows(onehot, a_ref[:, NB:])
    local = lax.broadcasted_iota(jnp.int32, (ROWS, 1), 0)
    rows = ((local >> 7) * PROW + prow) * NB + (local & 127)
    rows = chase(rows, piv_row_ref, range(PANELS - 1, -1, -1))
    origin_ref[...] = jnp.broadcast_to(rows, (ROWS, NB))


def place_of(origin):
    unit = (origin >> 2) & 31
    return (unit << 5) + 16 + ((origin >> 7) << 2) + (origin & 3)


def moved_rows(origin, gathered, kept):
    lane = lax.broadcasted_iota(jnp.int32, (ROWS, 1024), 1)
    onehot = jnp.where(lane == jnp.where(origin < TOP, place_of(origin), -1), 1.0, 0.0).astype(BF)
    return jnp.where(origin < TOP, select_rows(onehot, gathered), kept)


def column_kernel(origin_ref, gathered_ref, a_ref, out_ref):
    origin = origin_ref[:, :1]
    for unit in range(PROW):
        out_ref[unit * 16 : unit * 16 + 16, :] = gathered_ref[unit * 32 : unit * 32 + 16, :]
    out_ref[TOP:, :] = moved_rows(origin, gathered_ref[...], a_ref[:, :NB])


def exchange_first(picked, top):
    sent = jnp.concatenate([picked.reshape(PROW, 16, NB), top.reshape(PROW, 4, NB)], axis=1)
    got = lax.all_to_all(sent, "prow", 0, 0)
    chunk = jnp.concatenate([jnp.sum(got[:, :16], axis=0), got[:4, 16:].reshape(16, NB)], axis=0)
    sent = jnp.broadcast_to(chunk[None], (PROW, 32, NB))
    return lax.all_to_all(sent, "prow", 0, 0).reshape(PROW * 32, NB)


def exchange_rest(picked, top):
    sent = jnp.concatenate([picked.reshape(4, NB, REST), top.reshape(4, 32, REST)], axis=1)
    got = lax.all_to_all(sent, "prow", 0, 0, axis_index_groups=X_GROUPS)
    sent = jnp.concatenate(
        [jnp.sum(got[:, :NB], axis=0).reshape(8, 16, REST), got[0, NB:].reshape(8, 4, REST)], axis=1
    )
    got = lax.all_to_all(sent, "prow", 0, 0, axis_index_groups=Z_GROUPS)
    chunk = jnp.concatenate([jnp.sum(got[:, :16], axis=0), got[:4, 16:].reshape(16, REST)], axis=0)
    got = lax.all_to_all(
        jnp.broadcast_to(chunk[None], (8, 32, REST)), "prow", 0, 0, axis_index_groups=Z_GROUPS
    )
    got = got.reshape(256, REST)
    got = lax.all_to_all(
        jnp.broadcast_to(got[None], (4, 256, REST)), "prow", 0, 0, axis_index_groups=X_GROUPS
    )
    return got.reshape(PROW * 32, REST)


def spread_start(own):
    up = lax.ppermute(own, "pcol", [(q, q + 4) for q in range(4)])
    down = lax.ppermute(own, "pcol", [(q, q + 12) for q in range(4)])
    return up, down


def spread_columns(own, pcol):
    return spread_rest(own, *spread_start(own), pcol)


def spread_rest(own, up, down, pcol):
    near = jnp.where(pcol < 4, own, jnp.where(pcol < 8, up, down))
    half = near.shape[0] // 2
    left = lax.ppermute(near[:half], "pcol", [(q + 4, q + 8) for q in range(4)])
    right = lax.ppermute(near[half:], "pcol", [(q + 12, q + 8) for q in range(4)])
    far = (pcol >= 8) & (pcol < 12)
    near = jnp.where(far, jnp.concatenate([left, right], axis=0), near)
    across = lax.ppermute(near, "pcol", [(q, q ^ 2) for q in range(PCOL)])
    both = jnp.concatenate([near, across], axis=1)
    pair = lax.ppermute(both, "pcol", [(q, q ^ 1) for q in range(PCOL)])
    return near, across, pair


def lane_sum(mask, value):
    return jnp.sum(jnp.where(mask, value, 0.0), axis=1, keepdims=True)


def sub_sum(mask, value):
    return jnp.sum(jnp.where(mask, value, 0.0), axis=0, keepdims=True).astype(jnp.int32)


def iota(shape, axis):
    return lax.broadcasted_iota(jnp.int32, shape, axis)


def ranks(masks):
    count = len(masks)
    padded = -(-count // 8) * 8
    rows = [jnp.where(mask, 1.0, 0.0) for mask in masks]
    rows = rows + [jnp.zeros((1, NB), F32)] * (padded - count)
    before = jnp.where(iota((NB, NB), 0) < iota((NB, NB), 1), 1.0, 0.0).astype(BF)
    found = mm(jnp.concatenate(rows, axis=0).astype(BF), before)
    return [found[n : n + 1, :] for n in range(count)]


def slots(mask, rank, value, capacity):
    row = iota((capacity, NB), 0).astype(F32)
    return lane_sum(mask & (rank == row), value + 1.0).astype(jnp.int32) - 1


def onehot_of(column, width):
    return jnp.where(iota((column.shape[0], width), 1) == column, 1.0, 0.0).astype(BF)


def plan_kernel(pivots_ref, a_ref, send_ref, plan_ref, over_ref, source_ref, target_ref):
    prow = lax.axis_index("prow")
    x = prow >> 3
    z = prow & 7
    sub = iota((NB, NB), 0)
    lane = iota((NB, NB), 1)
    subf = sub.astype(F32)
    lane_row = iota((1, NB), 1)
    piv_row = [pivots_ref[m : m + 1, :] for m in range(PANELS)]
    piv_col = []
    for m in range(PANELS):
        piv_col.append(lane_sum(sub == lane, piv_row[m].astype(F32)).astype(jnp.int32))

    def met(m, rows):
        return sub_sum(piv_col[m] == rows, subf + float(m * NB + 1))

    source = []
    target = []
    for k in range(PANELS):
        rows = piv_row[k]
        for m in range(k - 1, -1, -1):
            hit = met(m, rows)
            rows = jnp.where(hit > 0, hit - 1, rows)
        source.append(rows)
        source_ref[k : k + 1, :] = rows
        rows = lane_row + k * NB
        for m in range(PANELS):
            if m == k:
                rows = jnp.where(rows == lane_row + k * NB, piv_row[k], rows)
                continue
            hit = met(m, rows)
            moved = jnp.where(hit > 0, hit - 1, rows)
            if m > k:
                look = sub_sum(sub + m * NB == rows, piv_col[m].astype(F32))
                moved = jnp.where(look > 0, look, moved)
            rows = moved
        target.append(rows)
        target_ref[k : k + 1, :] = rows

    def local_of(rows):
        return ((rows >> 12) << 7) | (rows & 127)

    def owner_of(rows):
        return (rows >> 7) & 31

    masks = [owner_of(source[k]) == prow for k in range(PANELS)]
    order = ranks(masks)
    pieces = [
        slots(masks[k], order[k], local_of(source[k]).astype(F32), 16) for k in range(PANELS)
    ]
    mine = target_ref[pl.ds(prow & 3, 1), :]
    leaves = (mine >= TOP) & (prow < PANELS)
    masks = [leaves & (((mine >> 10) & 3) == n) for n in range(4)]
    order = ranks(masks)
    lanef = lane_row.astype(F32)
    chosen = []
    for n in range(4):
        chosen.append(pieces[n])
        chosen.append(slots(masks[n], order[n], lanef, 48))
    send_ref[...] = select_rows(onehot_of(jnp.concatenate(chosen, axis=0), ROWS), a_ref[...])

    panel = source_ref[pl.ds(x, 1), :]
    panel_z = (panel >> 7) & 7
    panel_x = (panel >> 10) & 3
    here = panel_z == z
    masks = [here & (panel_x == n) for n in range(4)] + [here]
    order = ranks(masks)
    spot = jnp.zeros((1, NB), F32)
    for n in range(4):
        spot = spot + jnp.where(masks[n], order[n] + 64.0 * n, 0.0)
    wide = lambda column: jnp.broadcast_to(column, (column.shape[0], NB))
    plan_ref[0:32, :] = wide(slots(here, order[4], spot, 32))
    other = target_ref[pl.ds(z & 3, 1), :]
    along = (other >= TOP) & (z < PANELS) & (((other >> 10) & 3) == x)
    masks = [along & (((other >> 7) & 7) == n) for n in range(8)] + [along]
    order = ranks(masks)
    for n in range(8):
        plan_ref[32 + 16 * n : 48 + 16 * n, :] = wide(slots(masks[n], order[n], order[8], 16))
    zf = panel_z.astype(F32)
    zcol = lane_sum(sub == lane, zf)
    ahead = lane_sum((zf == zcol) & (lane < sub), 1.0)
    plan_ref[160:288, :] = wide((zcol * 32.0 + ahead).astype(jnp.int32))
    masks = [(target[k] >= TOP) & (owner_of(target[k]) == prow) for k in range(PANELS)]
    order = ranks(masks)
    row = iota((ROWS, NB), 0)
    total = jnp.zeros((ROWS, 1), F32)
    for k in range(PANELS):
        total = total + lane_sum(masks[k] & (local_of(target[k]) == row), order[k] + (16.0 * k + 1.0))
    plan_ref[288:544, :] = wide(total.astype(jnp.int32) - 1)
    unit = iota((PROW, NB), 0)
    over = jnp.zeros((PROW, 1), F32)
    for k in range(PANELS):
        leaves = target[k] >= TOP
        for mask, cap in (
            (owner_of(source[k]) == unit, 16.0),
            (((source[k] >> 7) & 7) == unit, 32.0),
            (leaves & (((target[k] >> 10) & 3) == unit), 48.0),
            (leaves & (owner_of(target[k]) == unit), 16.0),
        ):
            over = jnp.maximum(over, lane_sum(mask, 1.0) - cap)
    over = jnp.max(over, axis=0, keepdims=True)
    over_ref[...] = jnp.broadcast_to(over, (8, NB)).astype(jnp.int32)


def turn_kernel(plan_ref, got_ref, first_ref, rest_ref):
    got = got_ref[...].reshape(256, COLS)
    rows = select_rows(onehot_of(plan_ref[0:32, :1], 256), got)
    moved = plan_ref[32:160, :1]
    moved = jnp.where(moved < 0, -1, moved + 16)
    sent = select_rows(onehot_of(moved, 64), got[:64])
    for n in range(8):
        first_ref[n, 0:32, :] = rows[:, :NB]
        rest_ref[n, 0:32, :] = rows[:, NB:]
        first_ref[n, 32:48, :] = sent[n * 16 : n * 16 + 16, :NB]
        rest_ref[n, 32:48, :] = sent[n * 16 : n * 16 + 16, NB:]


def lead_kernel(plan_ref, got_ref, lead_ref):
    got = jnp.concatenate([got_ref[n, 0:32, :] for n in range(8)], axis=0)
    lead_ref[0:NB, :] = select_rows(onehot_of(plan_ref[160:288, :1], 256), got)
    for n in range(4):
        lead_ref[NB + n * 16 : NB + n * 16 + 16, :] = got_ref[n, 32:48, :]


def panel_kernel(plan_ref, lead_ref, got_ref, near_ref, across_ref, pair_ref, send_ref, moved_ref):
    panel = lax.axis_index("prow") >> 3
    got = jnp.concatenate([got_ref[n, 0:32, :] for n in range(8)], axis=0)
    rows = select_rows(onehot_of(plan_ref[160:288, :1], 256), got)
    for n in range(4):
        send_ref[n, :, :NB] = lead_ref[0:NB, :]
        send_ref[n, :, NB:COLS] = rows

    def store_send(index, value):
        @pl.when(index != panel)
        def _():
            spot = lane_block(COLS // NB + jnp.where(index < panel, index, index - 1))
            for n in range(4):
                send_ref[n, :, spot] = value

    def store_moved(index, value):
        moved_ref[:, lane_block(index)] = value

    put_columns(near_ref, across_ref, pair_ref, slice(0, NB), store_send)
    put_columns(near_ref, across_ref, pair_ref, slice(NB, NB + 64), store_moved)


def put_columns(near_ref, across_ref, pair_ref, rows, store):
    kind = lax.axis_index("pcol") & 3
    store(kind, near_ref[rows, :])
    store(kind ^ 2, across_ref[rows, :])
    store(kind ^ 1, pair_ref[rows, :NB])
    store(kind ^ 3, pair_ref[rows, NB:])


def lane_block(index):
    return pl.ds(pl.multiple_of(index * NB, NB), NB)


def own_rows_kernel(plan_ref, lead_ref, got_ref, a_ref, out_ref):
    slot = plan_ref[288:544, :1]
    rest = jnp.concatenate([got_ref[n, 32:48, :] for n in range(4)], axis=0)
    moved = jnp.concatenate([lead_ref[NB : NB + 64, :], rest], axis=1)
    out_ref[...] = jnp.where(slot >= 0, select_rows(onehot_of(slot, 64), moved), a_ref[...])


def panel_rows_kernel(plan_ref, moved_ref, near_ref, across_ref, pair_ref, out_ref):
    slot = plan_ref[288:544, :1]

    def store(index, value):
        out_ref[:, lane_block(index)] = value

    put_columns(near_ref, across_ref, pair_ref, slice(0, ROWS), store)
    moved = select_rows(onehot_of(slot, 64), moved_ref[...])
    out_ref[...] = jnp.where(slot >= 0, moved, out_ref[...])


def factor_kernel(
    top_ref, left_ref, right_ref, lower_ref, upper_ref, out_ref, z_ref, y_ref, m_ref, u_ref, d_ref
):
    prow = lax.axis_index("prow")
    pcol = lax.axis_index("pcol")
    for k in range(PANELS):
        rows = slice(k * NB, k * NB + NB)
        for spot in range(PANELS - 1):
            block = spot if spot < k else spot + 1
            z_ref[rows, block * NB : block * NB + NB] = top_ref[
                rows, COLS + spot * NB : COLS + spot * NB + NB
            ]
    z_ref[TOP:, :] = left_ref[...]
    for k in range(PANELS):
        s = k * NB
        e = s + NB
        before = top_ref if k == 0 else y_ref
        multipliers = dot3(z_ref[e:, s:e], upper_ref[k])
        z_ref[e:, s:e] = multipliers
        mh, ml = split2(multipliers)
        m3 = jnp.concatenate([mh, ml, mh], axis=1)
        m_ref[:, 3 * s : 3 * e] = m3[TOP - e :]
        lh, ll = split2(lower_ref[k])
        l3 = jnp.concatenate([lh, ll, lh], axis=1)
        if e < TOP:
            bh, bl = split2(z_ref[s:e, e:])
            corner = mm(l3, jnp.concatenate([bh, bh, bl], axis=0))
            z_ref[s:e, e:] = corner
            uh, ul = split2(corner)
            z_ref[e:, e:] = z_ref[e:, e:] - mm(m3, jnp.concatenate([uh, uh, ul], axis=0))
        d_ref[s:e, :] = before[s:e, :NB]
        bh, bl = split2(before[s:e, :COLS])
        upper_rows = mm(l3, jnp.concatenate([bh, bh, bl], axis=0))
        y_ref[s:e, :] = upper_rows
        uh, ul = split2(upper_rows)
        u3 = jnp.concatenate([uh, uh, ul], axis=0)
        u_ref[3 * s : 3 * e, :] = u3
        if e < TOP:
            y_ref[e:TOP, :] = before[e:TOP, :COLS] - mm(m3[: TOP - e], u3)
    out_ref[...] = right_ref[...] - mm(m_ref[...], u_ref[...])
    panel_cols = lane_block(pcol & 3)
    top_rows = pl.ds(pl.multiple_of((prow & 3) * NB, NB), NB)

    @pl.when(pcol < PANELS)
    def _():
        out_ref[:, :NB] = z_ref[TOP:, panel_cols]

    @pl.when(prow < PANELS)
    def _():
        out_ref[:NB, :] = y_ref[top_rows, :]

    @pl.when((prow < PANELS) & (pcol < PANELS))
    def _():
        out_ref[:NB, :NB] = jnp.where(
            prow == pcol, d_ref[top_rows, :], z_ref[top_rows, panel_cols]
        )


def kernel_call(body, shapes, scratch=()):
    def call(*args):
        return pl.pallas_call(
            body,
            in_specs=[VMEM] * len(args),
            out_specs=[VMEM] * len(shapes),
            out_shape=[jax.ShapeDtypeStruct(shape, kind) for shape, kind in shapes],
            scratch_shapes=list(scratch),
            compiler_params=pltpu.CompilerParams(vmem_limit_bytes=KERNEL_VMEM),
        )(*args)

    return call


def factor(*args):
    return pl.pallas_call(
        factor_kernel,
        in_specs=[VMEM] * len(args),
        out_specs=VMEM,
        out_shape=jax.ShapeDtypeStruct((ROWS, COLS), F32),
        scratch_shapes=[
            pltpu.VMEM((TOP + ROWS, TOP), F32),
            pltpu.VMEM((TOP, COLS), F32),
            pltpu.VMEM((ROWS, 3 * TOP), BF),
            pltpu.VMEM((3 * TOP, COLS), BF),
            pltpu.VMEM((TOP, NB), F32),
        ],
        compiler_params=pltpu.CompilerParams(vmem_limit_bytes=FACTOR_VMEM),
    )(*args)


def along(value, groups):
    return lax.all_to_all(value, "prow", 0, 0, axis_index_groups=groups)


def slotted(send, plan, matrix, lower_inverse, upper_inverse):
    pcol = lax.axis_index("pcol")
    got = along(send.reshape(4, 64, COLS), X_GROUPS)
    first, rest = kernel_call(turn_kernel, [((8, 48, NB), F32), ((8, 48, REST), F32)])(plan, got)
    first = along(first, Z_GROUPS)
    rest = along(rest, Z_GROUPS)
    (lead,) = kernel_call(lead_kernel, [((NB + 64, NB), F32)])(plan, first)
    ends = spread_start(lead)
    late = spread_rest(lead, *ends, pcol)
    send, moved = kernel_call(
        panel_kernel, [((4, NB, WIDE - NB), F32), ((64, TOP), F32)]
    )(plan, lead, rest, *late)
    top = along(send, X_GROUPS).reshape(TOP, WIDE - NB)
    block = matrix[:, :NB]
    ends = spread_start(block)
    raw = spread_rest(block, *ends, pcol)
    (right,) = kernel_call(own_rows_kernel, [((ROWS, COLS), F32)])(plan, lead, rest, matrix)
    (left,) = kernel_call(panel_rows_kernel, [((ROWS, TOP), F32)])(plan, moved, *raw)
    return factor(top, left, right, lower_inverse, upper_inverse)


def dense_rows_kernel(
    origin_ref, gathered_ref, a_ref, own_ref, near_ref, across_ref, pair_ref, top_ref, left_ref, right_ref
):
    def store_corner(index, value):
        for k in range(PANELS):

            @pl.when(index != k)
            def _():
                spot = lane_block(COLS // NB + jnp.where(index < k, index, index - 1))
                top_ref[k * NB : k * NB + NB, spot] = value[k * NB : k * NB + NB]

    def store_left(index, value):
        left_ref[:, lane_block(index)] = value

    put_columns(near_ref, across_ref, pair_ref, slice(0, TOP), store_corner)
    put_columns(near_ref, across_ref, pair_ref, slice(TOP, TOP + ROWS), store_left)
    top_ref[:, :NB] = own_ref[:TOP, :]
    right_ref[:, :NB] = own_ref[TOP:, :]
    for unit in range(PROW):
        top_ref[unit * 16 : unit * 16 + 16, NB:COLS] = gathered_ref[unit * 32 : unit * 32 + 16, :]
    origin = origin_ref[:, :1]

    @pl.loop(0, REST // NB)
    def _(c):
        right_ref[:, lane_block(c + 1)] = moved_rows(
            origin, gathered_ref[:, lane_block(c)], a_ref[:, lane_block(c + 1)]
        )


def dense(pivots, matrix, lower_inverse, upper_inverse):
    prow = lax.axis_index("prow")
    pcol = lax.axis_index("pcol")
    place = jnp.stack([prow, pcol]).astype(jnp.int32)
    picked_first, picked_rest, origin = pl.pallas_call(
        pick_kernel,
        in_specs=[SMEM, VMEM, VMEM, VMEM],
        out_specs=[VMEM] * 3,
        out_shape=[
            jax.ShapeDtypeStruct((TOP, NB), F32),
            jax.ShapeDtypeStruct((TOP, REST), F32),
            jax.ShapeDtypeStruct((ROWS, NB), jnp.int32),
        ],
    )(place, pivots.reshape(PANELS, NB), pivots.reshape(TOP, 1), matrix)
    gathered_first = exchange_first(picked_first, matrix[:NB, :NB])
    (own,) = kernel_call(column_kernel, [((TOP + ROWS, NB), F32)])(origin, gathered_first, matrix)
    near, across, pair = spread_columns(own, pcol)
    gathered_rest = exchange_rest(picked_rest, matrix[:NB, NB:])
    top, left, right = kernel_call(
        dense_rows_kernel,
        [((TOP, WIDE - NB), F32), ((ROWS, TOP), F32), ((ROWS, COLS), F32)],
    )(origin, gathered_rest, matrix, own, near, across, pair)
    return factor(top, left, right, lower_inverse, upper_inverse)


def per_device(matrix, pivots, lower_inverse, upper_inverse):
    send, plan, over = kernel_call(
        plan_kernel,
        [((256, COLS), F32), ((544, NB), jnp.int32), ((8, NB), jnp.int32)],
        [pltpu.VMEM((8, NB), jnp.int32), pltpu.VMEM((8, NB), jnp.int32)],
    )(pivots.reshape(PANELS, NB), matrix)
    return lax.cond(
        over[0, 0] <= 0,
        lambda: slotted(send, plan, matrix, lower_inverse, upper_inverse),
        lambda: dense(pivots, matrix, lower_inverse, upper_inverse),
    )


def solution(mesh):
    in_specs = (P("prow", "pcol"), P(), P(), P())
    out_specs = P("prow", "pcol")
    return jax.shard_map(
        per_device, mesh=mesh, in_specs=in_specs, out_specs=out_specs, check_vma=False
    )
```

```python
import jax
import jax.numpy as jnp
from jax import lax
from jax.experimental import pallas as pl
from jax.experimental.pallas import tpu as pltpu
from jax.sharding import PartitionSpec as P

NB = 128
PANELS = 4
TOP = NB * PANELS
PROW = 32
PCOL = 16
ROWS = 256
COLS = 768
REST = COLS - NB
WIDE = TOP + COLS
KERNEL_VMEM = 20 << 20
FACTOR_VMEM = 28 << 20
BF = jnp.bfloat16
F32 = jnp.float32
X_GROUPS = [[x * 8 + z for x in range(4)] for z in range(8)]
Z_GROUPS = [[x * 8 + z for z in range(8)] for x in range(4)]
VMEM = pl.BlockSpec(memory_space=pltpu.VMEM)
SMEM = pl.BlockSpec(memory_space=pltpu.SMEM)
HBM = pl.BlockSpec(memory_space=pltpu.HBM)


def mm(left, right):
    return lax.dot_general(left, right, (((1,), (0,)), ((), ())), preferred_element_type=F32)


def split2(value):
    high = value.astype(BF)
    low = (value - high.astype(F32)).astype(BF)
    return high, low


def select_rows(onehot, value):
    first = value.astype(BF)
    rest = value - first.astype(F32)
    second = rest.astype(BF)
    third = (rest - second.astype(F32)).astype(BF)
    return mm(onehot, first) + mm(onehot, second) + mm(onehot, third)


def dot3(left, right):
    lh, ll = split2(left)
    rh, rl = split2(right)
    return mm(jnp.concatenate([lh, ll, lh], axis=1), jnp.concatenate([rh, rh, rl], axis=0))


def chase(rows, piv_row_ref, panels):
    lanes = lax.broadcasted_iota(jnp.int32, (rows.shape[0], NB), 1).astype(F32)
    for m in panels:
        equal = rows == piv_row_ref[m : m + 1, :]
        hit = jnp.sum(jnp.where(equal, lanes + float(m * NB + 1), 0.0), axis=1, keepdims=True)
        hit = hit.astype(jnp.int32)
        rows = jnp.where(hit > 0, hit - 1, rows)
    return rows


def pick_kernel(place_ref, piv_row_ref, piv_col_ref, a_ref, first_ref, rest_ref, origin_ref):
    prow = place_ref[0]
    lane = lax.broadcasted_iota(jnp.int32, (NB, ROWS), 1)
    for k in range(PANELS):
        rows = chase(piv_col_ref[k * NB : (k + 1) * NB, :], piv_row_ref, range(k - 1, -1, -1))
        owner = (rows >> 7) & 31
        slot = ((rows >> 12) << 7) | (rows & 127)
        slot = jnp.where(owner == prow, slot, -1)
        onehot = jnp.where(lane == slot, 1.0, 0.0).astype(BF)
        first_ref[k * NB : (k + 1) * NB, :] = select_rows(onehot, a_ref[:, :NB])
        rest_ref[k * NB : (k + 1) * NB, :] = select_rows(onehot, a_ref[:, NB:])
    local = lax.broadcasted_iota(jnp.int32, (ROWS, 1), 0)
    rows = ((local >> 7) * PROW + prow) * NB + (local & 127)
    rows = chase(rows, piv_row_ref, range(PANELS - 1, -1, -1))
    origin_ref[...] = jnp.broadcast_to(rows, (ROWS, NB))


def place_of(origin):
    unit = (origin >> 2) & 31
    return (unit << 5) + 16 + ((origin >> 7) << 2) + (origin & 3)


def moved_rows(origin, gathered, kept):
    lane = lax.broadcasted_iota(jnp.int32, (ROWS, 1024), 1)
    onehot = jnp.where(lane == jnp.where(origin < TOP, place_of(origin), -1), 1.0, 0.0).astype(BF)
    return jnp.where(origin < TOP, select_rows(onehot, gathered), kept)


def column_kernel(origin_ref, gathered_ref, a_ref, out_ref):
    origin = origin_ref[:, :1]
    for unit in range(PROW):
        out_ref[unit * 16 : unit * 16 + 16, :] = gathered_ref[unit * 32 : unit * 32 + 16, :]
    out_ref[TOP:, :] = moved_rows(origin, gathered_ref[...], a_ref[:, :NB])


def exchange_first(picked, top):
    sent = jnp.concatenate([picked.reshape(PROW, 16, NB), top.reshape(PROW, 4, NB)], axis=1)
    got = lax.all_to_all(sent, "prow", 0, 0)
    chunk = jnp.concatenate([jnp.sum(got[:, :16], axis=0), got[:4, 16:].reshape(16, NB)], axis=0)
    sent = jnp.broadcast_to(chunk[None], (PROW, 32, NB))
    return lax.all_to_all(sent, "prow", 0, 0).reshape(PROW * 32, NB)


def exchange_rest(picked, top):
    sent = jnp.concatenate([picked.reshape(4, NB, REST), top.reshape(4, 32, REST)], axis=1)
    got = lax.all_to_all(sent, "prow", 0, 0, axis_index_groups=X_GROUPS)
    sent = jnp.concatenate(
        [jnp.sum(got[:, :NB], axis=0).reshape(8, 16, REST), got[0, NB:].reshape(8, 4, REST)], axis=1
    )
    got = lax.all_to_all(sent, "prow", 0, 0, axis_index_groups=Z_GROUPS)
    chunk = jnp.concatenate([jnp.sum(got[:, :16], axis=0), got[:4, 16:].reshape(16, REST)], axis=0)
    got = lax.all_to_all(
        jnp.broadcast_to(chunk[None], (8, 32, REST)), "prow", 0, 0, axis_index_groups=Z_GROUPS
    )
    got = got.reshape(256, REST)
    got = lax.all_to_all(
        jnp.broadcast_to(got[None], (4, 256, REST)), "prow", 0, 0, axis_index_groups=X_GROUPS
    )
    return got.reshape(PROW * 32, REST)


def spread_start(own):
    up = lax.ppermute(own, "pcol", [(q, q + 4) for q in range(4)])
    down = lax.ppermute(own, "pcol", [(q, q + 12) for q in range(4)])
    return up, down


def spread_columns(own, pcol):
    return spread_rest(own, *spread_start(own), pcol)


def spread_rest(own, up, down, pcol):
    near = jnp.where(pcol < 4, own, jnp.where(pcol < 8, up, down))
    half = near.shape[0] // 2
    left = lax.ppermute(near[:half], "pcol", [(q + 4, q + 8) for q in range(4)])
    right = lax.ppermute(near[half:], "pcol", [(q + 12, q + 8) for q in range(4)])
    far = (pcol >= 8) & (pcol < 12)
    near = jnp.where(far, jnp.concatenate([left, right], axis=0), near)
    return [near] + [lax.ppermute(near, "pcol", [(q, q ^ n) for q in range(PCOL)]) for n in (1, 2, 3)]


def lane_sum(mask, value):
    return jnp.sum(jnp.where(mask, value, 0.0), axis=1, keepdims=True)


def sub_sum(mask, value):
    return jnp.sum(jnp.where(mask, value, 0.0), axis=0, keepdims=True).astype(jnp.int32)


def iota(shape, axis):
    return lax.broadcasted_iota(jnp.int32, shape, axis)


def ranks(masks):
    count = len(masks)
    padded = -(-count // 8) * 8
    rows = [jnp.where(mask, 1.0, 0.0) for mask in masks]
    rows = rows + [jnp.zeros((1, NB), F32)] * (padded - count)
    before = jnp.where(iota((NB, NB), 0) < iota((NB, NB), 1), 1.0, 0.0).astype(BF)
    found = mm(jnp.concatenate(rows, axis=0).astype(BF), before)
    return [found[n : n + 1, :] for n in range(count)]


def slots(mask, rank, value, capacity):
    row = iota((capacity, NB), 0).astype(F32)
    return lane_sum(mask & (rank == row), value + 1.0).astype(jnp.int32) - 1


def onehot_of(column, width):
    return jnp.where(iota((column.shape[0], width), 1) == column, 1.0, 0.0).astype(BF)


def plan_kernel(pivots_ref, a_ref, send_ref, plan_ref, over_ref, source_ref, target_ref):
    prow = lax.axis_index("prow")
    x = prow >> 3
    z = prow & 7
    sub = iota((NB, NB), 0)
    lane = iota((NB, NB), 1)
    subf = sub.astype(F32)
    lane_row = iota((1, NB), 1)
    piv_row = [pivots_ref[m : m + 1, :] for m in range(PANELS)]
    piv_col = []
    for m in range(PANELS):
        piv_col.append(lane_sum(sub == lane, piv_row[m].astype(F32)).astype(jnp.int32))

    def met(m, rows):
        return sub_sum(piv_col[m] == rows, subf + float(m * NB + 1))

    source = []
    target = []
    for k in range(PANELS):
        rows = piv_row[k]
        for m in range(k - 1, -1, -1):
            hit = met(m, rows)
            rows = jnp.where(hit > 0, hit - 1, rows)
        source.append(rows)
        source_ref[k : k + 1, :] = rows
        rows = lane_row + k * NB
        for m in range(PANELS):
            if m == k:
                rows = jnp.where(rows == lane_row + k * NB, piv_row[k], rows)
                continue
            hit = met(m, rows)
            moved = jnp.where(hit > 0, hit - 1, rows)
            if m > k:
                look = sub_sum(sub + m * NB == rows, piv_col[m].astype(F32))
                moved = jnp.where(look > 0, look, moved)
            rows = moved
        target.append(rows)
        target_ref[k : k + 1, :] = rows

    def local_of(rows):
        return ((rows >> 12) << 7) | (rows & 127)

    def owner_of(rows):
        return (rows >> 7) & 31

    masks = [owner_of(source[k]) == prow for k in range(PANELS)]
    order = ranks(masks)
    pieces = [
        slots(masks[k], order[k], local_of(source[k]).astype(F32), 16) for k in range(PANELS)
    ]
    mine = target_ref[pl.ds(prow & 3, 1), :]
    leaves = (mine >= TOP) & (prow < PANELS)
    masks = [leaves & (((mine >> 10) & 3) == n) for n in range(4)]
    order = ranks(masks)
    lanef = lane_row.astype(F32)
    chosen = []
    for n in range(4):
        chosen.append(pieces[n])
        chosen.append(slots(masks[n], order[n], lanef, 48))
    send_ref[...] = select_rows(onehot_of(jnp.concatenate(chosen, axis=0), ROWS), a_ref[...])

    panel = source_ref[pl.ds(x, 1), :]
    panel_z = (panel >> 7) & 7
    panel_x = (panel >> 10) & 3
    here = panel_z == z
    masks = [here & (panel_x == n) for n in range(4)] + [here]
    order = ranks(masks)
    spot = jnp.zeros((1, NB), F32)
    for n in range(4):
        spot = spot + jnp.where(masks[n], order[n] + 64.0 * n, 0.0)
    wide = lambda column: jnp.broadcast_to(column, (column.shape[0], NB))
    plan_ref[0:32, :] = wide(slots(here, order[4], spot, 32))
    other = target_ref[pl.ds(z & 3, 1), :]
    along = (other >= TOP) & (z < PANELS) & (((other >> 10) & 3) == x)
    masks = [along & (((other >> 7) & 7) == n) for n in range(8)] + [along]
    order = ranks(masks)
    for n in range(8):
        plan_ref[32 + 16 * n : 48 + 16 * n, :] = wide(slots(masks[n], order[n], order[8], 16))
    zf = panel_z.astype(F32)
    zcol = lane_sum(sub == lane, zf)
    ahead = lane_sum((zf == zcol) & (lane < sub), 1.0)
    plan_ref[160:288, :] = wide((zcol * 32.0 + ahead).astype(jnp.int32))
    masks = [(target[k] >= TOP) & (owner_of(target[k]) == prow) for k in range(PANELS)]
    order = ranks(masks)
    row = iota((ROWS, NB), 0)
    total = jnp.zeros((ROWS, 1), F32)
    for k in range(PANELS):
        total = total + lane_sum(masks[k] & (local_of(target[k]) == row), order[k] + (16.0 * k + 1.0))
    plan_ref[288:544, :] = wide(total.astype(jnp.int32) - 1)
    unit = iota((PROW, NB), 0)
    over = jnp.zeros((PROW, 1), F32)
    for k in range(PANELS):
        leaves = target[k] >= TOP
        for mask, cap in (
            (owner_of(source[k]) == unit, 16.0),
            (((source[k] >> 7) & 7) == unit, 32.0),
            (leaves & (((target[k] >> 10) & 3) == unit), 48.0),
            (leaves & (owner_of(target[k]) == unit), 16.0),
        ):
            over = jnp.maximum(over, lane_sum(mask, 1.0) - cap)
    over = jnp.max(over, axis=0, keepdims=True)
    over_ref[...] = jnp.broadcast_to(over, (8, NB)).astype(jnp.int32)


def turn_kernel(plan_ref, got_ref, first_ref, rest_ref):
    got = got_ref[...].reshape(256, COLS)
    rows = select_rows(onehot_of(plan_ref[0:32, :1], 256), got)
    moved = plan_ref[32:160, :1]
    moved = jnp.where(moved < 0, -1, moved + 16)
    sent = select_rows(onehot_of(moved, 64), got[:64])
    for n in range(8):
        first_ref[n, 0:32, :] = rows[:, :NB]
        rest_ref[n, 0:32, :] = rows[:, NB:]
        first_ref[n, 32:48, :] = sent[n * 16 : n * 16 + 16, :NB]
        rest_ref[n, 32:48, :] = sent[n * 16 : n * 16 + 16, NB:]


def lead_kernel(plan_ref, got_ref, a_ref, lead_ref, rows_ref):
    got = jnp.concatenate([got_ref[n, 0:32, :] for n in range(8)], axis=0)
    lead_ref[...] = select_rows(onehot_of(plan_ref[160:288, :1], 256), got)
    moved = jnp.concatenate([got_ref[n, 32:48, :] for n in range(4)], axis=0)
    slot = plan_ref[288:544, :1]
    moved = select_rows(onehot_of(slot, 64), moved)
    rows_ref[...] = jnp.where(slot >= 0, moved, a_ref[:, :NB])


def panel_kernel(plan_ref, lead_ref, got_ref, *refs):
    blocks, send_ref, full_ref, sems = refs[:4], refs[4], refs[5], refs[6]
    panel = lax.axis_index("prow") >> 3
    got = jnp.concatenate([got_ref[n, 0:32, :] for n in range(8)], axis=0)
    full_ref[:, :NB] = lead_ref[...]
    full_ref[:, NB:COLS] = select_rows(onehot_of(plan_ref[160:288, :1], 256), got)

    def store(index, value):
        @pl.when(index != panel)
        def _():
            spot = COLS // NB + jnp.where(index < panel, index, index - 1)
            full_ref[:, lane_block(spot)] = value

    put_columns(blocks, slice(0, NB), store)
    copies = [
        pltpu.make_async_copy(full_ref, send_ref.at[n], sems.at[n]) for n in range(4)
    ]
    for copy in copies:
        copy.start()
    for copy in copies:
        copy.wait()


def put_columns(block_refs, rows, store):
    kind = lax.axis_index("pcol") & 3
    for n, ref in enumerate(block_refs):
        store(kind ^ n, ref[rows, :])


def lane_block(index):
    return pl.ds(pl.multiple_of(index * NB, NB), NB)


def own_rows_kernel(plan_ref, rows_ref, got_ref, a_ref, out_ref):
    slot = plan_ref[288:544, :1]
    moved = jnp.concatenate([got_ref[n, 32:48, :] for n in range(4)], axis=0)
    moved = select_rows(onehot_of(slot, 64), moved)
    out_ref[:, :NB] = rows_ref[...]
    out_ref[:, NB:] = jnp.where(slot >= 0, moved, a_ref[:, NB:])


def factor_kernel(
    top_ref, right_ref, lower_ref, upper_ref, left0_ref, left1_ref, left2_ref, left3_ref,
    result_ref, z_ref, y_ref, m_ref, u_ref, d_ref, out_ref, sems,
):
    prow = lax.axis_index("prow")
    pcol = lax.axis_index("pcol")
    fetches = []
    for n, ref in enumerate((left0_ref, left1_ref, left2_ref, left3_ref)):
        target = z_ref.at[TOP : TOP + ROWS, lane_block((pcol & 3) ^ n)]
        fetches.append(pltpu.make_async_copy(ref, target, sems.at[n]))
    fetches.append(pltpu.make_async_copy(right_ref, out_ref, sems.at[4]))
    for fetch in fetches:
        fetch.start()
    for k in range(PANELS):
        rows = slice(k * NB, k * NB + NB)
        for spot in range(PANELS - 1):
            block = spot if spot < k else spot + 1
            z_ref[rows, block * NB : block * NB + NB] = top_ref[
                rows, COLS + spot * NB : COLS + spot * NB + NB
            ]
    for fetch in fetches[:4]:
        fetch.wait()
    for k in range(PANELS):
        s = k * NB
        e = s + NB
        before = top_ref if k == 0 else y_ref
        multipliers = dot3(z_ref[e:, s:e], upper_ref[k])
        z_ref[e:, s:e] = multipliers
        mh, ml = split2(multipliers)
        m3 = jnp.concatenate([mh, ml, mh], axis=1)
        m_ref[:, 3 * s : 3 * e] = m3[TOP - e :]
        lh, ll = split2(lower_ref[k])
        l3 = jnp.concatenate([lh, ll, lh], axis=1)
        if e < TOP:
            bh, bl = split2(z_ref[s:e, e:])
            corner = mm(l3, jnp.concatenate([bh, bh, bl], axis=0))
            z_ref[s:e, e:] = corner
            uh, ul = split2(corner)
            z_ref[e:, e:] = z_ref[e:, e:] - mm(m3, jnp.concatenate([uh, uh, ul], axis=0))
        d_ref[s:e, :] = before[s:e, :NB]
        bh, bl = split2(before[s:e, :COLS])
        upper_rows = mm(l3, jnp.concatenate([bh, bh, bl], axis=0))
        y_ref[s:e, :] = upper_rows
        uh, ul = split2(upper_rows)
        u3 = jnp.concatenate([uh, uh, ul], axis=0)
        u_ref[3 * s : 3 * e, :] = u3
        if e < TOP:
            y_ref[e:TOP, :] = before[e:TOP, :COLS] - mm(m3[: TOP - e], u3)
    fetches[4].wait()
    out_ref[...] = out_ref[...] - mm(m_ref[...], u_ref[...])
    panel_cols = lane_block(pcol & 3)
    top_rows = pl.ds(pl.multiple_of((prow & 3) * NB, NB), NB)

    @pl.when(pcol < PANELS)
    def _():
        out_ref[:, :NB] = z_ref[TOP:, panel_cols]

    @pl.when(prow < PANELS)
    def _():
        out_ref[:NB, :] = y_ref[top_rows, :]

    @pl.when((prow < PANELS) & (pcol < PANELS))
    def _():
        out_ref[:NB, :NB] = jnp.where(
            prow == pcol, d_ref[top_rows, :], z_ref[top_rows, panel_cols]
        )

    copy = pltpu.make_async_copy(out_ref, result_ref, sems.at[5])
    copy.start()
    copy.wait()


def kernel_call(body, shapes, scratch=(), out=VMEM):
    def call(*args):
        return pl.pallas_call(
            body,
            in_specs=[VMEM] * len(args),
            out_specs=[out] * len(shapes),
            out_shape=[jax.ShapeDtypeStruct(shape, kind) for shape, kind in shapes],
            scratch_shapes=list(scratch),
            compiler_params=pltpu.CompilerParams(vmem_limit_bytes=KERNEL_VMEM),
        )(*args)

    return call


def factor(top, right, lower_inverse, upper_inverse, *left):
    right, *left = [
        pltpu.with_memory_space_constraint(value, pltpu.HBM) for value in (right, *left)
    ]
    args = (top, right, lower_inverse, upper_inverse, *left)
    result = pl.pallas_call(
        factor_kernel,
        in_specs=[VMEM, HBM, VMEM, VMEM] + [HBM] * 4,
        out_specs=HBM,
        out_shape=jax.ShapeDtypeStruct((ROWS, COLS), F32),
        scratch_shapes=[
            pltpu.VMEM((TOP + ROWS, TOP), F32),
            pltpu.VMEM((TOP, COLS), F32),
            pltpu.VMEM((ROWS, 3 * TOP), BF),
            pltpu.VMEM((3 * TOP, COLS), BF),
            pltpu.VMEM((TOP, NB), F32),
            pltpu.VMEM((ROWS, COLS), F32),
            pltpu.SemaphoreType.DMA((6,)),
        ],
        compiler_params=pltpu.CompilerParams(vmem_limit_bytes=FACTOR_VMEM),
    )(*args)
    return pltpu.with_memory_space_constraint(result, pltpu.HBM)


def along(value, groups):
    return lax.all_to_all(value, "prow", 0, 0, axis_index_groups=groups)


def slotted(send, plan, matrix, lower_inverse, upper_inverse):
    pcol = lax.axis_index("pcol")
    got = along(send.reshape(4, 64, COLS), X_GROUPS)
    first, rest = kernel_call(turn_kernel, [((8, 48, NB), F32), ((8, 48, REST), F32)])(plan, got)
    first = along(first, Z_GROUPS)
    rest = along(rest, Z_GROUPS)
    lead, rows = kernel_call(lead_kernel, [((NB, NB), F32), ((ROWS, NB), F32)])(
        plan, first, matrix
    )
    ends = spread_start(lead)
    late = spread_rest(lead, *ends, pcol)
    (send,) = kernel_call(
        panel_kernel,
        [((4, NB, WIDE - NB), F32)],
        [pltpu.VMEM((NB, WIDE - NB), F32), pltpu.SemaphoreType.DMA((4,))],
        HBM,
    )(plan, lead, rest, *late)
    top = along(send, X_GROUPS).reshape(TOP, WIDE - NB)
    ends = spread_start(rows)
    left = spread_rest(rows, *ends, pcol)
    (right,) = kernel_call(own_rows_kernel, [((ROWS, COLS), F32)])(plan, rows, rest, matrix)
    return factor(top, right, lower_inverse, upper_inverse, *left)


def dense_rows_kernel(
    origin_ref, gathered_ref, a_ref, own_ref, block0_ref, block1_ref, block2_ref, block3_ref,
    top_ref, right_ref,
):
    def store_corner(index, value):
        for k in range(PANELS):

            @pl.when(index != k)
            def _():
                spot = lane_block(COLS // NB + jnp.where(index < k, index, index - 1))
                top_ref[k * NB : k * NB + NB, spot] = value[k * NB : k * NB + NB]

    put_columns((block0_ref, block1_ref, block2_ref, block3_ref), slice(0, TOP), store_corner)
    top_ref[:, :NB] = own_ref[:TOP, :]
    right_ref[:, :NB] = own_ref[TOP:, :]
    for unit in range(PROW):
        top_ref[unit * 16 : unit * 16 + 16, NB:COLS] = gathered_ref[unit * 32 : unit * 32 + 16, :]
    origin = origin_ref[:, :1]

    @pl.loop(0, REST // NB)
    def _(c):
        right_ref[:, lane_block(c + 1)] = moved_rows(
            origin, gathered_ref[:, lane_block(c)], a_ref[:, lane_block(c + 1)]
        )


def dense(pivots, matrix, lower_inverse, upper_inverse):
    prow = lax.axis_index("prow")
    pcol = lax.axis_index("pcol")
    place = jnp.stack([prow, pcol]).astype(jnp.int32)
    picked_first, picked_rest, origin = pl.pallas_call(
        pick_kernel,
        in_specs=[SMEM, VMEM, VMEM, VMEM],
        out_specs=[VMEM] * 3,
        out_shape=[
            jax.ShapeDtypeStruct((TOP, NB), F32),
            jax.ShapeDtypeStruct((TOP, REST), F32),
            jax.ShapeDtypeStruct((ROWS, NB), jnp.int32),
        ],
    )(place, pivots.reshape(PANELS, NB), pivots.reshape(TOP, 1), matrix)
    gathered_first = exchange_first(picked_first, matrix[:NB, :NB])
    (own,) = kernel_call(column_kernel, [((TOP + ROWS, NB), F32)])(origin, gathered_first, matrix)
    blocks = spread_columns(own, pcol)
    gathered_rest = exchange_rest(picked_rest, matrix[:NB, NB:])
    top, right = kernel_call(
        dense_rows_kernel, [((TOP, WIDE - NB), F32), ((ROWS, COLS), F32)]
    )(origin, gathered_rest, matrix, own, *blocks)
    left = [block[TOP:] for block in blocks]
    return factor(top, right, lower_inverse, upper_inverse, *left)


def per_device(matrix, pivots, lower_inverse, upper_inverse):
    send, plan, over = kernel_call(
        plan_kernel,
        [((256, COLS), F32), ((544, NB), jnp.int32), ((8, NB), jnp.int32)],
        [pltpu.VMEM((8, NB), jnp.int32), pltpu.VMEM((8, NB), jnp.int32)],
    )(pivots.reshape(PANELS, NB), matrix)
    return lax.cond(
        over[0, 0] <= 0,
        lambda: slotted(send, plan, matrix, lower_inverse, upper_inverse),
        lambda: dense(pivots, matrix, lower_inverse, upper_inverse),
    )


def solution(mesh):
    in_specs = (P("prow", "pcol"), P(), P(), P())
    out_specs = P("prow", "pcol")
    return jax.shard_map(
        per_device, mesh=mesh, in_specs=in_specs, out_specs=out_specs, check_vma=False
    )
```

```python
import jax
import jax.numpy as jnp
from jax import lax
from jax.experimental import pallas as pl
from jax.experimental.pallas import tpu as pltpu
from jax.sharding import PartitionSpec as P

NB = 128
PANELS = 4
TOP = NB * PANELS
PROW = 32
PCOL = 16
ROWS = 256
COLS = 768
REST = COLS - NB
WIDE = TOP + COLS
KERNEL_VMEM = 20 << 20
FACTOR_VMEM = 28 << 20
BF = jnp.bfloat16
F32 = jnp.float32
X_GROUPS = [[x * 8 + z for x in range(4)] for z in range(8)]
Z_GROUPS = [[x * 8 + z for z in range(8)] for x in range(4)]
VMEM = pl.BlockSpec(memory_space=pltpu.VMEM)
SMEM = pl.BlockSpec(memory_space=pltpu.SMEM)
HBM = pl.BlockSpec(memory_space=pltpu.HBM)


def mm(left, right):
    return lax.dot_general(left, right, (((1,), (0,)), ((), ())), preferred_element_type=F32)


def split2(value):
    high = value.astype(BF)
    low = (value - high.astype(F32)).astype(BF)
    return high, low


def select_rows(onehot, value):
    first = value.astype(BF)
    rest = value - first.astype(F32)
    second = rest.astype(BF)
    third = (rest - second.astype(F32)).astype(BF)
    return mm(onehot, first) + mm(onehot, second) + mm(onehot, third)


def dot3(left, right):
    lh, ll = split2(left)
    rh, rl = split2(right)
    return mm(jnp.concatenate([lh, ll, lh], axis=1), jnp.concatenate([rh, rh, rl], axis=0))


def chase(rows, piv_row_ref, panels):
    lanes = lax.broadcasted_iota(jnp.int32, (rows.shape[0], NB), 1).astype(F32)
    for m in panels:
        equal = rows == piv_row_ref[m : m + 1, :]
        hit = jnp.sum(jnp.where(equal, lanes + float(m * NB + 1), 0.0), axis=1, keepdims=True)
        hit = hit.astype(jnp.int32)
        rows = jnp.where(hit > 0, hit - 1, rows)
    return rows


def pick_kernel(place_ref, piv_row_ref, piv_col_ref, a_ref, first_ref, rest_ref, origin_ref):
    prow = place_ref[0]
    lane = lax.broadcasted_iota(jnp.int32, (NB, ROWS), 1)
    for k in range(PANELS):
        rows = chase(piv_col_ref[k * NB : (k + 1) * NB, :], piv_row_ref, range(k - 1, -1, -1))
        owner = (rows >> 7) & 31
        slot = ((rows >> 12) << 7) | (rows & 127)
        slot = jnp.where(owner == prow, slot, -1)
        onehot = jnp.where(lane == slot, 1.0, 0.0).astype(BF)
        first_ref[k * NB : (k + 1) * NB, :] = select_rows(onehot, a_ref[:, :NB])
        rest_ref[k * NB : (k + 1) * NB, :] = select_rows(onehot, a_ref[:, NB:])
    local = lax.broadcasted_iota(jnp.int32, (ROWS, 1), 0)
    rows = ((local >> 7) * PROW + prow) * NB + (local & 127)
    rows = chase(rows, piv_row_ref, range(PANELS - 1, -1, -1))
    origin_ref[...] = jnp.broadcast_to(rows, (ROWS, NB))


def place_of(origin):
    unit = (origin >> 2) & 31
    return (unit << 5) + 16 + ((origin >> 7) << 2) + (origin & 3)


def moved_rows(origin, gathered, kept):
    lane = lax.broadcasted_iota(jnp.int32, (ROWS, 1024), 1)
    onehot = jnp.where(lane == jnp.where(origin < TOP, place_of(origin), -1), 1.0, 0.0).astype(BF)
    return jnp.where(origin < TOP, select_rows(onehot, gathered), kept)


def column_kernel(origin_ref, gathered_ref, a_ref, out_ref):
    origin = origin_ref[:, :1]
    for unit in range(PROW):
        out_ref[unit * 16 : unit * 16 + 16, :] = gathered_ref[unit * 32 : unit * 32 + 16, :]
    out_ref[TOP:, :] = moved_rows(origin, gathered_ref[...], a_ref[:, :NB])


def exchange_first(picked, top):
    sent = jnp.concatenate([picked.reshape(PROW, 16, NB), top.reshape(PROW, 4, NB)], axis=1)
    got = lax.all_to_all(sent, "prow", 0, 0)
    chunk = jnp.concatenate([jnp.sum(got[:, :16], axis=0), got[:4, 16:].reshape(16, NB)], axis=0)
    sent = jnp.broadcast_to(chunk[None], (PROW, 32, NB))
    return lax.all_to_all(sent, "prow", 0, 0).reshape(PROW * 32, NB)


def exchange_rest(picked, top):
    sent = jnp.concatenate([picked.reshape(4, NB, REST), top.reshape(4, 32, REST)], axis=1)
    got = lax.all_to_all(sent, "prow", 0, 0, axis_index_groups=X_GROUPS)
    sent = jnp.concatenate(
        [jnp.sum(got[:, :NB], axis=0).reshape(8, 16, REST), got[0, NB:].reshape(8, 4, REST)], axis=1
    )
    got = lax.all_to_all(sent, "prow", 0, 0, axis_index_groups=Z_GROUPS)
    chunk = jnp.concatenate([jnp.sum(got[:, :16], axis=0), got[:4, 16:].reshape(16, REST)], axis=0)
    got = lax.all_to_all(
        jnp.broadcast_to(chunk[None], (8, 32, REST)), "prow", 0, 0, axis_index_groups=Z_GROUPS
    )
    got = got.reshape(256, REST)
    got = lax.all_to_all(
        jnp.broadcast_to(got[None], (4, 256, REST)), "prow", 0, 0, axis_index_groups=X_GROUPS
    )
    return got.reshape(PROW * 32, REST)


def spread_start(own):
    up = lax.ppermute(own, "pcol", [(q, q + 4) for q in range(4)])
    down = lax.ppermute(own, "pcol", [(q, q + 12) for q in range(4)])
    return up, down


def spread_columns(own, pcol):
    return spread_rest(own, *spread_start(own), pcol)


def spread_rest(own, up, down, pcol):
    near = jnp.where(pcol < 4, own, jnp.where(pcol < 8, up, down))
    half = near.shape[0] // 2
    left = lax.ppermute(near[:half], "pcol", [(q + 4, q + 8) for q in range(4)])
    right = lax.ppermute(near[half:], "pcol", [(q + 12, q + 8) for q in range(4)])
    far = (pcol >= 8) & (pcol < 12)
    near = jnp.where(far, jnp.concatenate([left, right], axis=0), near)
    return [near] + [lax.ppermute(near, "pcol", [(q, q ^ n) for q in range(PCOL)]) for n in (1, 2, 3)]


def lane_sum(mask, value):
    return jnp.sum(jnp.where(mask, value, 0.0), axis=1, keepdims=True)


def sub_sum(mask, value):
    return jnp.sum(jnp.where(mask, value, 0.0), axis=0, keepdims=True).astype(jnp.int32)


def iota(shape, axis):
    return lax.broadcasted_iota(jnp.int32, shape, axis)


def ranks(masks):
    count = len(masks)
    padded = -(-count // 8) * 8
    rows = [jnp.where(mask, 1.0, 0.0) for mask in masks]
    rows = rows + [jnp.zeros((1, NB), F32)] * (padded - count)
    before = jnp.where(iota((NB, NB), 0) < iota((NB, NB), 1), 1.0, 0.0).astype(BF)
    found = mm(jnp.concatenate(rows, axis=0).astype(BF), before)
    return [found[n : n + 1, :] for n in range(count)]


def slots(mask, rank, value, capacity):
    row = iota((capacity, NB), 0).astype(F32)
    return lane_sum(mask & (rank == row), value + 1.0).astype(jnp.int32) - 1


def onehot_of(column, width):
    return jnp.where(iota((column.shape[0], width), 1) == column, 1.0, 0.0).astype(BF)


def plan_kernel(pivots_ref, a_ref, send_ref, plan_ref, over_ref, source_ref, target_ref):
    prow = lax.axis_index("prow")
    x = prow >> 3
    z = prow & 7
    sub = iota((NB, NB), 0)
    lane = iota((NB, NB), 1)
    subf = sub.astype(F32)
    lane_row = iota((1, NB), 1)
    piv_row = [pivots_ref[m : m + 1, :] for m in range(PANELS)]
    piv_col = []
    for m in range(PANELS):
        piv_col.append(lane_sum(sub == lane, piv_row[m].astype(F32)).astype(jnp.int32))

    def met(m, rows):
        return sub_sum(piv_col[m] == rows, subf + float(m * NB + 1))

    source = []
    target = []
    for k in range(PANELS):
        rows = piv_row[k]
        for m in range(k - 1, -1, -1):
            hit = met(m, rows)
            rows = jnp.where(hit > 0, hit - 1, rows)
        source.append(rows)
        source_ref[k : k + 1, :] = rows
        rows = lane_row + k * NB
        for m in range(PANELS):
            if m == k:
                rows = jnp.where(rows == lane_row + k * NB, piv_row[k], rows)
                continue
            hit = met(m, rows)
            moved = jnp.where(hit > 0, hit - 1, rows)
            if m > k:
                look = sub_sum(sub + m * NB == rows, piv_col[m].astype(F32))
                moved = jnp.where(look > 0, look, moved)
            rows = moved
        target.append(rows)
        target_ref[k : k + 1, :] = rows

    def local_of(rows):
        return ((rows >> 12) << 7) | (rows & 127)

    def owner_of(rows):
        return (rows >> 7) & 31

    masks = [owner_of(source[k]) == prow for k in range(PANELS)]
    order = ranks(masks)
    pieces = [
        slots(masks[k], order[k], local_of(source[k]).astype(F32), 16) for k in range(PANELS)
    ]
    mine = target_ref[pl.ds(prow & 3, 1), :]
    leaves = (mine >= TOP) & (prow < PANELS)
    masks = [leaves & (((mine >> 10) & 3) == n) for n in range(4)]
    order = ranks(masks)
    lanef = lane_row.astype(F32)
    chosen = []
    for n in range(4):
        chosen.append(pieces[n])
        chosen.append(slots(masks[n], order[n], lanef, 48))
    send_ref[...] = select_rows(onehot_of(jnp.concatenate(chosen, axis=0), ROWS), a_ref[...])

    panel = source_ref[pl.ds(x, 1), :]
    panel_z = (panel >> 7) & 7
    panel_x = (panel >> 10) & 3
    here = panel_z == z
    masks = [here & (panel_x == n) for n in range(4)] + [here]
    order = ranks(masks)
    spot = jnp.zeros((1, NB), F32)
    for n in range(4):
        spot = spot + jnp.where(masks[n], order[n] + 64.0 * n, 0.0)
    wide = lambda column: jnp.broadcast_to(column, (column.shape[0], NB))
    plan_ref[0:32, :] = wide(slots(here, order[4], spot, 32))
    other = target_ref[pl.ds(z & 3, 1), :]
    along = (other >= TOP) & (z < PANELS) & (((other >> 10) & 3) == x)
    masks = [along & (((other >> 7) & 7) == n) for n in range(8)] + [along]
    order = ranks(masks)
    for n in range(8):
        plan_ref[32 + 16 * n : 48 + 16 * n, :] = wide(slots(masks[n], order[n], order[8], 16))
    zf = panel_z.astype(F32)
    zcol = lane_sum(sub == lane, zf)
    ahead = lane_sum((zf == zcol) & (lane < sub), 1.0)
    plan_ref[160:288, :] = wide((zcol * 32.0 + ahead).astype(jnp.int32))
    masks = [(target[k] >= TOP) & (owner_of(target[k]) == prow) for k in range(PANELS)]
    order = ranks(masks)
    row = iota((ROWS, NB), 0)
    total = jnp.zeros((ROWS, 1), F32)
    for k in range(PANELS):
        total = total + lane_sum(masks[k] & (local_of(target[k]) == row), order[k] + (16.0 * k + 1.0))
    plan_ref[288:544, :] = wide(total.astype(jnp.int32) - 1)
    unit = iota((PROW, NB), 0)
    over = jnp.zeros((PROW, 1), F32)
    for k in range(PANELS):
        leaves = target[k] >= TOP
        for mask, cap in (
            (owner_of(source[k]) == unit, 16.0),
            (((source[k] >> 7) & 7) == unit, 32.0),
            (leaves & (((target[k] >> 10) & 3) == unit), 48.0),
            (leaves & (owner_of(target[k]) == unit), 16.0),
        ):
            over = jnp.maximum(over, lane_sum(mask, 1.0) - cap)
    over = jnp.max(over, axis=0, keepdims=True)
    over_ref[...] = jnp.broadcast_to(over, (8, NB)).astype(jnp.int32)


def turn_kernel(plan_ref, got_ref, first_ref, rest_ref):
    got = got_ref[...].reshape(256, COLS)
    rows = select_rows(onehot_of(plan_ref[0:32, :1], 256), got)
    moved = plan_ref[32:160, :1]
    moved = jnp.where(moved < 0, -1, moved + 16)
    sent = select_rows(onehot_of(moved, 64), got[:64])
    for n in range(8):
        first_ref[n, 0:32, :] = rows[:, :NB]
        rest_ref[n, 0:32, :] = rows[:, NB:]
        first_ref[n, 32:48, :] = sent[n * 16 : n * 16 + 16, :NB]
        rest_ref[n, 32:48, :] = sent[n * 16 : n * 16 + 16, NB:]


def lead_kernel(plan_ref, got_ref, a_ref, lead_ref, rows_ref):
    got = jnp.concatenate([got_ref[n, 0:32, :] for n in range(8)], axis=0)
    lead_ref[...] = select_rows(onehot_of(plan_ref[160:288, :1], 256), got)
    moved = jnp.concatenate([got_ref[n, 32:48, :] for n in range(4)], axis=0)
    slot = plan_ref[288:544, :1]
    moved = select_rows(onehot_of(slot, 64), moved)
    rows_ref[...] = jnp.where(slot >= 0, moved, a_ref[:, :NB])


def panel_kernel(plan_ref, lead_ref, got_ref, *refs):
    blocks, send_ref, full_ref, sems = refs[:4], refs[4], refs[5], refs[6]
    panel = lax.axis_index("prow") >> 3
    got = jnp.concatenate([got_ref[n, 0:32, :] for n in range(8)], axis=0)
    full_ref[:, :NB] = lead_ref[...]
    full_ref[:, NB:COLS] = select_rows(onehot_of(plan_ref[160:288, :1], 256), got)

    def store(index, value):
        @pl.when(index != panel)
        def _():
            spot = COLS // NB + jnp.where(index < panel, index, index - 1)
            full_ref[:, lane_block(spot)] = value

    put_columns(blocks, slice(0, NB), store)
    copies = [
        pltpu.make_async_copy(full_ref, send_ref.at[n], sems.at[n]) for n in range(4)
    ]
    for copy in copies:
        copy.start()
    for copy in copies:
        copy.wait()


def put_columns(block_refs, rows, store):
    kind = lax.axis_index("pcol") & 3
    for n, ref in enumerate(block_refs):
        store(kind ^ n, ref[rows, :])


def lane_block(index):
    return pl.ds(pl.multiple_of(index * NB, NB), NB)


def own_rows_kernel(plan_ref, rows_ref, got_ref, a_ref, out_ref):
    slot = plan_ref[288:544, :1]
    moved = jnp.concatenate([got_ref[n, 32:48, :] for n in range(4)], axis=0)
    moved = select_rows(onehot_of(slot, 64), moved)
    out_ref[:, :NB] = rows_ref[...]
    out_ref[:, NB:] = jnp.where(slot >= 0, moved, a_ref[:, NB:])


def factor_kernel(
    top_ref, right_ref, lower_ref, upper_ref, left0_ref, left1_ref, left2_ref, left3_ref,
    result_ref, z_ref, y_ref, m_ref, u_ref, d_ref, out_ref, sems,
):
    prow = lax.axis_index("prow")
    pcol = lax.axis_index("pcol")
    fetches = []
    for n, ref in enumerate((left0_ref, left1_ref, left2_ref, left3_ref)):
        target = z_ref.at[TOP : TOP + ROWS, lane_block((pcol & 3) ^ n)]
        fetches.append(pltpu.make_async_copy(ref, target, sems.at[n]))
    fetches.append(pltpu.make_async_copy(right_ref, out_ref, sems.at[4]))
    for fetch in fetches:
        fetch.start()
    for k in range(PANELS):
        rows = slice(k * NB, k * NB + NB)
        for spot in range(PANELS - 1):
            block = spot if spot < k else spot + 1
            z_ref[rows, block * NB : block * NB + NB] = top_ref[
                rows, COLS + spot * NB : COLS + spot * NB + NB
            ]
    for k in range(PANELS):
        s = k * NB
        e = s + NB
        before = top_ref if k == 0 else y_ref
        lh, ll = split2(lower_ref[k])
        l3 = jnp.concatenate([lh, ll, lh], axis=1)
        if e < TOP:
            bh, bl = split2(z_ref[s:e, e:])
            corner = mm(l3, jnp.concatenate([bh, bh, bl], axis=0))
            z_ref[s:e, e:] = corner
            uh, ul = split2(corner)
            corner3 = jnp.concatenate([uh, uh, ul], axis=0)
        d_ref[s:e, :] = before[s:e, :NB]
        bh, bl = split2(before[s:e, :COLS])
        upper_rows = mm(l3, jnp.concatenate([bh, bh, bl], axis=0))
        y_ref[s:e, :] = upper_rows
        uh, ul = split2(upper_rows)
        u3 = jnp.concatenate([uh, uh, ul], axis=0)
        u_ref[3 * s : 3 * e, :] = u3
        if k == 0:
            for fetch in fetches[:4]:
                fetch.wait()
        multipliers = dot3(z_ref[e:, s:e], upper_ref[k])
        z_ref[e:, s:e] = multipliers
        mh, ml = split2(multipliers)
        m3 = jnp.concatenate([mh, ml, mh], axis=1)
        m_ref[:, 3 * s : 3 * e] = m3[TOP - e :]
        if e < TOP:
            z_ref[e:, e:] = z_ref[e:, e:] - mm(m3, corner3)
            y_ref[e:TOP, :] = before[e:TOP, :COLS] - mm(m3[: TOP - e], u3)
    fetches[4].wait()
    out_ref[...] = out_ref[...] - mm(m_ref[...], u_ref[...])
    panel_cols = lane_block(pcol & 3)
    top_rows = pl.ds(pl.multiple_of((prow & 3) * NB, NB), NB)

    @pl.when(pcol < PANELS)
    def _():
        out_ref[:, :NB] = z_ref[TOP:, panel_cols]

    @pl.when(prow < PANELS)
    def _():
        out_ref[:NB, :] = y_ref[top_rows, :]

    @pl.when((prow < PANELS) & (pcol < PANELS))
    def _():
        out_ref[:NB, :NB] = jnp.where(
            prow == pcol, d_ref[top_rows, :], z_ref[top_rows, panel_cols]
        )

    copy = pltpu.make_async_copy(out_ref, result_ref, sems.at[5])
    copy.start()
    copy.wait()


def kernel_call(body, shapes, scratch=(), out=VMEM):
    def call(*args):
        return pl.pallas_call(
            body,
            in_specs=[VMEM] * len(args),
            out_specs=[out] * len(shapes),
            out_shape=[jax.ShapeDtypeStruct(shape, kind) for shape, kind in shapes],
            scratch_shapes=list(scratch),
            compiler_params=pltpu.CompilerParams(vmem_limit_bytes=KERNEL_VMEM),
        )(*args)

    return call


def factor(top, right, lower_inverse, upper_inverse, *left):
    right, *left = [
        pltpu.with_memory_space_constraint(value, pltpu.HBM) for value in (right, *left)
    ]
    args = (top, right, lower_inverse, upper_inverse, *left)
    result = pl.pallas_call(
        factor_kernel,
        in_specs=[VMEM, HBM, VMEM, VMEM] + [HBM] * 4,
        out_specs=HBM,
        out_shape=jax.ShapeDtypeStruct((ROWS, COLS), F32),
        scratch_shapes=[
            pltpu.VMEM((TOP + ROWS, TOP), F32),
            pltpu.VMEM((TOP, COLS), F32),
            pltpu.VMEM((ROWS, 3 * TOP), BF),
            pltpu.VMEM((3 * TOP, COLS), BF),
            pltpu.VMEM((TOP, NB), F32),
            pltpu.VMEM((ROWS, COLS), F32),
            pltpu.SemaphoreType.DMA((6,)),
        ],
        compiler_params=pltpu.CompilerParams(vmem_limit_bytes=FACTOR_VMEM),
    )(*args)
    return pltpu.with_memory_space_constraint(result, pltpu.HBM)


def along(value, groups):
    return lax.all_to_all(value, "prow", 0, 0, axis_index_groups=groups)


def slotted(got, plan, matrix, lower_inverse, upper_inverse):
    pcol = lax.axis_index("pcol")
    first, rest = kernel_call(turn_kernel, [((8, 48, NB), F32), ((8, 48, REST), F32)])(plan, got)
    first = along(first, Z_GROUPS)
    rest = along(rest, Z_GROUPS)
    lead, rows = kernel_call(lead_kernel, [((NB, NB), F32), ((ROWS, NB), F32)])(
        plan, first, matrix
    )
    ends = spread_start(lead)
    late = spread_rest(lead, *ends, pcol)
    (send,) = kernel_call(
        panel_kernel,
        [((4, NB, WIDE - NB), F32)],
        [pltpu.VMEM((NB, WIDE - NB), F32), pltpu.SemaphoreType.DMA((4,))],
        HBM,
    )(plan, lead, rest, *late)
    top = along(send, X_GROUPS).reshape(TOP, WIDE - NB)
    ends = spread_start(rows)
    left = spread_rest(rows, *ends, pcol)
    (right,) = kernel_call(own_rows_kernel, [((ROWS, COLS), F32)])(plan, rows, rest, matrix)
    return factor(top, right, lower_inverse, upper_inverse, *left)


def dense_rows_kernel(
    origin_ref, gathered_ref, a_ref, own_ref, block0_ref, block1_ref, block2_ref, block3_ref,
    top_ref, right_ref,
):
    def store_corner(index, value):
        for k in range(PANELS):

            @pl.when(index != k)
            def _():
                spot = lane_block(COLS // NB + jnp.where(index < k, index, index - 1))
                top_ref[k * NB : k * NB + NB, spot] = value[k * NB : k * NB + NB]

    put_columns((block0_ref, block1_ref, block2_ref, block3_ref), slice(0, TOP), store_corner)
    top_ref[:, :NB] = own_ref[:TOP, :]
    right_ref[:, :NB] = own_ref[TOP:, :]
    for unit in range(PROW):
        top_ref[unit * 16 : unit * 16 + 16, NB:COLS] = gathered_ref[unit * 32 : unit * 32 + 16, :]
    origin = origin_ref[:, :1]

    @pl.loop(0, REST // NB)
    def _(c):
        right_ref[:, lane_block(c + 1)] = moved_rows(
            origin, gathered_ref[:, lane_block(c)], a_ref[:, lane_block(c + 1)]
        )


def dense(pivots, matrix, lower_inverse, upper_inverse):
    prow = lax.axis_index("prow")
    pcol = lax.axis_index("pcol")
    place = jnp.stack([prow, pcol]).astype(jnp.int32)
    picked_first, picked_rest, origin = pl.pallas_call(
        pick_kernel,
        in_specs=[SMEM, VMEM, VMEM, VMEM],
        out_specs=[VMEM] * 3,
        out_shape=[
            jax.ShapeDtypeStruct((TOP, NB), F32),
            jax.ShapeDtypeStruct((TOP, REST), F32),
            jax.ShapeDtypeStruct((ROWS, NB), jnp.int32),
        ],
    )(place, pivots.reshape(PANELS, NB), pivots.reshape(TOP, 1), matrix)
    gathered_first = exchange_first(picked_first, matrix[:NB, :NB])
    (own,) = kernel_call(column_kernel, [((TOP + ROWS, NB), F32)])(origin, gathered_first, matrix)
    blocks = spread_columns(own, pcol)
    gathered_rest = exchange_rest(picked_rest, matrix[:NB, NB:])
    top, right = kernel_call(
        dense_rows_kernel, [((TOP, WIDE - NB), F32), ((ROWS, COLS), F32)]
    )(origin, gathered_rest, matrix, own, *blocks)
    left = [block[TOP:] for block in blocks]
    return factor(top, right, lower_inverse, upper_inverse, *left)


def per_device(matrix, pivots, lower_inverse, upper_inverse):
    send, plan, over = kernel_call(
        plan_kernel,
        [((256, COLS), F32), ((544, NB), jnp.int32), ((8, NB), jnp.int32)],
        [pltpu.VMEM((8, NB), jnp.int32), pltpu.VMEM((8, NB), jnp.int32)],
    )(pivots.reshape(PANELS, NB), matrix)
    got = along(send.reshape(4, 64, COLS), X_GROUPS)
    return lax.cond(
        over[0, 0] <= 0,
        lambda: slotted(got, plan, matrix, lower_inverse, upper_inverse),
        lambda: dense(pivots, matrix, lower_inverse, upper_inverse),
    )


def solution(mesh):
    in_specs = (P("prow", "pcol"), P(), P(), P())
    out_specs = P("prow", "pcol")
    return jax.shard_map(
        per_device, mesh=mesh, in_specs=in_specs, out_specs=out_specs, check_vma=False
    )
```

```python
import jax
import jax.numpy as jnp
from jax import lax
from jax.experimental import pallas as pl
from jax.experimental.pallas import tpu as pltpu
from jax.sharding import PartitionSpec as P

NB = 128
PANELS = 4
TOP = NB * PANELS
PROW = 32
PCOL = 16
ROWS = 256
COLS = 768
REST = COLS - NB
WIDE = TOP + COLS
KERNEL_VMEM = 20 << 20
FACTOR_VMEM = 28 << 20
BF = jnp.bfloat16
F32 = jnp.float32
X_GROUPS = [[x * 8 + z for x in range(4)] for z in range(8)]
Z_GROUPS = [[x * 8 + z for z in range(8)] for x in range(4)]
VMEM = pl.BlockSpec(memory_space=pltpu.VMEM)
SMEM = pl.BlockSpec(memory_space=pltpu.SMEM)
HBM = pl.BlockSpec(memory_space=pltpu.HBM)


def mm(left, right):
    return lax.dot_general(left, right, (((1,), (0,)), ((), ())), preferred_element_type=F32)


def split2(value):
    high = value.astype(BF)
    low = (value - high.astype(F32)).astype(BF)
    return high, low


def select_rows(onehot, value):
    first = value.astype(BF)
    rest = value - first.astype(F32)
    second = rest.astype(BF)
    third = (rest - second.astype(F32)).astype(BF)
    return mm(onehot, first) + mm(onehot, second) + mm(onehot, third)


def dot3(left, right):
    lh, ll = split2(left)
    rh, rl = split2(right)
    return mm(jnp.concatenate([lh, ll, lh], axis=1), jnp.concatenate([rh, rh, rl], axis=0))


def chase(rows, piv_row_ref, panels):
    lanes = lax.broadcasted_iota(jnp.int32, (rows.shape[0], NB), 1).astype(F32)
    for m in panels:
        equal = rows == piv_row_ref[m : m + 1, :]
        hit = jnp.sum(jnp.where(equal, lanes + float(m * NB + 1), 0.0), axis=1, keepdims=True)
        hit = hit.astype(jnp.int32)
        rows = jnp.where(hit > 0, hit - 1, rows)
    return rows


def pick_kernel(place_ref, piv_row_ref, piv_col_ref, a_ref, first_ref, rest_ref, origin_ref):
    prow = place_ref[0]
    lane = lax.broadcasted_iota(jnp.int32, (NB, ROWS), 1)
    for k in range(PANELS):
        rows = chase(piv_col_ref[k * NB : (k + 1) * NB, :], piv_row_ref, range(k - 1, -1, -1))
        owner = (rows >> 7) & 31
        slot = ((rows >> 12) << 7) | (rows & 127)
        slot = jnp.where(owner == prow, slot, -1)
        onehot = jnp.where(lane == slot, 1.0, 0.0).astype(BF)
        first_ref[k * NB : (k + 1) * NB, :] = select_rows(onehot, a_ref[:, :NB])
        rest_ref[k * NB : (k + 1) * NB, :] = select_rows(onehot, a_ref[:, NB:])
    local = lax.broadcasted_iota(jnp.int32, (ROWS, 1), 0)
    rows = ((local >> 7) * PROW + prow) * NB + (local & 127)
    rows = chase(rows, piv_row_ref, range(PANELS - 1, -1, -1))
    origin_ref[...] = jnp.broadcast_to(rows, (ROWS, NB))


def place_of(origin):
    unit = (origin >> 2) & 31
    return (unit << 5) + 16 + ((origin >> 7) << 2) + (origin & 3)


def moved_rows(origin, gathered, kept):
    lane = lax.broadcasted_iota(jnp.int32, (ROWS, 1024), 1)
    onehot = jnp.where(lane == jnp.where(origin < TOP, place_of(origin), -1), 1.0, 0.0).astype(BF)
    return jnp.where(origin < TOP, select_rows(onehot, gathered), kept)


def column_kernel(origin_ref, gathered_ref, a_ref, out_ref):
    origin = origin_ref[:, :1]
    for unit in range(PROW):
        out_ref[unit * 16 : unit * 16 + 16, :] = gathered_ref[unit * 32 : unit * 32 + 16, :]
    out_ref[TOP:, :] = moved_rows(origin, gathered_ref[...], a_ref[:, :NB])


def exchange_first(picked, top):
    sent = jnp.concatenate([picked.reshape(PROW, 16, NB), top.reshape(PROW, 4, NB)], axis=1)
    got = lax.all_to_all(sent, "prow", 0, 0)
    chunk = jnp.concatenate([jnp.sum(got[:, :16], axis=0), got[:4, 16:].reshape(16, NB)], axis=0)
    sent = jnp.broadcast_to(chunk[None], (PROW, 32, NB))
    return lax.all_to_all(sent, "prow", 0, 0).reshape(PROW * 32, NB)


def exchange_rest(picked, top):
    sent = jnp.concatenate([picked.reshape(4, NB, REST), top.reshape(4, 32, REST)], axis=1)
    got = lax.all_to_all(sent, "prow", 0, 0, axis_index_groups=X_GROUPS)
    sent = jnp.concatenate(
        [jnp.sum(got[:, :NB], axis=0).reshape(8, 16, REST), got[0, NB:].reshape(8, 4, REST)], axis=1
    )
    got = lax.all_to_all(sent, "prow", 0, 0, axis_index_groups=Z_GROUPS)
    chunk = jnp.concatenate([jnp.sum(got[:, :16], axis=0), got[:4, 16:].reshape(16, REST)], axis=0)
    got = lax.all_to_all(
        jnp.broadcast_to(chunk[None], (8, 32, REST)), "prow", 0, 0, axis_index_groups=Z_GROUPS
    )
    got = got.reshape(256, REST)
    got = lax.all_to_all(
        jnp.broadcast_to(got[None], (4, 256, REST)), "prow", 0, 0, axis_index_groups=X_GROUPS
    )
    return got.reshape(PROW * 32, REST)


def spread_start(own):
    up = lax.ppermute(own, "pcol", [(q, q + 4) for q in range(4)])
    down = lax.ppermute(own, "pcol", [(q, q + 12) for q in range(4)])
    return up, down


def spread_columns(own, pcol):
    return spread_rest(own, *spread_start(own), pcol)


def spread_rest(own, up, down, pcol):
    near = jnp.where(pcol < 4, own, jnp.where(pcol < 8, up, down))
    half = near.shape[0] // 2
    left = lax.ppermute(near[:half], "pcol", [(q + 4, q + 8) for q in range(4)])
    right = lax.ppermute(near[half:], "pcol", [(q + 12, q + 8) for q in range(4)])
    far = (pcol >= 8) & (pcol < 12)
    near = jnp.where(far, jnp.concatenate([left, right], axis=0), near)
    return [near] + [lax.ppermute(near, "pcol", [(q, q ^ n) for q in range(PCOL)]) for n in (1, 2, 3)]


def lane_sum(mask, value):
    return jnp.sum(jnp.where(mask, value, 0.0), axis=1, keepdims=True)


def sub_sum(mask, value):
    return jnp.sum(jnp.where(mask, value, 0.0), axis=0, keepdims=True).astype(jnp.int32)


def iota(shape, axis):
    return lax.broadcasted_iota(jnp.int32, shape, axis)


def ranks(masks):
    count = len(masks)
    padded = -(-count // 8) * 8
    rows = [jnp.where(mask, 1.0, 0.0) for mask in masks]
    rows = rows + [jnp.zeros((1, NB), F32)] * (padded - count)
    before = jnp.where(iota((NB, NB), 0) < iota((NB, NB), 1), 1.0, 0.0).astype(BF)
    found = mm(jnp.concatenate(rows, axis=0).astype(BF), before)
    return [found[n : n + 1, :] for n in range(count)]


def slots(mask, rank, value, capacity):
    row = iota((capacity, NB), 0).astype(F32)
    return lane_sum(mask & (rank == row), value + 1.0).astype(jnp.int32) - 1


def onehot_of(column, width):
    return jnp.where(iota((column.shape[0], width), 1) == column, 1.0, 0.0).astype(BF)


def plan_kernel(
    pivots_ref, a_ref, first_ref, send_ref, plan_ref, over_ref, source_ref, target_ref
):
    prow = lax.axis_index("prow")
    x = prow >> 3
    z = prow & 7
    sub = iota((NB, NB), 0)
    lane = iota((NB, NB), 1)
    subf = sub.astype(F32)
    lane_row = iota((1, NB), 1)
    piv_row = [pivots_ref[m : m + 1, :] for m in range(PANELS)]
    piv_col = []
    for m in range(PANELS):
        piv_col.append(lane_sum(sub == lane, piv_row[m].astype(F32)).astype(jnp.int32))

    def met(m, rows):
        return sub_sum(piv_col[m] == rows, subf + float(m * NB + 1))

    source = []
    target = []
    for k in range(PANELS):
        rows = piv_row[k]
        for m in range(k - 1, -1, -1):
            hit = met(m, rows)
            rows = jnp.where(hit > 0, hit - 1, rows)
        source.append(rows)
        source_ref[k : k + 1, :] = rows
        rows = lane_row + k * NB
        for m in range(PANELS):
            if m == k:
                rows = jnp.where(rows == lane_row + k * NB, piv_row[k], rows)
                continue
            hit = met(m, rows)
            moved = jnp.where(hit > 0, hit - 1, rows)
            if m > k:
                look = sub_sum(sub + m * NB == rows, piv_col[m].astype(F32))
                moved = jnp.where(look > 0, look, moved)
            rows = moved
        target.append(rows)
        target_ref[k : k + 1, :] = rows

    def local_of(rows):
        return ((rows >> 12) << 7) | (rows & 127)

    def owner_of(rows):
        return (rows >> 7) & 31

    masks = [owner_of(source[k]) == prow for k in range(PANELS)]
    order = ranks(masks)
    pieces = [
        slots(masks[k], order[k], local_of(source[k]).astype(F32), 16) for k in range(PANELS)
    ]
    mine = target_ref[pl.ds(prow & 3, 1), :]
    leaves = (mine >= TOP) & (prow < PANELS)
    masks = [leaves & (((mine >> 10) & 3) == n) for n in range(4)]
    order = ranks(masks)
    lanef = lane_row.astype(F32)
    chosen = []
    for n in range(4):
        chosen.append(pieces[n])
        chosen.append(slots(masks[n], order[n], lanef, 48))
    picked = select_rows(onehot_of(jnp.concatenate(chosen, axis=0), ROWS), a_ref[...])
    send_ref[...] = picked
    for n in range(PROW):
        first_ref[n] = picked[64 * (n // 8) : 64 * (n // 8) + 16, :NB]

    panel = source_ref[pl.ds(x, 1), :]
    panel_z = (panel >> 7) & 7
    panel_x = (panel >> 10) & 3
    here = panel_z == z
    masks = [here & (panel_x == n) for n in range(4)] + [here]
    order = ranks(masks)
    spot = jnp.zeros((1, NB), F32)
    for n in range(4):
        spot = spot + jnp.where(masks[n], order[n] + 64.0 * n, 0.0)
    wide = lambda column: jnp.broadcast_to(column, (column.shape[0], NB))
    plan_ref[0:32, :] = wide(slots(here, order[4], spot, 32))
    other = target_ref[pl.ds(z & 3, 1), :]
    along = (other >= TOP) & (z < PANELS) & (((other >> 10) & 3) == x)
    masks = [along & (((other >> 7) & 7) == n) for n in range(8)] + [along]
    order = ranks(masks)
    for n in range(8):
        plan_ref[32 + 16 * n : 48 + 16 * n, :] = wide(slots(masks[n], order[n], order[8], 16))
    zf = panel_z.astype(F32)
    zcol = lane_sum(sub == lane, zf)
    ahead = lane_sum((zf == zcol) & (lane < sub), 1.0)
    plan_ref[160:288, :] = wide((zcol * 32.0 + ahead).astype(jnp.int32))
    own = owner_of(panel).astype(F32)
    owncol = lane_sum(sub == lane, own)
    ahead = lane_sum((own == owncol) & (lane < sub), 1.0)
    plan_ref[544:672, :] = wide((owncol * 16.0 + ahead).astype(jnp.int32))
    masks = [(target[k] >= TOP) & (owner_of(target[k]) == prow) for k in range(PANELS)]
    order = ranks(masks)
    row = iota((ROWS, NB), 0)
    total = jnp.zeros((ROWS, 1), F32)
    for k in range(PANELS):
        total = total + lane_sum(masks[k] & (local_of(target[k]) == row), order[k] + (16.0 * k + 1.0))
    plan_ref[288:544, :] = wide(total.astype(jnp.int32) - 1)
    unit = iota((PROW, NB), 0)
    over = jnp.zeros((PROW, 1), F32)
    for k in range(PANELS):
        leaves = target[k] >= TOP
        for mask, cap in (
            (owner_of(source[k]) == unit, 16.0),
            (((source[k] >> 7) & 7) == unit, 32.0),
            (leaves & (((target[k] >> 10) & 3) == unit), 48.0),
            (leaves & (owner_of(target[k]) == unit), 16.0),
        ):
            over = jnp.maximum(over, lane_sum(mask, 1.0) - cap)
    over = jnp.max(over, axis=0, keepdims=True)
    over_ref[...] = jnp.broadcast_to(over, (8, NB)).astype(jnp.int32)


def turn_kernel(plan_ref, got_ref, send_ref):
    got = got_ref[...].reshape(256, COLS)
    rows = select_rows(onehot_of(plan_ref[0:32, :1], 256), got[:, NB:])
    moved = plan_ref[32:160, :1]
    moved = jnp.where(moved < 0, -1, moved + 16)
    sent = select_rows(onehot_of(moved, 64), got[:64])
    for n in range(8):
        for c in range(REST // NB):
            send_ref[n, 32 * c : 32 * c + 32, :] = rows[:, c * NB : c * NB + NB]
        for c in range(COLS // NB):
            spot = 160 + 16 * c
            send_ref[n, spot : spot + 16, :] = sent[16 * n : 16 * n + 16, c * NB : c * NB + NB]


def pivot_part(got_ref, c):
    return jnp.concatenate([got_ref[n, 32 * c : 32 * c + 32, :] for n in range(8)], axis=0)


def moved_part(got_ref, c):
    spot = 160 + 16 * c
    return jnp.concatenate([got_ref[n, spot : spot + 16, :] for n in range(4)], axis=0)


def lead_kernel(plan_ref, got_ref, lead_ref):
    lead_ref[...] = select_rows(onehot_of(plan_ref[544:672, :1], PROW * 16), got_ref[...])


def panel_kernel(plan_ref, lead_ref, got_ref, *refs):
    blocks, send_ref, full_ref, sems = refs[:4], refs[4], refs[5], refs[6]
    panel = lax.axis_index("prow") >> 3
    got = jnp.concatenate([pivot_part(got_ref, c) for c in range(REST // NB)], axis=1)
    full_ref[:, :NB] = lead_ref[...]
    full_ref[:, NB:COLS] = select_rows(onehot_of(plan_ref[160:288, :1], 256), got)

    def store(index, value):
        @pl.when(index != panel)
        def _():
            spot = COLS // NB + jnp.where(index < panel, index, index - 1)
            full_ref[:, lane_block(spot)] = value

    put_columns(blocks, slice(0, NB), store)
    copies = [
        pltpu.make_async_copy(full_ref, send_ref.at[n], sems.at[n]) for n in range(4)
    ]
    for copy in copies:
        copy.start()
    for copy in copies:
        copy.wait()


def put_columns(block_refs, rows, store):
    kind = lax.axis_index("pcol") & 3
    for n, ref in enumerate(block_refs):
        store(kind ^ n, ref[rows, :])


def lane_block(index):
    return pl.ds(pl.multiple_of(index * NB, NB), NB)


def first_rows_kernel(plan_ref, got_ref, a_ref, out_ref):
    slot = plan_ref[288:544, :1]
    moved = select_rows(onehot_of(slot, 64), moved_part(got_ref, 0))
    out_ref[...] = jnp.where(slot >= 0, moved, a_ref[:, :NB])


def own_rows_kernel(plan_ref, rows_ref, got_ref, a_ref, out_ref):
    slot = plan_ref[288:544, :1]
    moved = jnp.concatenate([moved_part(got_ref, c) for c in range(1, COLS // NB)], axis=1)
    moved = select_rows(onehot_of(slot, 64), moved)
    out_ref[:, :NB] = rows_ref[...]
    out_ref[:, NB:] = jnp.where(slot >= 0, moved, a_ref[:, NB:])


def factor_kernel(
    top_ref, right_ref, lower_ref, upper_ref, left0_ref, left1_ref, left2_ref, left3_ref,
    result_ref, z_ref, y_ref, m_ref, u_ref, d_ref, out_ref, sems,
):
    prow = lax.axis_index("prow")
    pcol = lax.axis_index("pcol")
    fetches = []
    for n, ref in enumerate((left0_ref, left1_ref, left2_ref, left3_ref)):
        target = z_ref.at[TOP : TOP + ROWS, lane_block((pcol & 3) ^ n)]
        fetches.append(pltpu.make_async_copy(ref, target, sems.at[n]))
    fetches.append(pltpu.make_async_copy(right_ref, out_ref, sems.at[4]))
    for fetch in fetches:
        fetch.start()
    for k in range(PANELS):
        rows = slice(k * NB, k * NB + NB)
        for spot in range(PANELS - 1):
            block = spot if spot < k else spot + 1
            z_ref[rows, block * NB : block * NB + NB] = top_ref[
                rows, COLS + spot * NB : COLS + spot * NB + NB
            ]
    for k in range(PANELS):
        s = k * NB
        e = s + NB
        before = top_ref if k == 0 else y_ref
        lh, ll = split2(lower_ref[k])
        l3 = jnp.concatenate([lh, ll, lh], axis=1)
        if e < TOP:
            bh, bl = split2(z_ref[s:e, e:])
            corner = mm(l3, jnp.concatenate([bh, bh, bl], axis=0))
            z_ref[s:e, e:] = corner
            uh, ul = split2(corner)
            corner3 = jnp.concatenate([uh, uh, ul], axis=0)
        d_ref[s:e, :] = before[s:e, :NB]
        bh, bl = split2(before[s:e, :COLS])
        upper_rows = mm(l3, jnp.concatenate([bh, bh, bl], axis=0))
        y_ref[s:e, :] = upper_rows
        uh, ul = split2(upper_rows)
        u3 = jnp.concatenate([uh, uh, ul], axis=0)
        u_ref[3 * s : 3 * e, :] = u3
        if k == 0:
            for fetch in fetches[:4]:
                fetch.wait()
        multipliers = dot3(z_ref[e:, s:e], upper_ref[k])
        z_ref[e:, s:e] = multipliers
        mh, ml = split2(multipliers)
        m3 = jnp.concatenate([mh, ml, mh], axis=1)
        m_ref[:, 3 * s : 3 * e] = m3[TOP - e :]
        if e < TOP:
            z_ref[e:, e:] = z_ref[e:, e:] - mm(m3, corner3)
            y_ref[e:TOP, :] = before[e:TOP, :COLS] - mm(m3[: TOP - e], u3)
    fetches[4].wait()
    out_ref[...] = out_ref[...] - mm(m_ref[...], u_ref[...])
    panel_cols = lane_block(pcol & 3)
    top_rows = pl.ds(pl.multiple_of((prow & 3) * NB, NB), NB)

    @pl.when(pcol < PANELS)
    def _():
        out_ref[:, :NB] = z_ref[TOP:, panel_cols]

    @pl.when(prow < PANELS)
    def _():
        out_ref[:NB, :] = y_ref[top_rows, :]

    @pl.when((prow < PANELS) & (pcol < PANELS))
    def _():
        out_ref[:NB, :NB] = jnp.where(
            prow == pcol, d_ref[top_rows, :], z_ref[top_rows, panel_cols]
        )

    copy = pltpu.make_async_copy(out_ref, result_ref, sems.at[5])
    copy.start()
    copy.wait()


def kernel_call(body, shapes, scratch=(), out=VMEM):
    def call(*args):
        return pl.pallas_call(
            body,
            in_specs=[VMEM] * len(args),
            out_specs=[out] * len(shapes),
            out_shape=[jax.ShapeDtypeStruct(shape, kind) for shape, kind in shapes],
            scratch_shapes=list(scratch),
            compiler_params=pltpu.CompilerParams(vmem_limit_bytes=KERNEL_VMEM),
        )(*args)

    return call


def factor(top, right, lower_inverse, upper_inverse, *left):
    right, *left = [
        pltpu.with_memory_space_constraint(value, pltpu.HBM) for value in (right, *left)
    ]
    args = (top, right, lower_inverse, upper_inverse, *left)
    result = pl.pallas_call(
        factor_kernel,
        in_specs=[VMEM, HBM, VMEM, VMEM] + [HBM] * 4,
        out_specs=HBM,
        out_shape=jax.ShapeDtypeStruct((ROWS, COLS), F32),
        scratch_shapes=[
            pltpu.VMEM((TOP + ROWS, TOP), F32),
            pltpu.VMEM((TOP, COLS), F32),
            pltpu.VMEM((ROWS, 3 * TOP), BF),
            pltpu.VMEM((3 * TOP, COLS), BF),
            pltpu.VMEM((TOP, NB), F32),
            pltpu.VMEM((ROWS, COLS), F32),
            pltpu.SemaphoreType.DMA((6,)),
        ],
        compiler_params=pltpu.CompilerParams(vmem_limit_bytes=FACTOR_VMEM),
    )(*args)
    return pltpu.with_memory_space_constraint(result, pltpu.HBM)


def along(value, groups):
    return lax.all_to_all(value, "prow", 0, 0, axis_index_groups=groups)


def slotted(first, send, plan, matrix, lower_inverse, upper_inverse):
    pcol = lax.axis_index("pcol")
    (lead,) = kernel_call(lead_kernel, [((NB, NB), F32)])(plan, first)
    got = along(send.reshape(4, 64, COLS), X_GROUPS)
    ends = spread_start(lead)
    (rest,) = kernel_call(turn_kernel, [((8, 256, NB), F32)])(plan, got)
    rest = along(rest, Z_GROUPS)
    late = spread_rest(lead, *ends, pcol)
    (send,) = kernel_call(
        panel_kernel,
        [((4, NB, WIDE - NB), F32)],
        [pltpu.VMEM((NB, WIDE - NB), F32), pltpu.SemaphoreType.DMA((4,))],
        HBM,
    )(plan, lead, rest, *late)
    top = along(send, X_GROUPS).reshape(TOP, WIDE - NB)
    (rows,) = kernel_call(first_rows_kernel, [((ROWS, NB), F32)])(plan, rest, matrix)
    ends = spread_start(rows)
    left = spread_rest(rows, *ends, pcol)
    (right,) = kernel_call(own_rows_kernel, [((ROWS, COLS), F32)])(plan, rows, rest, matrix)
    return factor(top, right, lower_inverse, upper_inverse, *left)


def dense_rows_kernel(
    origin_ref, gathered_ref, a_ref, own_ref, block0_ref, block1_ref, block2_ref, block3_ref,
    top_ref, right_ref,
):
    def store_corner(index, value):
        for k in range(PANELS):

            @pl.when(index != k)
            def _():
                spot = lane_block(COLS // NB + jnp.where(index < k, index, index - 1))
                top_ref[k * NB : k * NB + NB, spot] = value[k * NB : k * NB + NB]

    put_columns((block0_ref, block1_ref, block2_ref, block3_ref), slice(0, TOP), store_corner)
    top_ref[:, :NB] = own_ref[:TOP, :]
    right_ref[:, :NB] = own_ref[TOP:, :]
    for unit in range(PROW):
        top_ref[unit * 16 : unit * 16 + 16, NB:COLS] = gathered_ref[unit * 32 : unit * 32 + 16, :]
    origin = origin_ref[:, :1]

    @pl.loop(0, REST // NB)
    def _(c):
        right_ref[:, lane_block(c + 1)] = moved_rows(
            origin, gathered_ref[:, lane_block(c)], a_ref[:, lane_block(c + 1)]
        )


def dense(pivots, matrix, lower_inverse, upper_inverse):
    prow = lax.axis_index("prow")
    pcol = lax.axis_index("pcol")
    place = jnp.stack([prow, pcol]).astype(jnp.int32)
    picked_first, picked_rest, origin = pl.pallas_call(
        pick_kernel,
        in_specs=[SMEM, VMEM, VMEM, VMEM],
        out_specs=[VMEM] * 3,
        out_shape=[
            jax.ShapeDtypeStruct((TOP, NB), F32),
            jax.ShapeDtypeStruct((TOP, REST), F32),
            jax.ShapeDtypeStruct((ROWS, NB), jnp.int32),
        ],
    )(place, pivots.reshape(PANELS, NB), pivots.reshape(TOP, 1), matrix)
    gathered_first = exchange_first(picked_first, matrix[:NB, :NB])
    (own,) = kernel_call(column_kernel, [((TOP + ROWS, NB), F32)])(origin, gathered_first, matrix)
    blocks = spread_columns(own, pcol)
    gathered_rest = exchange_rest(picked_rest, matrix[:NB, NB:])
    top, right = kernel_call(
        dense_rows_kernel, [((TOP, WIDE - NB), F32), ((ROWS, COLS), F32)]
    )(origin, gathered_rest, matrix, own, *blocks)
    left = [block[TOP:] for block in blocks]
    return factor(top, right, lower_inverse, upper_inverse, *left)


def per_device(matrix, pivots, lower_inverse, upper_inverse):
    first, send, plan, over = kernel_call(
        plan_kernel,
        [
            ((PROW, 16, NB), F32),
            ((256, COLS), F32),
            ((672, NB), jnp.int32),
            ((8, NB), jnp.int32),
        ],
        [pltpu.VMEM((8, NB), jnp.int32), pltpu.VMEM((8, NB), jnp.int32)],
    )(pivots.reshape(PANELS, NB), matrix)
    first = lax.all_to_all(first, "prow", 0, 0).reshape(PROW * 16, NB)
    return lax.cond(
        over[0, 0] <= 0,
        lambda: slotted(first, send, plan, matrix, lower_inverse, upper_inverse),
        lambda: dense(pivots, matrix, lower_inverse, upper_inverse),
    )


def solution(mesh):
    in_specs = (P("prow", "pcol"), P(), P(), P())
    out_specs = P("prow", "pcol")
    return jax.shard_map(
        per_device, mesh=mesh, in_specs=in_specs, out_specs=out_specs, check_vma=False
    )
```

```python
import jax
import jax.numpy as jnp
from jax import lax
from jax.experimental import pallas as pl
from jax.experimental.pallas import tpu as pltpu
from jax.sharding import PartitionSpec as P

NB = 128
PANELS = 4
TOP = NB * PANELS
PROW = 32
PCOL = 16
ROWS = 256
COLS = 768
REST = COLS - NB
WIDE = TOP + COLS
KERNEL_VMEM = 20 << 20
FACTOR_VMEM = 28 << 20
BF = jnp.bfloat16
F32 = jnp.float32
X_GROUPS = [[x * 8 + z for x in range(4)] for z in range(8)]
Z_GROUPS = [[x * 8 + z for z in range(8)] for x in range(4)]
VMEM = pl.BlockSpec(memory_space=pltpu.VMEM)
SMEM = pl.BlockSpec(memory_space=pltpu.SMEM)
HBM = pl.BlockSpec(memory_space=pltpu.HBM)


def mm(left, right):
    return lax.dot_general(left, right, (((1,), (0,)), ((), ())), preferred_element_type=F32)


def split2(value):
    high = value.astype(BF)
    low = (value - high.astype(F32)).astype(BF)
    return high, low


def select_rows(onehot, value):
    first = value.astype(BF)
    rest = value - first.astype(F32)
    second = rest.astype(BF)
    third = (rest - second.astype(F32)).astype(BF)
    return mm(onehot, first) + mm(onehot, second) + mm(onehot, third)


def dot3(left, right):
    lh, ll = split2(left)
    rh, rl = split2(right)
    return mm(jnp.concatenate([lh, ll, lh], axis=1), jnp.concatenate([rh, rh, rl], axis=0))


def chase(rows, piv_row_ref, panels):
    lanes = lax.broadcasted_iota(jnp.int32, (rows.shape[0], NB), 1).astype(F32)
    for m in panels:
        equal = rows == piv_row_ref[m : m + 1, :]
        hit = jnp.sum(jnp.where(equal, lanes + float(m * NB + 1), 0.0), axis=1, keepdims=True)
        hit = hit.astype(jnp.int32)
        rows = jnp.where(hit > 0, hit - 1, rows)
    return rows


def pick_kernel(place_ref, piv_row_ref, piv_col_ref, a_ref, first_ref, rest_ref, origin_ref):
    prow = place_ref[0]
    lane = lax.broadcasted_iota(jnp.int32, (NB, ROWS), 1)
    for k in range(PANELS):
        rows = chase(piv_col_ref[k * NB : (k + 1) * NB, :], piv_row_ref, range(k - 1, -1, -1))
        owner = (rows >> 7) & 31
        slot = ((rows >> 12) << 7) | (rows & 127)
        slot = jnp.where(owner == prow, slot, -1)
        onehot = jnp.where(lane == slot, 1.0, 0.0).astype(BF)
        first_ref[k * NB : (k + 1) * NB, :] = select_rows(onehot, a_ref[:, :NB])
        rest_ref[k * NB : (k + 1) * NB, :] = select_rows(onehot, a_ref[:, NB:])
    local = lax.broadcasted_iota(jnp.int32, (ROWS, 1), 0)
    rows = ((local >> 7) * PROW + prow) * NB + (local & 127)
    rows = chase(rows, piv_row_ref, range(PANELS - 1, -1, -1))
    origin_ref[...] = jnp.broadcast_to(rows, (ROWS, NB))


def place_of(origin):
    unit = (origin >> 2) & 31
    return (unit << 5) + 16 + ((origin >> 7) << 2) + (origin & 3)


def moved_rows(origin, gathered, kept):
    lane = lax.broadcasted_iota(jnp.int32, (ROWS, 1024), 1)
    onehot = jnp.where(lane == jnp.where(origin < TOP, place_of(origin), -1), 1.0, 0.0).astype(BF)
    return jnp.where(origin < TOP, select_rows(onehot, gathered), kept)


def column_kernel(origin_ref, gathered_ref, a_ref, out_ref):
    origin = origin_ref[:, :1]
    for unit in range(PROW):
        out_ref[unit * 16 : unit * 16 + 16, :] = gathered_ref[unit * 32 : unit * 32 + 16, :]
    out_ref[TOP:, :] = moved_rows(origin, gathered_ref[...], a_ref[:, :NB])


def exchange_first(picked, top):
    sent = jnp.concatenate([picked.reshape(PROW, 16, NB), top.reshape(PROW, 4, NB)], axis=1)
    got = lax.all_to_all(sent, "prow", 0, 0)
    chunk = jnp.concatenate([jnp.sum(got[:, :16], axis=0), got[:4, 16:].reshape(16, NB)], axis=0)
    sent = jnp.broadcast_to(chunk[None], (PROW, 32, NB))
    return lax.all_to_all(sent, "prow", 0, 0).reshape(PROW * 32, NB)


def exchange_rest(picked, top):
    sent = jnp.concatenate([picked.reshape(4, NB, REST), top.reshape(4, 32, REST)], axis=1)
    got = lax.all_to_all(sent, "prow", 0, 0, axis_index_groups=X_GROUPS)
    sent = jnp.concatenate(
        [jnp.sum(got[:, :NB], axis=0).reshape(8, 16, REST), got[0, NB:].reshape(8, 4, REST)], axis=1
    )
    got = lax.all_to_all(sent, "prow", 0, 0, axis_index_groups=Z_GROUPS)
    chunk = jnp.concatenate([jnp.sum(got[:, :16], axis=0), got[:4, 16:].reshape(16, REST)], axis=0)
    got = lax.all_to_all(
        jnp.broadcast_to(chunk[None], (8, 32, REST)), "prow", 0, 0, axis_index_groups=Z_GROUPS
    )
    got = got.reshape(256, REST)
    got = lax.all_to_all(
        jnp.broadcast_to(got[None], (4, 256, REST)), "prow", 0, 0, axis_index_groups=X_GROUPS
    )
    return got.reshape(PROW * 32, REST)


def spread_start(own):
    up = lax.ppermute(own, "pcol", [(q, q + 4) for q in range(4)])
    down = lax.ppermute(own, "pcol", [(q, q + 12) for q in range(4)])
    return up, down


def spread_columns(own, pcol):
    return spread_rest(own, *spread_start(own), pcol)


def spread_rest(own, up, down, pcol):
    near = jnp.where(pcol < 4, own, jnp.where(pcol < 8, up, down))
    half = near.shape[0] // 2
    left = lax.ppermute(near[:half], "pcol", [(q + 4, q + 8) for q in range(4)])
    right = lax.ppermute(near[half:], "pcol", [(q + 12, q + 8) for q in range(4)])
    far = (pcol >= 8) & (pcol < 12)
    near = jnp.where(far, jnp.concatenate([left, right], axis=0), near)
    return [near] + [lax.ppermute(near, "pcol", [(q, q ^ n) for q in range(PCOL)]) for n in (1, 2, 3)]


def lane_sum(mask, value):
    return jnp.sum(jnp.where(mask, value, 0.0), axis=1, keepdims=True)


def sub_sum(mask, value):
    return jnp.sum(jnp.where(mask, value, 0.0), axis=0, keepdims=True).astype(jnp.int32)


def iota(shape, axis):
    return lax.broadcasted_iota(jnp.int32, shape, axis)


def ranks(masks):
    count = len(masks)
    padded = -(-count // 8) * 8
    rows = [jnp.where(mask, 1.0, 0.0) for mask in masks]
    rows = rows + [jnp.zeros((1, NB), F32)] * (padded - count)
    before = jnp.where(iota((NB, NB), 0) < iota((NB, NB), 1), 1.0, 0.0).astype(BF)
    found = mm(jnp.concatenate(rows, axis=0).astype(BF), before)
    return [found[n : n + 1, :] for n in range(count)]


def slots(mask, rank, value, capacity):
    row = iota((capacity, NB), 0).astype(F32)
    return lane_sum(mask & (rank == row), value + 1.0).astype(jnp.int32) - 1


def onehot_of(column, width):
    return jnp.where(iota((column.shape[0], width), 1) == column, 1.0, 0.0).astype(BF)


def plan_kernel(
    pivots_ref, a_ref, send_ref, leave0_ref, leave1_ref, leave2_ref, leave3_ref, plan_ref, over_ref,
    source_ref, target_ref,
):
    prow = lax.axis_index("prow")
    x = prow >> 3
    z = prow & 7
    sub = iota((NB, NB), 0)
    lane = iota((NB, NB), 1)
    subf = sub.astype(F32)
    lane_row = iota((1, NB), 1)
    piv_row = [pivots_ref[m : m + 1, :] for m in range(PANELS)]
    piv_col = []
    for m in range(PANELS):
        piv_col.append(lane_sum(sub == lane, piv_row[m].astype(F32)).astype(jnp.int32))

    def met(m, rows):
        return sub_sum(piv_col[m] == rows, subf + float(m * NB + 1))

    source = []
    target = []
    for k in range(PANELS):
        rows = piv_row[k]
        for m in range(k - 1, -1, -1):
            hit = met(m, rows)
            rows = jnp.where(hit > 0, hit - 1, rows)
        source.append(rows)
        source_ref[k : k + 1, :] = rows
        rows = lane_row + k * NB
        for m in range(PANELS):
            if m == k:
                rows = jnp.where(rows == lane_row + k * NB, piv_row[k], rows)
                continue
            hit = met(m, rows)
            moved = jnp.where(hit > 0, hit - 1, rows)
            if m > k:
                look = sub_sum(sub + m * NB == rows, piv_col[m].astype(F32))
                moved = jnp.where(look > 0, look, moved)
            rows = moved
        target.append(rows)
        target_ref[k : k + 1, :] = rows

    def local_of(rows):
        return ((rows >> 12) << 7) | (rows & 127)

    def owner_of(rows):
        return (rows >> 7) & 31

    masks = [owner_of(source[k]) == prow for k in range(PANELS)]
    order = ranks(masks)
    chosen = [
        slots(masks[k], order[k], local_of(source[k]).astype(F32), 16) for k in range(PANELS)
    ]
    send_ref[...] = select_rows(onehot_of(jnp.concatenate(chosen, axis=0), ROWS), a_ref[...])
    mine = target_ref[pl.ds(prow & 3, 1), :]
    leaves = (mine >= TOP) & (prow < PANELS)
    masks = [leaves & (((mine >> 10) & 3) == n) for n in range(4)]
    order = ranks(masks)
    lanef = lane_row.astype(F32)
    chosen = [slots(masks[n], order[n], lanef, 48) for n in range(4)]
    leaving = select_rows(onehot_of(jnp.concatenate(chosen, axis=0), NB), a_ref[:NB, :])
    for n, ref in enumerate((leave0_ref, leave1_ref, leave2_ref, leave3_ref)):
        ref[...] = leaving[48 * n : 48 * n + 48]

    panel = source_ref[pl.ds(x, 1), :]
    panel_z = (panel >> 7) & 7
    panel_x = (panel >> 10) & 3
    here = panel_z == z
    masks = [here & (panel_x == n) for n in range(4)] + [here]
    order = ranks(masks)
    spot = jnp.zeros((1, NB), F32)
    for n in range(4):
        spot = spot + jnp.where(masks[n], order[n] + 16.0 * n, 0.0)
    wide = lambda column: jnp.broadcast_to(column, (column.shape[0], NB))
    plan_ref[0:32, :] = wide(slots(here, order[4], spot, 32))
    other = target_ref[pl.ds(z & 3, 1), :]
    along = (other >= TOP) & (z < PANELS) & (((other >> 10) & 3) == x)
    masks = [along & (((other >> 7) & 7) == n) for n in range(8)] + [along]
    order = ranks(masks)
    for n in range(8):
        plan_ref[32 + 16 * n : 48 + 16 * n, :] = wide(slots(masks[n], order[n], order[8], 16))
    zf = panel_z.astype(F32)
    zcol = lane_sum(sub == lane, zf)
    ahead = lane_sum((zf == zcol) & (lane < sub), 1.0)
    plan_ref[160:288, :] = wide((zcol * 32.0 + ahead).astype(jnp.int32))
    masks = [(target[k] >= TOP) & (owner_of(target[k]) == prow) for k in range(PANELS)]
    order = ranks(masks)
    row = iota((ROWS, NB), 0)
    total = jnp.zeros((ROWS, 1), F32)
    for k in range(PANELS):
        total = total + lane_sum(masks[k] & (local_of(target[k]) == row), order[k] + (16.0 * k + 1.0))
    plan_ref[288:544, :] = wide(total.astype(jnp.int32) - 1)
    unit = iota((PROW, NB), 0)
    over = jnp.zeros((PROW, 1), F32)
    for k in range(PANELS):
        leaves = target[k] >= TOP
        for mask, cap in (
            (owner_of(source[k]) == unit, 16.0),
            (((source[k] >> 7) & 7) == unit, 32.0),
            (leaves & (((target[k] >> 10) & 3) == unit), 48.0),
            (leaves & (owner_of(target[k]) == unit), 16.0),
        ):
            over = jnp.maximum(over, lane_sum(mask, 1.0) - cap)
    over = jnp.max(over, axis=0, keepdims=True)
    over_ref[...] = jnp.broadcast_to(over, (8, NB)).astype(jnp.int32)


def turn_kernel(plan_ref, got_ref, first_ref, rest_ref):
    rows = select_rows(onehot_of(plan_ref[0:32, :1], 64), got_ref[...])
    for n in range(8):
        first_ref[n] = rows[:, :NB]
    rest_ref[...] = rows[:, NB:]


def join_kernel(plan_ref, rows_ref, leave0_ref, leave1_ref, leave2_ref, leave3_ref, send_ref):
    held = leave1_ref[...] + leave2_ref[...] + leave3_ref[...]
    held = jnp.where(lax.axis_index("prow") < 8, leave0_ref[...], held)
    sent = select_rows(onehot_of(plan_ref[32:160, :1], 48), held)
    for n in range(8):
        for c in range(REST // NB):
            send_ref[n, 32 * c : 32 * c + 32, :] = rows_ref[:, c * NB : c * NB + NB]
        for c in range(COLS // NB):
            spot = 160 + 16 * c
            send_ref[n, spot : spot + 16, :] = sent[16 * n : 16 * n + 16, c * NB : c * NB + NB]


def lead_kernel(plan_ref, got_ref, lead_ref):
    lead_ref[...] = select_rows(onehot_of(plan_ref[160:288, :1], 256), got_ref[...])


def pivot_part(got_ref, c):
    return jnp.concatenate([got_ref[n, 32 * c : 32 * c + 32, :] for n in range(8)], axis=0)


def moved_part(got_ref, c):
    spot = 160 + 16 * c
    return jnp.concatenate([got_ref[n, spot : spot + 16, :] for n in range(4)], axis=0)


def panel_kernel(plan_ref, lead_ref, got_ref, *refs):
    blocks, send_ref, full_ref, sems = refs[:4], refs[4], refs[5], refs[6]
    panel = lax.axis_index("prow") >> 3
    got = jnp.concatenate([pivot_part(got_ref, c) for c in range(REST // NB)], axis=1)
    full_ref[:, :NB] = lead_ref[...]
    full_ref[:, NB:COLS] = select_rows(onehot_of(plan_ref[160:288, :1], 256), got)

    def store(index, value):
        @pl.when(index != panel)
        def _():
            spot = COLS // NB + jnp.where(index < panel, index, index - 1)
            full_ref[:, lane_block(spot)] = value

    put_columns(blocks, slice(0, NB), store)
    copies = [
        pltpu.make_async_copy(full_ref, send_ref.at[n], sems.at[n]) for n in range(4)
    ]
    for copy in copies:
        copy.start()
    for copy in copies:
        copy.wait()


def put_columns(block_refs, rows, store):
    kind = lax.axis_index("pcol") & 3
    for n, ref in enumerate(block_refs):
        store(kind ^ n, ref[rows, :])


def lane_block(index):
    return pl.ds(pl.multiple_of(index * NB, NB), NB)


def first_rows_kernel(plan_ref, got_ref, a_ref, out_ref):
    slot = plan_ref[288:544, :1]
    moved = select_rows(onehot_of(slot, 64), moved_part(got_ref, 0))
    out_ref[...] = jnp.where(slot >= 0, moved, a_ref[:, :NB])


def own_rows_kernel(plan_ref, rows_ref, got_ref, a_ref, out_ref):
    slot = plan_ref[288:544, :1]
    moved = jnp.concatenate([moved_part(got_ref, c) for c in range(1, COLS // NB)], axis=1)
    moved = select_rows(onehot_of(slot, 64), moved)
    out_ref[:, :NB] = rows_ref[...]
    out_ref[:, NB:] = jnp.where(slot >= 0, moved, a_ref[:, NB:])


def factor_kernel(
    top_ref, right_ref, lower_ref, upper_ref, left0_ref, left1_ref, left2_ref, left3_ref,
    result_ref, z_ref, y_ref, m_ref, u_ref, d_ref, out_ref, sems,
):
    prow = lax.axis_index("prow")
    pcol = lax.axis_index("pcol")
    fetches = []
    for n, ref in enumerate((left0_ref, left1_ref, left2_ref, left3_ref)):
        target = z_ref.at[TOP : TOP + ROWS, lane_block((pcol & 3) ^ n)]
        fetches.append(pltpu.make_async_copy(ref, target, sems.at[n]))
    fetches.append(pltpu.make_async_copy(right_ref, out_ref, sems.at[4]))
    for fetch in fetches:
        fetch.start()
    for k in range(PANELS):
        rows = slice(k * NB, k * NB + NB)
        for spot in range(PANELS - 1):
            block = spot if spot < k else spot + 1
            z_ref[rows, block * NB : block * NB + NB] = top_ref[
                rows, COLS + spot * NB : COLS + spot * NB + NB
            ]
    for k in range(PANELS):
        s = k * NB
        e = s + NB
        before = top_ref if k == 0 else y_ref
        lh, ll = split2(lower_ref[k])
        l3 = jnp.concatenate([lh, ll, lh], axis=1)
        if e < TOP:
            bh, bl = split2(z_ref[s:e, e:])
            corner = mm(l3, jnp.concatenate([bh, bh, bl], axis=0))
            z_ref[s:e, e:] = corner
            uh, ul = split2(corner)
            corner3 = jnp.concatenate([uh, uh, ul], axis=0)
        d_ref[s:e, :] = before[s:e, :NB]
        bh, bl = split2(before[s:e, :COLS])
        upper_rows = mm(l3, jnp.concatenate([bh, bh, bl], axis=0))
        y_ref[s:e, :] = upper_rows
        uh, ul = split2(upper_rows)
        u3 = jnp.concatenate([uh, uh, ul], axis=0)
        u_ref[3 * s : 3 * e, :] = u3
        if k == 0:
            for fetch in fetches[:4]:
                fetch.wait()
        multipliers = dot3(z_ref[e:, s:e], upper_ref[k])
        z_ref[e:, s:e] = multipliers
        mh, ml = split2(multipliers)
        m3 = jnp.concatenate([mh, ml, mh], axis=1)
        m_ref[:, 3 * s : 3 * e] = m3[TOP - e :]
        if e < TOP:
            z_ref[e:, e:] = z_ref[e:, e:] - mm(m3, corner3)
            y_ref[e:TOP, :] = before[e:TOP, :COLS] - mm(m3[: TOP - e], u3)
    fetches[4].wait()
    out_ref[...] = out_ref[...] - mm(m_ref[...], u_ref[...])
    panel_cols = lane_block(pcol & 3)
    top_rows = pl.ds(pl.multiple_of((prow & 3) * NB, NB), NB)

    @pl.when(pcol < PANELS)
    def _():
        out_ref[:, :NB] = z_ref[TOP:, panel_cols]

    @pl.when(prow < PANELS)
    def _():
        out_ref[:NB, :] = y_ref[top_rows, :]

    @pl.when((prow < PANELS) & (pcol < PANELS))
    def _():
        out_ref[:NB, :NB] = jnp.where(
            prow == pcol, d_ref[top_rows, :], z_ref[top_rows, panel_cols]
        )

    copy = pltpu.make_async_copy(out_ref, result_ref, sems.at[5])
    copy.start()
    copy.wait()


def kernel_call(body, shapes, scratch=(), out=VMEM):
    def call(*args):
        return pl.pallas_call(
            body,
            in_specs=[VMEM] * len(args),
            out_specs=[out] * len(shapes),
            out_shape=[jax.ShapeDtypeStruct(shape, kind) for shape, kind in shapes],
            scratch_shapes=list(scratch),
            compiler_params=pltpu.CompilerParams(vmem_limit_bytes=KERNEL_VMEM),
        )(*args)

    return call


def factor(top, right, lower_inverse, upper_inverse, *left):
    right, *left = [
        pltpu.with_memory_space_constraint(value, pltpu.HBM) for value in (right, *left)
    ]
    args = (top, right, lower_inverse, upper_inverse, *left)
    result = pl.pallas_call(
        factor_kernel,
        in_specs=[VMEM, HBM, VMEM, VMEM] + [HBM] * 4,
        out_specs=HBM,
        out_shape=jax.ShapeDtypeStruct((ROWS, COLS), F32),
        scratch_shapes=[
            pltpu.VMEM((TOP + ROWS, TOP), F32),
            pltpu.VMEM((TOP, COLS), F32),
            pltpu.VMEM((ROWS, 3 * TOP), BF),
            pltpu.VMEM((3 * TOP, COLS), BF),
            pltpu.VMEM((TOP, NB), F32),
            pltpu.VMEM((ROWS, COLS), F32),
            pltpu.SemaphoreType.DMA((6,)),
        ],
        compiler_params=pltpu.CompilerParams(vmem_limit_bytes=FACTOR_VMEM),
    )(*args)
    return pltpu.with_memory_space_constraint(result, pltpu.HBM)


def along(value, groups):
    return lax.all_to_all(value, "prow", 0, 0, axis_index_groups=groups)


def slotted(send, leaving, plan, matrix, lower_inverse, upper_inverse):
    pcol = lax.axis_index("pcol")
    got = along(send.reshape(4, 16, COLS), X_GROUPS)
    held = [leaving[0]]
    for n in range(1, 4):
        pairs = [(k, 8 * n + k) for k in range(PANELS)]
        held.append(lax.ppermute(leaving[n], "prow", pairs))
    first, rest = kernel_call(turn_kernel, [((8, 32, NB), F32), ((32, REST), F32)])(
        plan, got.reshape(64, COLS)
    )
    first = along(first, Z_GROUPS)
    (rest,) = kernel_call(join_kernel, [((8, 256, NB), F32)])(plan, rest, *held)
    rest = along(rest, Z_GROUPS)
    (lead,) = kernel_call(lead_kernel, [((NB, NB), F32)])(plan, first.reshape(256, NB))
    ends = spread_start(lead)
    late = spread_rest(lead, *ends, pcol)
    (send,) = kernel_call(
        panel_kernel,
        [((4, NB, WIDE - NB), F32)],
        [pltpu.VMEM((NB, WIDE - NB), F32), pltpu.SemaphoreType.DMA((4,))],
        HBM,
    )(plan, lead, rest, *late)
    top = along(send, X_GROUPS).reshape(TOP, WIDE - NB)
    (rows,) = kernel_call(first_rows_kernel, [((ROWS, NB), F32)])(plan, rest, matrix)
    ends = spread_start(rows)
    left = spread_rest(rows, *ends, pcol)
    (right,) = kernel_call(own_rows_kernel, [((ROWS, COLS), F32)])(plan, rows, rest, matrix)
    return factor(top, right, lower_inverse, upper_inverse, *left)


def dense_rows_kernel(
    origin_ref, gathered_ref, a_ref, own_ref, block0_ref, block1_ref, block2_ref, block3_ref,
    top_ref, right_ref,
):
    def store_corner(index, value):
        for k in range(PANELS):

            @pl.when(index != k)
            def _():
                spot = lane_block(COLS // NB + jnp.where(index < k, index, index - 1))
                top_ref[k * NB : k * NB + NB, spot] = value[k * NB : k * NB + NB]

    put_columns((block0_ref, block1_ref, block2_ref, block3_ref), slice(0, TOP), store_corner)
    top_ref[:, :NB] = own_ref[:TOP, :]
    right_ref[:, :NB] = own_ref[TOP:, :]
    for unit in range(PROW):
        top_ref[unit * 16 : unit * 16 + 16, NB:COLS] = gathered_ref[unit * 32 : unit * 32 + 16, :]
    origin = origin_ref[:, :1]

    @pl.loop(0, REST // NB)
    def _(c):
        right_ref[:, lane_block(c + 1)] = moved_rows(
            origin, gathered_ref[:, lane_block(c)], a_ref[:, lane_block(c + 1)]
        )


def dense(pivots, matrix, lower_inverse, upper_inverse):
    prow = lax.axis_index("prow")
    pcol = lax.axis_index("pcol")
    place = jnp.stack([prow, pcol]).astype(jnp.int32)
    picked_first, picked_rest, origin = pl.pallas_call(
        pick_kernel,
        in_specs=[SMEM, VMEM, VMEM, VMEM],
        out_specs=[VMEM] * 3,
        out_shape=[
            jax.ShapeDtypeStruct((TOP, NB), F32),
            jax.ShapeDtypeStruct((TOP, REST), F32),
            jax.ShapeDtypeStruct((ROWS, NB), jnp.int32),
        ],
    )(place, pivots.reshape(PANELS, NB), pivots.reshape(TOP, 1), matrix)
    gathered_first = exchange_first(picked_first, matrix[:NB, :NB])
    (own,) = kernel_call(column_kernel, [((TOP + ROWS, NB), F32)])(origin, gathered_first, matrix)
    blocks = spread_columns(own, pcol)
    gathered_rest = exchange_rest(picked_rest, matrix[:NB, NB:])
    top, right = kernel_call(
        dense_rows_kernel, [((TOP, WIDE - NB), F32), ((ROWS, COLS), F32)]
    )(origin, gathered_rest, matrix, own, *blocks)
    left = [block[TOP:] for block in blocks]
    return factor(top, right, lower_inverse, upper_inverse, *left)


def per_device(matrix, pivots, lower_inverse, upper_inverse):
    send, *leaving, plan, over = kernel_call(
        plan_kernel,
        [((64, COLS), F32)]
        + [((48, COLS), F32)] * 4
        + [((544, NB), jnp.int32), ((8, NB), jnp.int32)],
        [pltpu.VMEM((8, NB), jnp.int32), pltpu.VMEM((8, NB), jnp.int32)],
    )(pivots.reshape(PANELS, NB), matrix)
    return lax.cond(
        over[0, 0] <= 0,
        lambda: slotted(send, leaving, plan, matrix, lower_inverse, upper_inverse),
        lambda: dense(pivots, matrix, lower_inverse, upper_inverse),
    )


def solution(mesh):
    in_specs = (P("prow", "pcol"), P(), P(), P())
    out_specs = P("prow", "pcol")
    return jax.shard_map(
        per_device, mesh=mesh, in_specs=in_specs, out_specs=out_specs, check_vma=False
    )
```

```python
import jax
import jax.numpy as jnp
from jax import lax
from jax.experimental import pallas as pl
from jax.experimental.pallas import tpu as pltpu
from jax.sharding import PartitionSpec as P

NB = 128
PANELS = 4
TOP = NB * PANELS
PROW = 32
PCOL = 16
ROWS = 256
COLS = 768
REST = COLS - NB
WIDE = TOP + COLS
KERNEL_VMEM = 20 << 20
FACTOR_VMEM = 28 << 20
BF = jnp.bfloat16
F32 = jnp.float32
X_GROUPS = [[x * 8 + z for x in range(4)] for z in range(8)]
Z_GROUPS = [[x * 8 + z for z in range(8)] for x in range(4)]
VMEM = pl.BlockSpec(memory_space=pltpu.VMEM)
SMEM = pl.BlockSpec(memory_space=pltpu.SMEM)
HBM = pl.BlockSpec(memory_space=pltpu.HBM)


def mm(left, right):
    return lax.dot_general(left, right, (((1,), (0,)), ((), ())), preferred_element_type=F32)


def split2(value):
    high = value.astype(BF)
    low = (value - high.astype(F32)).astype(BF)
    return high, low


def select_rows(onehot, value):
    first = value.astype(BF)
    rest = value - first.astype(F32)
    second = rest.astype(BF)
    third = (rest - second.astype(F32)).astype(BF)
    return mm(onehot, first) + mm(onehot, second) + mm(onehot, third)


def dot3(left, right):
    lh, ll = split2(left)
    rh, rl = split2(right)
    return mm(jnp.concatenate([lh, ll, lh], axis=1), jnp.concatenate([rh, rh, rl], axis=0))


def chase(rows, piv_row_ref, panels):
    lanes = lax.broadcasted_iota(jnp.int32, (rows.shape[0], NB), 1).astype(F32)
    for m in panels:
        equal = rows == piv_row_ref[m : m + 1, :]
        hit = jnp.sum(jnp.where(equal, lanes + float(m * NB + 1), 0.0), axis=1, keepdims=True)
        hit = hit.astype(jnp.int32)
        rows = jnp.where(hit > 0, hit - 1, rows)
    return rows


def pick_kernel(place_ref, piv_row_ref, piv_col_ref, a_ref, first_ref, rest_ref, origin_ref):
    prow = place_ref[0]
    lane = lax.broadcasted_iota(jnp.int32, (NB, ROWS), 1)
    for k in range(PANELS):
        rows = chase(piv_col_ref[k * NB : (k + 1) * NB, :], piv_row_ref, range(k - 1, -1, -1))
        owner = (rows >> 7) & 31
        slot = ((rows >> 12) << 7) | (rows & 127)
        slot = jnp.where(owner == prow, slot, -1)
        onehot = jnp.where(lane == slot, 1.0, 0.0).astype(BF)
        first_ref[k * NB : (k + 1) * NB, :] = select_rows(onehot, a_ref[:, :NB])
        rest_ref[k * NB : (k + 1) * NB, :] = select_rows(onehot, a_ref[:, NB:])
    local = lax.broadcasted_iota(jnp.int32, (ROWS, 1), 0)
    rows = ((local >> 7) * PROW + prow) * NB + (local & 127)
    rows = chase(rows, piv_row_ref, range(PANELS - 1, -1, -1))
    origin_ref[...] = jnp.broadcast_to(rows, (ROWS, NB))


def place_of(origin):
    unit = (origin >> 2) & 31
    return (unit << 5) + 16 + ((origin >> 7) << 2) + (origin & 3)


def moved_rows(origin, gathered, kept):
    lane = lax.broadcasted_iota(jnp.int32, (ROWS, 1024), 1)
    onehot = jnp.where(lane == jnp.where(origin < TOP, place_of(origin), -1), 1.0, 0.0).astype(BF)
    return jnp.where(origin < TOP, select_rows(onehot, gathered), kept)


def column_kernel(origin_ref, gathered_ref, a_ref, out_ref):
    origin = origin_ref[:, :1]
    for unit in range(PROW):
        out_ref[unit * 16 : unit * 16 + 16, :] = gathered_ref[unit * 32 : unit * 32 + 16, :]
    out_ref[TOP:, :] = moved_rows(origin, gathered_ref[...], a_ref[:, :NB])


def exchange_first(picked, top):
    sent = jnp.concatenate([picked.reshape(PROW, 16, NB), top.reshape(PROW, 4, NB)], axis=1)
    got = lax.all_to_all(sent, "prow", 0, 0)
    chunk = jnp.concatenate([jnp.sum(got[:, :16], axis=0), got[:4, 16:].reshape(16, NB)], axis=0)
    sent = jnp.broadcast_to(chunk[None], (PROW, 32, NB))
    return lax.all_to_all(sent, "prow", 0, 0).reshape(PROW * 32, NB)


def exchange_rest(picked, top):
    sent = jnp.concatenate([picked.reshape(4, NB, REST), top.reshape(4, 32, REST)], axis=1)
    got = lax.all_to_all(sent, "prow", 0, 0, axis_index_groups=X_GROUPS)
    sent = jnp.concatenate(
        [jnp.sum(got[:, :NB], axis=0).reshape(8, 16, REST), got[0, NB:].reshape(8, 4, REST)], axis=1
    )
    got = lax.all_to_all(sent, "prow", 0, 0, axis_index_groups=Z_GROUPS)
    chunk = jnp.concatenate([jnp.sum(got[:, :16], axis=0), got[:4, 16:].reshape(16, REST)], axis=0)
    got = lax.all_to_all(
        jnp.broadcast_to(chunk[None], (8, 32, REST)), "prow", 0, 0, axis_index_groups=Z_GROUPS
    )
    got = got.reshape(256, REST)
    got = lax.all_to_all(
        jnp.broadcast_to(got[None], (4, 256, REST)), "prow", 0, 0, axis_index_groups=X_GROUPS
    )
    return got.reshape(PROW * 32, REST)


def spread_start(own):
    up = lax.ppermute(own, "pcol", [(q, q + 4) for q in range(4)])
    down = lax.ppermute(own, "pcol", [(q, q + 12) for q in range(4)])
    return up, down


def spread_columns(own, pcol):
    return spread_rest(own, *spread_start(own), pcol)


def spread_rest(own, up, down, pcol):
    near = jnp.where(pcol < 4, own, jnp.where(pcol < 8, up, down))
    half = near.shape[0] // 2
    left = lax.ppermute(near[:half], "pcol", [(q + 4, q + 8) for q in range(4)])
    right = lax.ppermute(near[half:], "pcol", [(q + 12, q + 8) for q in range(4)])
    far = (pcol >= 8) & (pcol < 12)
    near = jnp.where(far, jnp.concatenate([left, right], axis=0), near)
    return [near] + [lax.ppermute(near, "pcol", [(q, q ^ n) for q in range(PCOL)]) for n in (1, 2, 3)]


def lane_sum(mask, value):
    return jnp.sum(jnp.where(mask, value, 0.0), axis=1, keepdims=True)


def sub_sum(mask, value):
    return jnp.sum(jnp.where(mask, value, 0.0), axis=0, keepdims=True).astype(jnp.int32)


def iota(shape, axis):
    return lax.broadcasted_iota(jnp.int32, shape, axis)


def ranks(masks):
    count = len(masks)
    padded = -(-count // 8) * 8
    rows = [jnp.where(mask, 1.0, 0.0) for mask in masks]
    rows = rows + [jnp.zeros((1, NB), F32)] * (padded - count)
    before = jnp.where(iota((NB, NB), 0) < iota((NB, NB), 1), 1.0, 0.0).astype(BF)
    found = mm(jnp.concatenate(rows, axis=0).astype(BF), before)
    return [found[n : n + 1, :] for n in range(count)]


def slots(mask, rank, value, capacity):
    row = iota((capacity, NB), 0).astype(F32)
    return lane_sum(mask & (rank == row), value + 1.0).astype(jnp.int32) - 1


def onehot_of(column, width):
    return jnp.where(iota((column.shape[0], width), 1) == column, 1.0, 0.0).astype(BF)


def plan_kernel(
    pivots_ref, a_ref, send_ref, leave0_ref, leave1_ref, leave2_ref, leave3_ref, block_ref, plan_ref,
    over_ref, source_ref, target_ref,
):
    prow = lax.axis_index("prow")
    x = prow >> 3
    z = prow & 7
    sub = iota((NB, NB), 0)
    lane = iota((NB, NB), 1)
    subf = sub.astype(F32)
    lane_row = iota((1, NB), 1)
    piv_row = [pivots_ref[m : m + 1, :] for m in range(PANELS)]
    piv_col = []
    for m in range(PANELS):
        piv_col.append(lane_sum(sub == lane, piv_row[m].astype(F32)).astype(jnp.int32))

    def met(m, rows):
        return sub_sum(piv_col[m] == rows, subf + float(m * NB + 1))

    source = []
    target = []
    for k in range(PANELS):
        rows = piv_row[k]
        for m in range(k - 1, -1, -1):
            hit = met(m, rows)
            rows = jnp.where(hit > 0, hit - 1, rows)
        source.append(rows)
        source_ref[k : k + 1, :] = rows
        rows = lane_row + k * NB
        for m in range(PANELS):
            if m == k:
                rows = jnp.where(rows == lane_row + k * NB, piv_row[k], rows)
                continue
            hit = met(m, rows)
            moved = jnp.where(hit > 0, hit - 1, rows)
            if m > k:
                look = sub_sum(sub + m * NB == rows, piv_col[m].astype(F32))
                moved = jnp.where(look > 0, look, moved)
            rows = moved
        target.append(rows)
        target_ref[k : k + 1, :] = rows

    def local_of(rows):
        return ((rows >> 12) << 7) | (rows & 127)

    def owner_of(rows):
        return (rows >> 7) & 31

    masks = [owner_of(source[k]) == prow for k in range(PANELS)]
    order = ranks(masks)
    chosen = [
        slots(masks[k], order[k], local_of(source[k]).astype(F32), 16) for k in range(PANELS)
    ]
    send_ref[...] = select_rows(onehot_of(jnp.concatenate(chosen, axis=0), ROWS), a_ref[...])
    mine = target_ref[pl.ds(prow & 3, 1), :]
    leaves = (mine >= TOP) & (prow < PANELS)
    masks = [leaves & (((mine >> 10) & 3) == n) for n in range(4)]
    order = ranks(masks)
    lanef = lane_row.astype(F32)
    chosen = [slots(masks[n], order[n], lanef, 48) for n in range(4)]
    leaving = select_rows(onehot_of(jnp.concatenate(chosen, axis=0), NB), a_ref[:NB, :])
    block_ref[...] = a_ref[:, :NB]
    for n, ref in enumerate((leave0_ref, leave1_ref, leave2_ref, leave3_ref)):
        ref[...] = leaving[48 * n : 48 * n + 48]

    panel = source_ref[pl.ds(x, 1), :]
    panel_z = (panel >> 7) & 7
    panel_x = (panel >> 10) & 3
    here = panel_z == z
    masks = [here & (panel_x == n) for n in range(4)] + [here]
    order = ranks(masks)
    spot = jnp.zeros((1, NB), F32)
    for n in range(4):
        spot = spot + jnp.where(masks[n], order[n] + 16.0 * n, 0.0)
    wide = lambda column: jnp.broadcast_to(column, (column.shape[0], NB))
    plan_ref[0:32, :] = wide(slots(here, order[4], spot, 32))
    other = target_ref[pl.ds(z & 3, 1), :]
    along = (other >= TOP) & (z < PANELS) & (((other >> 10) & 3) == x)
    masks = [along & (((other >> 7) & 7) == n) for n in range(8)] + [along]
    order = ranks(masks)
    for n in range(8):
        plan_ref[32 + 16 * n : 48 + 16 * n, :] = wide(slots(masks[n], order[n], order[8], 16))
    zf = panel_z.astype(F32)
    zcol = lane_sum(sub == lane, zf)
    ahead = lane_sum((zf == zcol) & (lane < sub), 1.0)
    plan_ref[160:288, :] = wide((zcol * 32.0 + ahead).astype(jnp.int32))
    masks = [(target[k] >= TOP) & (owner_of(target[k]) == prow) for k in range(PANELS)]
    order = ranks(masks)
    row = iota((ROWS, NB), 0)
    total = jnp.zeros((ROWS, 1), F32)
    for k in range(PANELS):
        total = total + lane_sum(masks[k] & (local_of(target[k]) == row), order[k] + (16.0 * k + 1.0))
    plan_ref[288:544, :] = wide(total.astype(jnp.int32) - 1)
    unit = iota((PROW, NB), 0)
    over = jnp.zeros((PROW, 1), F32)
    for k in range(PANELS):
        leaves = target[k] >= TOP
        for mask, cap in (
            (owner_of(source[k]) == unit, 16.0),
            (((source[k] >> 7) & 7) == unit, 32.0),
            (leaves & (((target[k] >> 10) & 3) == unit), 48.0),
            (leaves & (owner_of(target[k]) == unit), 16.0),
        ):
            over = jnp.maximum(over, lane_sum(mask, 1.0) - cap)
    over = jnp.max(over, axis=0, keepdims=True)
    over_ref[...] = jnp.broadcast_to(over, (8, NB)).astype(jnp.int32)


def turn_kernel(plan_ref, got_ref, first_ref, rest_ref):
    rows = select_rows(onehot_of(plan_ref[0:32, :1], 64), got_ref[...])
    for n in range(8):
        first_ref[n] = rows[:, :NB]
    rest_ref[...] = rows[:, NB:]


def join_kernel(plan_ref, rows_ref, leave0_ref, leave1_ref, leave2_ref, leave3_ref, send_ref):
    held = leave1_ref[...] + leave2_ref[...] + leave3_ref[...]
    held = jnp.where(lax.axis_index("prow") < 8, leave0_ref[...], held)
    sent = select_rows(onehot_of(plan_ref[32:160, :1], 48), held)
    for n in range(8):
        for c in range(REST // NB):
            send_ref[n, 32 * c : 32 * c + 32, :] = rows_ref[:, c * NB : c * NB + NB]
        for c in range(COLS // NB):
            spot = 160 + 16 * c
            send_ref[n, spot : spot + 16, :] = sent[16 * n : 16 * n + 16, c * NB : c * NB + NB]


def lead_kernel(plan_ref, got_ref, lead_ref):
    lead_ref[...] = select_rows(onehot_of(plan_ref[160:288, :1], 256), got_ref[...])


def pivot_part(got_ref, c):
    return jnp.concatenate([got_ref[n, 32 * c : 32 * c + 32, :] for n in range(8)], axis=0)


def moved_part(got_ref, c):
    spot = 160 + 16 * c
    return jnp.concatenate([got_ref[n, spot : spot + 16, :] for n in range(4)], axis=0)


def panel_kernel(plan_ref, lead_ref, got_ref, block_ref, *refs):
    blocks, (send_ref, rows_ref, full_ref, sems) = refs[:4], refs[4:]
    panel = lax.axis_index("prow") >> 3
    got = jnp.concatenate([pivot_part(got_ref, c) for c in range(REST // NB)], axis=1)
    full_ref[:, :NB] = lead_ref[...]
    full_ref[:, NB:COLS] = select_rows(onehot_of(plan_ref[160:288, :1], 256), got)

    def store(index, value):
        @pl.when(index != panel)
        def _():
            spot = COLS // NB + jnp.where(index < panel, index, index - 1)
            full_ref[:, lane_block(spot)] = value

    put_columns(blocks, slice(0, NB), store)
    copies = [
        pltpu.make_async_copy(full_ref, send_ref.at[n], sems.at[n]) for n in range(4)
    ]
    for copy in copies:
        copy.start()
    slot = plan_ref[288:544, :1]
    moved = select_rows(onehot_of(slot, 64), moved_part(got_ref, 0))
    rows_ref[...] = jnp.where(slot >= 0, moved, block_ref[...])
    for copy in copies:
        copy.wait()


def put_columns(block_refs, rows, store):
    kind = lax.axis_index("pcol") & 3
    for n, ref in enumerate(block_refs):
        store(kind ^ n, ref[rows, :])


def lane_block(index):
    return pl.ds(pl.multiple_of(index * NB, NB), NB)


def own_rows_kernel(plan_ref, rows_ref, got_ref, a_ref, out_ref):
    slot = plan_ref[288:544, :1]
    moved = jnp.concatenate([moved_part(got_ref, c) for c in range(1, COLS // NB)], axis=1)
    moved = select_rows(onehot_of(slot, 64), moved)
    out_ref[:, :NB] = rows_ref[...]
    out_ref[:, NB:] = jnp.where(slot >= 0, moved, a_ref[:, NB:])


def factor_kernel(
    top_ref, right_ref, lower_ref, upper_ref, left0_ref, left1_ref, left2_ref, left3_ref,
    result_ref, z_ref, y_ref, m_ref, u_ref, d_ref, out_ref, sems,
):
    prow = lax.axis_index("prow")
    pcol = lax.axis_index("pcol")
    fetches = []
    for n, ref in enumerate((left0_ref, left1_ref, left2_ref, left3_ref)):
        target = z_ref.at[TOP : TOP + ROWS, lane_block((pcol & 3) ^ n)]
        fetches.append(pltpu.make_async_copy(ref, target, sems.at[n]))
    fetches.append(pltpu.make_async_copy(right_ref, out_ref, sems.at[4]))
    for fetch in fetches:
        fetch.start()
    for k in range(PANELS):
        rows = slice(k * NB, k * NB + NB)
        for spot in range(PANELS - 1):
            block = spot if spot < k else spot + 1
            z_ref[rows, block * NB : block * NB + NB] = top_ref[
                rows, COLS + spot * NB : COLS + spot * NB + NB
            ]
    for k in range(PANELS):
        s = k * NB
        e = s + NB
        before = top_ref if k == 0 else y_ref
        lh, ll = split2(lower_ref[k])
        l3 = jnp.concatenate([lh, ll, lh], axis=1)
        if e < TOP:
            bh, bl = split2(z_ref[s:e, e:])
            corner = mm(l3, jnp.concatenate([bh, bh, bl], axis=0))
            z_ref[s:e, e:] = corner
            uh, ul = split2(corner)
            corner3 = jnp.concatenate([uh, uh, ul], axis=0)
        d_ref[s:e, :] = before[s:e, :NB]
        bh, bl = split2(before[s:e, :COLS])
        upper_rows = mm(l3, jnp.concatenate([bh, bh, bl], axis=0))
        y_ref[s:e, :] = upper_rows
        uh, ul = split2(upper_rows)
        u3 = jnp.concatenate([uh, uh, ul], axis=0)
        u_ref[3 * s : 3 * e, :] = u3
        if k == 0:
            for fetch in fetches[:4]:
                fetch.wait()
        multipliers = dot3(z_ref[e:, s:e], upper_ref[k])
        z_ref[e:, s:e] = multipliers
        mh, ml = split2(multipliers)
        m3 = jnp.concatenate([mh, ml, mh], axis=1)
        m_ref[:, 3 * s : 3 * e] = m3[TOP - e :]
        if e < TOP:
            z_ref[e:, e:] = z_ref[e:, e:] - mm(m3, corner3)
            y_ref[e:TOP, :] = before[e:TOP, :COLS] - mm(m3[: TOP - e], u3)
    fetches[4].wait()
    out_ref[...] = out_ref[...] - mm(m_ref[...], u_ref[...])
    panel_cols = lane_block(pcol & 3)
    top_rows = pl.ds(pl.multiple_of((prow & 3) * NB, NB), NB)

    @pl.when(pcol < PANELS)
    def _():
        out_ref[:, :NB] = z_ref[TOP:, panel_cols]

    @pl.when(prow < PANELS)
    def _():
        out_ref[:NB, :] = y_ref[top_rows, :]

    @pl.when((prow < PANELS) & (pcol < PANELS))
    def _():
        out_ref[:NB, :NB] = jnp.where(
            prow == pcol, d_ref[top_rows, :], z_ref[top_rows, panel_cols]
        )

    copy = pltpu.make_async_copy(out_ref, result_ref, sems.at[5])
    copy.start()
    copy.wait()


def kernel_call(body, shapes, scratch=(), out=None):
    def call(*args):
        return pl.pallas_call(
            body,
            in_specs=[VMEM] * len(args),
            out_specs=out or [VMEM] * len(shapes),
            out_shape=[jax.ShapeDtypeStruct(shape, kind) for shape, kind in shapes],
            scratch_shapes=list(scratch),
            compiler_params=pltpu.CompilerParams(vmem_limit_bytes=KERNEL_VMEM),
        )(*args)

    return call


def factor(top, right, lower_inverse, upper_inverse, *left):
    right, *left = [
        pltpu.with_memory_space_constraint(value, pltpu.HBM) for value in (right, *left)
    ]
    args = (top, right, lower_inverse, upper_inverse, *left)
    result = pl.pallas_call(
        factor_kernel,
        in_specs=[VMEM, HBM, VMEM, VMEM] + [HBM] * 4,
        out_specs=HBM,
        out_shape=jax.ShapeDtypeStruct((ROWS, COLS), F32),
        scratch_shapes=[
            pltpu.VMEM((TOP + ROWS, TOP), F32),
            pltpu.VMEM((TOP, COLS), F32),
            pltpu.VMEM((ROWS, 3 * TOP), BF),
            pltpu.VMEM((3 * TOP, COLS), BF),
            pltpu.VMEM((TOP, NB), F32),
            pltpu.VMEM((ROWS, COLS), F32),
            pltpu.SemaphoreType.DMA((6,)),
        ],
        compiler_params=pltpu.CompilerParams(vmem_limit_bytes=FACTOR_VMEM),
    )(*args)
    return pltpu.with_memory_space_constraint(result, pltpu.HBM)


def along(value, groups):
    return lax.all_to_all(value, "prow", 0, 0, axis_index_groups=groups)


def slotted(send, leaving, block, plan, matrix, lower_inverse, upper_inverse):
    pcol = lax.axis_index("pcol")
    got = along(send.reshape(4, 16, COLS), X_GROUPS)
    held = [leaving[0]]
    for n in range(1, 4):
        pairs = [(k, 8 * n + k) for k in range(PANELS)]
        held.append(lax.ppermute(leaving[n], "prow", pairs))
    first, rest = kernel_call(turn_kernel, [((8, 32, NB), F32), ((32, REST), F32)])(
        plan, got.reshape(64, COLS)
    )
    first = along(first, Z_GROUPS)
    (rest,) = kernel_call(join_kernel, [((8, 256, NB), F32)])(plan, rest, *held)
    rest = along(rest, Z_GROUPS)
    (lead,) = kernel_call(lead_kernel, [((NB, NB), F32)])(plan, first.reshape(256, NB))
    ends = spread_start(lead)
    late = spread_rest(lead, *ends, pcol)
    send, rows = kernel_call(
        panel_kernel,
        [((4, NB, WIDE - NB), F32), ((ROWS, NB), F32)],
        [pltpu.VMEM((NB, WIDE - NB), F32), pltpu.SemaphoreType.DMA((4,))],
        [HBM, VMEM],
    )(plan, lead, rest, block, *late)
    top = along(send, X_GROUPS).reshape(TOP, WIDE - NB)
    ends = spread_start(rows)
    left = spread_rest(rows, *ends, pcol)
    (right,) = kernel_call(own_rows_kernel, [((ROWS, COLS), F32)])(plan, rows, rest, matrix)
    return factor(top, right, lower_inverse, upper_inverse, *left)


def dense_rows_kernel(
    origin_ref, gathered_ref, a_ref, own_ref, block0_ref, block1_ref, block2_ref, block3_ref,
    top_ref, right_ref,
):
    def store_corner(index, value):
        for k in range(PANELS):

            @pl.when(index != k)
            def _():
                spot = lane_block(COLS // NB + jnp.where(index < k, index, index - 1))
                top_ref[k * NB : k * NB + NB, spot] = value[k * NB : k * NB + NB]

    put_columns((block0_ref, block1_ref, block2_ref, block3_ref), slice(0, TOP), store_corner)
    top_ref[:, :NB] = own_ref[:TOP, :]
    right_ref[:, :NB] = own_ref[TOP:, :]
    for unit in range(PROW):
        top_ref[unit * 16 : unit * 16 + 16, NB:COLS] = gathered_ref[unit * 32 : unit * 32 + 16, :]
    origin = origin_ref[:, :1]

    @pl.loop(0, REST // NB)
    def _(c):
        right_ref[:, lane_block(c + 1)] = moved_rows(
            origin, gathered_ref[:, lane_block(c)], a_ref[:, lane_block(c + 1)]
        )


def dense(pivots, matrix, lower_inverse, upper_inverse):
    prow = lax.axis_index("prow")
    pcol = lax.axis_index("pcol")
    place = jnp.stack([prow, pcol]).astype(jnp.int32)
    picked_first, picked_rest, origin = pl.pallas_call(
        pick_kernel,
        in_specs=[SMEM, VMEM, VMEM, VMEM],
        out_specs=[VMEM] * 3,
        out_shape=[
            jax.ShapeDtypeStruct((TOP, NB), F32),
            jax.ShapeDtypeStruct((TOP, REST), F32),
            jax.ShapeDtypeStruct((ROWS, NB), jnp.int32),
        ],
    )(place, pivots.reshape(PANELS, NB), pivots.reshape(TOP, 1), matrix)
    gathered_first = exchange_first(picked_first, matrix[:NB, :NB])
    (own,) = kernel_call(column_kernel, [((TOP + ROWS, NB), F32)])(origin, gathered_first, matrix)
    blocks = spread_columns(own, pcol)
    gathered_rest = exchange_rest(picked_rest, matrix[:NB, NB:])
    top, right = kernel_call(
        dense_rows_kernel, [((TOP, WIDE - NB), F32), ((ROWS, COLS), F32)]
    )(origin, gathered_rest, matrix, own, *blocks)
    left = [block[TOP:] for block in blocks]
    return factor(top, right, lower_inverse, upper_inverse, *left)


def per_device(matrix, pivots, lower_inverse, upper_inverse):
    send, *leaving, block, plan, over = kernel_call(
        plan_kernel,
        [((64, COLS), F32)]
        + [((48, COLS), F32)] * 4
        + [((ROWS, NB), F32), ((544, NB), jnp.int32), ((8, NB), jnp.int32)],
        [pltpu.VMEM((8, NB), jnp.int32), pltpu.VMEM((8, NB), jnp.int32)],
    )(pivots.reshape(PANELS, NB), matrix)
    return lax.cond(
        over[0, 0] <= 0,
        lambda: slotted(send, leaving, block, plan, matrix, lower_inverse, upper_inverse),
        lambda: dense(pivots, matrix, lower_inverse, upper_inverse),
    )


def solution(mesh):
    in_specs = (P("prow", "pcol"), P(), P(), P())
    out_specs = P("prow", "pcol")
    return jax.shard_map(
        per_device, mesh=mesh, in_specs=in_specs, out_specs=out_specs, check_vma=False
    )
```

```python
import jax
import jax.numpy as jnp
from jax import lax
from jax.experimental import pallas as pl
from jax.experimental.pallas import tpu as pltpu
from jax.sharding import PartitionSpec as P

NB = 128
PANELS = 4
TOP = NB * PANELS
PROW = 32
PCOL = 16
ROWS = 256
COLS = 768
REST = COLS - NB
WIDE = TOP + COLS
KERNEL_VMEM = 20 << 20
FACTOR_VMEM = 28 << 20
BF = jnp.bfloat16
F32 = jnp.float32
X_GROUPS = [[x * 8 + z for x in range(4)] for z in range(8)]
Z_GROUPS = [[x * 8 + z for z in range(8)] for x in range(4)]
VMEM = pl.BlockSpec(memory_space=pltpu.VMEM)
SMEM = pl.BlockSpec(memory_space=pltpu.SMEM)
HBM = pl.BlockSpec(memory_space=pltpu.HBM)


def mm(left, right):
    return lax.dot_general(left, right, (((1,), (0,)), ((), ())), preferred_element_type=F32)


def split2(value):
    high = value.astype(BF)
    low = (value - high.astype(F32)).astype(BF)
    return high, low


def select_rows(onehot, value):
    first = value.astype(BF)
    rest = value - first.astype(F32)
    second = rest.astype(BF)
    third = (rest - second.astype(F32)).astype(BF)
    return mm(onehot, first) + mm(onehot, second) + mm(onehot, third)


def dot3(left, right):
    lh, ll = split2(left)
    rh, rl = split2(right)
    return mm(jnp.concatenate([lh, ll, lh], axis=1), jnp.concatenate([rh, rh, rl], axis=0))


def chase(rows, piv_row_ref, panels):
    lanes = lax.broadcasted_iota(jnp.int32, (rows.shape[0], NB), 1).astype(F32)
    for m in panels:
        equal = rows == piv_row_ref[m : m + 1, :]
        hit = jnp.sum(jnp.where(equal, lanes + float(m * NB + 1), 0.0), axis=1, keepdims=True)
        hit = hit.astype(jnp.int32)
        rows = jnp.where(hit > 0, hit - 1, rows)
    return rows


def pick_kernel(place_ref, piv_row_ref, piv_col_ref, a_ref, first_ref, rest_ref, origin_ref):
    prow = place_ref[0]
    lane = lax.broadcasted_iota(jnp.int32, (NB, ROWS), 1)
    for k in range(PANELS):
        rows = chase(piv_col_ref[k * NB : (k + 1) * NB, :], piv_row_ref, range(k - 1, -1, -1))
        owner = (rows >> 7) & 31
        slot = ((rows >> 12) << 7) | (rows & 127)
        slot = jnp.where(owner == prow, slot, -1)
        onehot = jnp.where(lane == slot, 1.0, 0.0).astype(BF)
        first_ref[k * NB : (k + 1) * NB, :] = select_rows(onehot, a_ref[:, :NB])
        rest_ref[k * NB : (k + 1) * NB, :] = select_rows(onehot, a_ref[:, NB:])
    local = lax.broadcasted_iota(jnp.int32, (ROWS, 1), 0)
    rows = ((local >> 7) * PROW + prow) * NB + (local & 127)
    rows = chase(rows, piv_row_ref, range(PANELS - 1, -1, -1))
    origin_ref[...] = jnp.broadcast_to(rows, (ROWS, NB))


def place_of(origin):
    unit = (origin >> 2) & 31
    return (unit << 5) + 16 + ((origin >> 7) << 2) + (origin & 3)


def moved_rows(origin, gathered, kept):
    lane = lax.broadcasted_iota(jnp.int32, (ROWS, 1024), 1)
    onehot = jnp.where(lane == jnp.where(origin < TOP, place_of(origin), -1), 1.0, 0.0).astype(BF)
    return jnp.where(origin < TOP, select_rows(onehot, gathered), kept)


def column_kernel(origin_ref, gathered_ref, a_ref, out_ref):
    origin = origin_ref[:, :1]
    for unit in range(PROW):
        out_ref[unit * 16 : unit * 16 + 16, :] = gathered_ref[unit * 32 : unit * 32 + 16, :]
    out_ref[TOP:, :] = moved_rows(origin, gathered_ref[...], a_ref[:, :NB])


def exchange_first(picked, top):
    sent = jnp.concatenate([picked.reshape(PROW, 16, NB), top.reshape(PROW, 4, NB)], axis=1)
    got = lax.all_to_all(sent, "prow", 0, 0)
    chunk = jnp.concatenate([jnp.sum(got[:, :16], axis=0), got[:4, 16:].reshape(16, NB)], axis=0)
    sent = jnp.broadcast_to(chunk[None], (PROW, 32, NB))
    return lax.all_to_all(sent, "prow", 0, 0).reshape(PROW * 32, NB)


def exchange_rest(picked, top):
    sent = jnp.concatenate([picked.reshape(4, NB, REST), top.reshape(4, 32, REST)], axis=1)
    got = lax.all_to_all(sent, "prow", 0, 0, axis_index_groups=X_GROUPS)
    sent = jnp.concatenate(
        [jnp.sum(got[:, :NB], axis=0).reshape(8, 16, REST), got[0, NB:].reshape(8, 4, REST)], axis=1
    )
    got = lax.all_to_all(sent, "prow", 0, 0, axis_index_groups=Z_GROUPS)
    chunk = jnp.concatenate([jnp.sum(got[:, :16], axis=0), got[:4, 16:].reshape(16, REST)], axis=0)
    got = lax.all_to_all(
        jnp.broadcast_to(chunk[None], (8, 32, REST)), "prow", 0, 0, axis_index_groups=Z_GROUPS
    )
    got = got.reshape(256, REST)
    got = lax.all_to_all(
        jnp.broadcast_to(got[None], (4, 256, REST)), "prow", 0, 0, axis_index_groups=X_GROUPS
    )
    return got.reshape(PROW * 32, REST)


def spread_start(own):
    up = lax.ppermute(own, "pcol", [(q, q + 4) for q in range(4)])
    down = lax.ppermute(own, "pcol", [(q, q + 12) for q in range(4)])
    return up, down


def spread_columns(own, pcol):
    return spread_rest(own, *spread_start(own), pcol)


def spread_rest(own, up, down, pcol):
    near = jnp.where(pcol < 4, own, jnp.where(pcol < 8, up, down))
    half = near.shape[0] // 2
    left = lax.ppermute(near[:half], "pcol", [(q + 4, q + 8) for q in range(4)])
    right = lax.ppermute(near[half:], "pcol", [(q + 12, q + 8) for q in range(4)])
    far = (pcol >= 8) & (pcol < 12)
    near = jnp.where(far, jnp.concatenate([left, right], axis=0), near)
    return [near] + [lax.ppermute(near, "pcol", [(q, q ^ n) for q in range(PCOL)]) for n in (1, 2, 3)]


def lane_sum(mask, value):
    return jnp.sum(jnp.where(mask, value, 0.0), axis=1, keepdims=True)


def sub_sum(mask, value):
    return jnp.sum(jnp.where(mask, value, 0.0), axis=0, keepdims=True).astype(jnp.int32)


def iota(shape, axis):
    return lax.broadcasted_iota(jnp.int32, shape, axis)


def ranks(masks):
    count = len(masks)
    padded = -(-count // 8) * 8
    rows = [jnp.where(mask, 1.0, 0.0) for mask in masks]
    rows = rows + [jnp.zeros((1, NB), F32)] * (padded - count)
    before = jnp.where(iota((NB, NB), 0) < iota((NB, NB), 1), 1.0, 0.0).astype(BF)
    found = mm(jnp.concatenate(rows, axis=0).astype(BF), before)
    return [found[n : n + 1, :] for n in range(count)]


def slots(mask, rank, value, capacity):
    row = iota((capacity, NB), 0).astype(F32)
    return lane_sum(mask & (rank == row), value + 1.0).astype(jnp.int32) - 1


def onehot_of(column, width):
    return jnp.where(iota((column.shape[0], width), 1) == column, 1.0, 0.0).astype(BF)


def plan_kernel(
    pivots_ref, a_ref, send_ref, leave0_ref, leave1_ref, leave2_ref, leave3_ref, block_ref, plan_ref,
    over_ref, source_ref, target_ref,
):
    prow = lax.axis_index("prow")
    x = prow >> 3
    z = prow & 7
    sub = iota((NB, NB), 0)
    lane = iota((NB, NB), 1)
    subf = sub.astype(F32)
    lane_row = iota((1, NB), 1)
    piv_row = [pivots_ref[m : m + 1, :] for m in range(PANELS)]
    piv_col = []
    for m in range(PANELS):
        piv_col.append(lane_sum(sub == lane, piv_row[m].astype(F32)).astype(jnp.int32))

    def met(m, rows):
        return sub_sum(piv_col[m] == rows, subf + float(m * NB + 1))

    source = []
    target = []
    for k in range(PANELS):
        rows = piv_row[k]
        for m in range(k - 1, -1, -1):
            hit = met(m, rows)
            rows = jnp.where(hit > 0, hit - 1, rows)
        source.append(rows)
        source_ref[k : k + 1, :] = rows
        rows = lane_row + k * NB
        for m in range(PANELS):
            if m == k:
                rows = jnp.where(rows == lane_row + k * NB, piv_row[k], rows)
                continue
            hit = met(m, rows)
            moved = jnp.where(hit > 0, hit - 1, rows)
            if m > k:
                look = sub_sum(sub + m * NB == rows, piv_col[m].astype(F32))
                moved = jnp.where(look > 0, look, moved)
            rows = moved
        target.append(rows)
        target_ref[k : k + 1, :] = rows

    def local_of(rows):
        return ((rows >> 12) << 7) | (rows & 127)

    def owner_of(rows):
        return (rows >> 7) & 31

    masks = [owner_of(source[k]) == prow for k in range(PANELS)]
    order = ranks(masks)
    chosen = [
        slots(masks[k], order[k], local_of(source[k]).astype(F32), 16) for k in range(PANELS)
    ]
    send_ref[...] = select_rows(onehot_of(jnp.concatenate(chosen, axis=0), ROWS), a_ref[...])
    mine = target_ref[pl.ds(prow & 3, 1), :]
    leaves = (mine >= TOP) & (prow < PANELS)
    masks = [leaves & (((mine >> 10) & 3) == n) for n in range(4)]
    order = ranks(masks)
    lanef = lane_row.astype(F32)
    chosen = [slots(masks[n], order[n], lanef, 48) for n in range(4)]
    leaving = select_rows(onehot_of(jnp.concatenate(chosen, axis=0), NB), a_ref[:NB, :])
    block_ref[...] = a_ref[:, :NB]
    for n, ref in enumerate((leave0_ref, leave1_ref, leave2_ref, leave3_ref)):
        ref[...] = leaving[48 * n : 48 * n + 48]

    panel = source_ref[pl.ds(x, 1), :]
    panel_z = (panel >> 7) & 7
    panel_x = (panel >> 10) & 3
    here = panel_z == z
    masks = [here & (panel_x == n) for n in range(4)] + [here]
    order = ranks(masks)
    spot = jnp.zeros((1, NB), F32)
    for n in range(4):
        spot = spot + jnp.where(masks[n], order[n] + 16.0 * n, 0.0)
    wide = lambda column: jnp.broadcast_to(column, (column.shape[0], NB))
    plan_ref[0:32, :] = wide(slots(here, order[4], spot, 32))
    other = target_ref[pl.ds(z & 3, 1), :]
    along = (other >= TOP) & (z < PANELS) & (((other >> 10) & 3) == x)
    masks = [along & (((other >> 7) & 7) == n) for n in range(8)] + [along]
    order = ranks(masks)
    for n in range(8):
        plan_ref[32 + 16 * n : 48 + 16 * n, :] = wide(slots(masks[n], order[n], order[8], 16))
    zf = panel_z.astype(F32)
    zcol = lane_sum(sub == lane, zf)
    ahead = lane_sum((zf == zcol) & (lane < sub), 1.0)
    plan_ref[160:288, :] = wide((zcol * 32.0 + ahead).astype(jnp.int32))
    masks = [(target[k] >= TOP) & (owner_of(target[k]) == prow) for k in range(PANELS)]
    order = ranks(masks)
    row = iota((ROWS, NB), 0)
    total = jnp.zeros((ROWS, 1), F32)
    for k in range(PANELS):
        total = total + lane_sum(masks[k] & (local_of(target[k]) == row), order[k] + (16.0 * k + 1.0))
    plan_ref[288:544, :] = wide(total.astype(jnp.int32) - 1)
    unit = iota((PROW, NB), 0)
    over = jnp.zeros((PROW, 1), F32)
    for k in range(PANELS):
        leaves = target[k] >= TOP
        for mask, cap in (
            (owner_of(source[k]) == unit, 16.0),
            (((source[k] >> 7) & 7) == unit, 32.0),
            (leaves & (((target[k] >> 10) & 3) == unit), 48.0),
            (leaves & (owner_of(target[k]) == unit), 16.0),
        ):
            over = jnp.maximum(over, lane_sum(mask, 1.0) - cap)
    over = jnp.max(over, axis=0, keepdims=True)
    over_ref[...] = jnp.broadcast_to(over, (8, NB)).astype(jnp.int32)


def turn_kernel(plan_ref, got_ref, first_ref, rest_ref):
    rows = select_rows(onehot_of(plan_ref[0:32, :1], 64), got_ref[...])
    for n in range(8):
        first_ref[n] = rows[:, :NB]
    rest_ref[...] = rows[:, NB:]


def join_kernel(plan_ref, rows_ref, leave0_ref, leave1_ref, leave2_ref, leave3_ref, send_ref):
    held = leave1_ref[...] + leave2_ref[...] + leave3_ref[...]
    held = jnp.where(lax.axis_index("prow") < 8, leave0_ref[...], held)
    sent = select_rows(onehot_of(plan_ref[32:160, :1], 48), held)
    for n in range(8):
        for c in range(REST // NB):
            send_ref[n, 32 * c : 32 * c + 32, :] = rows_ref[:, c * NB : c * NB + NB]
        for c in range(COLS // NB):
            spot = 160 + 16 * c
            send_ref[n, spot : spot + 16, :] = sent[16 * n : 16 * n + 16, c * NB : c * NB + NB]


def lead_kernel(plan_ref, got_ref, lead_ref):
    lead_ref[...] = select_rows(onehot_of(plan_ref[160:288, :1], 256), got_ref[...])


def pivot_part(got_ref, c):
    return jnp.concatenate([got_ref[n, 32 * c : 32 * c + 32, :] for n in range(8)], axis=0)


def moved_part(got_ref, c):
    spot = 160 + 16 * c
    return jnp.concatenate([got_ref[n, spot : spot + 16, :] for n in range(4)], axis=0)


def panel_kernel(plan_ref, lead_ref, got_ref, *refs):
    blocks, (send_ref, full_ref, sems) = refs[:4], refs[4:]
    panel = lax.axis_index("prow") >> 3
    got = jnp.concatenate([pivot_part(got_ref, c) for c in range(REST // NB)], axis=1)
    full_ref[:, :NB] = lead_ref[...]
    full_ref[:, NB:COLS] = select_rows(onehot_of(plan_ref[160:288, :1], 256), got)

    def store(index, value):
        @pl.when(index != panel)
        def _():
            spot = COLS // NB + jnp.where(index < panel, index, index - 1)
            full_ref[:, lane_block(spot)] = value

    put_columns(blocks, slice(0, NB), store)
    copies = [
        pltpu.make_async_copy(full_ref, send_ref.at[n], sems.at[n]) for n in range(4)
    ]
    for copy in copies:
        copy.start()
    for copy in copies:
        copy.wait()


def put_columns(block_refs, rows, store):
    kind = lax.axis_index("pcol") & 3
    for n, ref in enumerate(block_refs):
        store(kind ^ n, ref[rows, :])


def lane_block(index):
    return pl.ds(pl.multiple_of(index * NB, NB), NB)


def first_rows_kernel(plan_ref, got_ref, block_ref, out_ref):
    slot = plan_ref[288:544, :1]
    moved = select_rows(onehot_of(slot, 64), moved_part(got_ref, 0))
    out_ref[...] = jnp.where(slot >= 0, moved, block_ref[...])


def own_rows_kernel(plan_ref, rows_ref, got_ref, a_ref, out_ref):
    slot = plan_ref[288:544, :1]
    moved = jnp.concatenate([moved_part(got_ref, c) for c in range(1, COLS // NB)], axis=1)
    moved = select_rows(onehot_of(slot, 64), moved)
    out_ref[:, :NB] = rows_ref[...]
    out_ref[:, NB:] = jnp.where(slot >= 0, moved, a_ref[:, NB:])


def factor_kernel(
    top_ref, right_ref, lower_ref, upper_ref, left0_ref, left1_ref, left2_ref, left3_ref,
    result_ref, z_ref, y_ref, m_ref, u_ref, d_ref, out_ref, sems,
):
    prow = lax.axis_index("prow")
    pcol = lax.axis_index("pcol")
    fetches = []
    for n, ref in enumerate((left0_ref, left1_ref, left2_ref, left3_ref)):
        target = z_ref.at[TOP : TOP + ROWS, lane_block((pcol & 3) ^ n)]
        fetches.append(pltpu.make_async_copy(ref, target, sems.at[n]))
    fetches.append(pltpu.make_async_copy(right_ref, out_ref, sems.at[4]))
    for fetch in fetches:
        fetch.start()
    for k in range(PANELS):
        rows = slice(k * NB, k * NB + NB)
        for spot in range(PANELS - 1):
            block = spot if spot < k else spot + 1
            z_ref[rows, block * NB : block * NB + NB] = top_ref[
                rows, COLS + spot * NB : COLS + spot * NB + NB
            ]
    for k in range(PANELS):
        s = k * NB
        e = s + NB
        before = top_ref if k == 0 else y_ref
        lh, ll = split2(lower_ref[k])
        l3 = jnp.concatenate([lh, ll, lh], axis=1)
        if e < TOP:
            bh, bl = split2(z_ref[s:e, e:])
            corner = mm(l3, jnp.concatenate([bh, bh, bl], axis=0))
            z_ref[s:e, e:] = corner
            uh, ul = split2(corner)
            corner3 = jnp.concatenate([uh, uh, ul], axis=0)
        d_ref[s:e, :] = before[s:e, :NB]
        bh, bl = split2(before[s:e, :COLS])
        upper_rows = mm(l3, jnp.concatenate([bh, bh, bl], axis=0))
        y_ref[s:e, :] = upper_rows
        uh, ul = split2(upper_rows)
        u3 = jnp.concatenate([uh, uh, ul], axis=0)
        u_ref[3 * s : 3 * e, :] = u3
        if k == 0:
            for fetch in fetches[:4]:
                fetch.wait()
        multipliers = dot3(z_ref[e:, s:e], upper_ref[k])
        z_ref[e:, s:e] = multipliers
        mh, ml = split2(multipliers)
        m3 = jnp.concatenate([mh, ml, mh], axis=1)
        m_ref[:, 3 * s : 3 * e] = m3[TOP - e :]
        if e < TOP:
            z_ref[e:, e:] = z_ref[e:, e:] - mm(m3, corner3)
            y_ref[e:TOP, :] = before[e:TOP, :COLS] - mm(m3[: TOP - e], u3)
    fetches[4].wait()
    out_ref[...] = out_ref[...] - mm(m_ref[...], u_ref[...])
    panel_cols = lane_block(pcol & 3)
    top_rows = pl.ds(pl.multiple_of((prow & 3) * NB, NB), NB)

    @pl.when(pcol < PANELS)
    def _():
        out_ref[:, :NB] = z_ref[TOP:, panel_cols]

    @pl.when(prow < PANELS)
    def _():
        out_ref[:NB, :] = y_ref[top_rows, :]

    @pl.when((prow < PANELS) & (pcol < PANELS))
    def _():
        out_ref[:NB, :NB] = jnp.where(
            prow == pcol, d_ref[top_rows, :], z_ref[top_rows, panel_cols]
        )

    copy = pltpu.make_async_copy(out_ref, result_ref, sems.at[5])
    copy.start()
    copy.wait()


def kernel_call(body, shapes, scratch=(), out=None):
    def call(*args):
        return pl.pallas_call(
            body,
            in_specs=[VMEM] * len(args),
            out_specs=out or [VMEM] * len(shapes),
            out_shape=[jax.ShapeDtypeStruct(shape, kind) for shape, kind in shapes],
            scratch_shapes=list(scratch),
            compiler_params=pltpu.CompilerParams(vmem_limit_bytes=KERNEL_VMEM),
        )(*args)

    return call


def factor(top, right, lower_inverse, upper_inverse, *left):
    right, *left = [
        pltpu.with_memory_space_constraint(value, pltpu.HBM) for value in (right, *left)
    ]
    args = (top, right, lower_inverse, upper_inverse, *left)
    result = pl.pallas_call(
        factor_kernel,
        in_specs=[VMEM, HBM, VMEM, VMEM] + [HBM] * 4,
        out_specs=HBM,
        out_shape=jax.ShapeDtypeStruct((ROWS, COLS), F32),
        scratch_shapes=[
            pltpu.VMEM((TOP + ROWS, TOP), F32),
            pltpu.VMEM((TOP, COLS), F32),
            pltpu.VMEM((ROWS, 3 * TOP), BF),
            pltpu.VMEM((3 * TOP, COLS), BF),
            pltpu.VMEM((TOP, NB), F32),
            pltpu.VMEM((ROWS, COLS), F32),
            pltpu.SemaphoreType.DMA((6,)),
        ],
        compiler_params=pltpu.CompilerParams(vmem_limit_bytes=FACTOR_VMEM),
    )(*args)
    return pltpu.with_memory_space_constraint(result, pltpu.HBM)


def along(value, groups):
    return lax.all_to_all(value, "prow", 0, 0, axis_index_groups=groups)


def slotted(send, leaving, block, plan, matrix, lower_inverse, upper_inverse):
    pcol = lax.axis_index("pcol")
    got = along(send.reshape(4, 16, COLS), X_GROUPS)
    held = [leaving[0]]
    for n in range(1, 4):
        pairs = [(k, 8 * n + k) for k in range(PANELS)]
        held.append(lax.ppermute(leaving[n], "prow", pairs))
    first, rest = kernel_call(turn_kernel, [((8, 32, NB), F32), ((32, REST), F32)])(
        plan, got.reshape(64, COLS)
    )
    first = along(first, Z_GROUPS)
    (rest,) = kernel_call(join_kernel, [((8, 256, NB), F32)])(plan, rest, *held)
    rest = along(rest, Z_GROUPS)
    (lead,) = kernel_call(lead_kernel, [((NB, NB), F32)])(plan, first.reshape(256, NB))
    ends = spread_start(lead)
    late = spread_rest(lead, *ends, pcol)
    (send,) = kernel_call(
        panel_kernel,
        [((4, NB, WIDE - NB), F32)],
        [pltpu.VMEM((NB, WIDE - NB), F32), pltpu.SemaphoreType.DMA((4,))],
        [HBM],
    )(plan, lead, rest, *late)
    top = along(send, X_GROUPS).reshape(TOP, WIDE - NB)
    (rows,) = kernel_call(first_rows_kernel, [((ROWS, NB), F32)])(plan, rest, block)
    ends = spread_start(rows)
    left = spread_rest(rows, *ends, pcol)
    (right,) = kernel_call(own_rows_kernel, [((ROWS, COLS), F32)])(plan, rows, rest, matrix)
    return factor(top, right, lower_inverse, upper_inverse, *left)


def dense_rows_kernel(
    origin_ref, gathered_ref, a_ref, own_ref, block0_ref, block1_ref, block2_ref, block3_ref,
    top_ref, right_ref,
):
    def store_corner(index, value):
        for k in range(PANELS):

            @pl.when(index != k)
            def _():
                spot = lane_block(COLS // NB + jnp.where(index < k, index, index - 1))
                top_ref[k * NB : k * NB + NB, spot] = value[k * NB : k * NB + NB]

    put_columns((block0_ref, block1_ref, block2_ref, block3_ref), slice(0, TOP), store_corner)
    top_ref[:, :NB] = own_ref[:TOP, :]
    right_ref[:, :NB] = own_ref[TOP:, :]
    for unit in range(PROW):
        top_ref[unit * 16 : unit * 16 + 16, NB:COLS] = gathered_ref[unit * 32 : unit * 32 + 16, :]
    origin = origin_ref[:, :1]

    @pl.loop(0, REST // NB)
    def _(c):
        right_ref[:, lane_block(c + 1)] = moved_rows(
            origin, gathered_ref[:, lane_block(c)], a_ref[:, lane_block(c + 1)]
        )


def dense(pivots, matrix, lower_inverse, upper_inverse):
    prow = lax.axis_index("prow")
    pcol = lax.axis_index("pcol")
    place = jnp.stack([prow, pcol]).astype(jnp.int32)
    picked_first, picked_rest, origin = pl.pallas_call(
        pick_kernel,
        in_specs=[SMEM, VMEM, VMEM, VMEM],
        out_specs=[VMEM] * 3,
        out_shape=[
            jax.ShapeDtypeStruct((TOP, NB), F32),
            jax.ShapeDtypeStruct((TOP, REST), F32),
            jax.ShapeDtypeStruct((ROWS, NB), jnp.int32),
        ],
    )(place, pivots.reshape(PANELS, NB), pivots.reshape(TOP, 1), matrix)
    gathered_first = exchange_first(picked_first, matrix[:NB, :NB])
    (own,) = kernel_call(column_kernel, [((TOP + ROWS, NB), F32)])(origin, gathered_first, matrix)
    blocks = spread_columns(own, pcol)
    gathered_rest = exchange_rest(picked_rest, matrix[:NB, NB:])
    top, right = kernel_call(
        dense_rows_kernel, [((TOP, WIDE - NB), F32), ((ROWS, COLS), F32)]
    )(origin, gathered_rest, matrix, own, *blocks)
    left = [block[TOP:] for block in blocks]
    return factor(top, right, lower_inverse, upper_inverse, *left)


def per_device(matrix, pivots, lower_inverse, upper_inverse):
    send, *leaving, block, plan, over = kernel_call(
        plan_kernel,
        [((64, COLS), F32)]
        + [((48, COLS), F32)] * 4
        + [((ROWS, NB), F32), ((544, NB), jnp.int32), ((8, NB), jnp.int32)],
        [pltpu.VMEM((8, NB), jnp.int32), pltpu.VMEM((8, NB), jnp.int32)],
    )(pivots.reshape(PANELS, NB), matrix)
    return lax.cond(
        over[0, 0] <= 0,
        lambda: slotted(send, leaving, block, plan, matrix, lower_inverse, upper_inverse),
        lambda: dense(pivots, matrix, lower_inverse, upper_inverse),
    )


def solution(mesh):
    in_specs = (P("prow", "pcol"), P(), P(), P())
    out_specs = P("prow", "pcol")
    return jax.shard_map(
        per_device, mesh=mesh, in_specs=in_specs, out_specs=out_specs, check_vma=False
    )
```

```python
import jax
import jax.numpy as jnp
from jax import lax
from jax.experimental import pallas as pl
from jax.experimental.pallas import tpu as pltpu
from jax.sharding import PartitionSpec as P

NB = 128
PANELS = 4
TOP = NB * PANELS
PROW = 32
PCOL = 16
ROWS = 256
COLS = 768
REST = COLS - NB
WIDE = TOP + COLS
KERNEL_VMEM = 20 << 20
FACTOR_VMEM = 28 << 20
BF = jnp.bfloat16
F32 = jnp.float32
X_GROUPS = [[x * 8 + z for x in range(4)] for z in range(8)]
Z_GROUPS = [[x * 8 + z for z in range(8)] for x in range(4)]
VMEM = pl.BlockSpec(memory_space=pltpu.VMEM)
SMEM = pl.BlockSpec(memory_space=pltpu.SMEM)
HBM = pl.BlockSpec(memory_space=pltpu.HBM)


def mm(left, right):
    return lax.dot_general(left, right, (((1,), (0,)), ((), ())), preferred_element_type=F32)


def split2(value):
    high = value.astype(BF)
    low = (value - high.astype(F32)).astype(BF)
    return high, low


def select_rows(onehot, value):
    first = value.astype(BF)
    rest = value - first.astype(F32)
    second = rest.astype(BF)
    third = (rest - second.astype(F32)).astype(BF)
    return mm(onehot, first) + mm(onehot, second) + mm(onehot, third)


def dot3(left, right):
    lh, ll = split2(left)
    rh, rl = split2(right)
    return mm(jnp.concatenate([lh, ll, lh], axis=1), jnp.concatenate([rh, rh, rl], axis=0))


def chase(rows, piv_row_ref, panels):
    lanes = lax.broadcasted_iota(jnp.int32, (rows.shape[0], NB), 1).astype(F32)
    for m in panels:
        equal = rows == piv_row_ref[m : m + 1, :]
        hit = jnp.sum(jnp.where(equal, lanes + float(m * NB + 1), 0.0), axis=1, keepdims=True)
        hit = hit.astype(jnp.int32)
        rows = jnp.where(hit > 0, hit - 1, rows)
    return rows


def pick_kernel(place_ref, piv_row_ref, piv_col_ref, a_ref, first_ref, rest_ref, origin_ref):
    prow = place_ref[0]
    lane = lax.broadcasted_iota(jnp.int32, (NB, ROWS), 1)
    for k in range(PANELS):
        rows = chase(piv_col_ref[k * NB : (k + 1) * NB, :], piv_row_ref, range(k - 1, -1, -1))
        owner = (rows >> 7) & 31
        slot = ((rows >> 12) << 7) | (rows & 127)
        slot = jnp.where(owner == prow, slot, -1)
        onehot = jnp.where(lane == slot, 1.0, 0.0).astype(BF)
        first_ref[k * NB : (k + 1) * NB, :] = select_rows(onehot, a_ref[:, :NB])
        rest_ref[k * NB : (k + 1) * NB, :] = select_rows(onehot, a_ref[:, NB:])
    local = lax.broadcasted_iota(jnp.int32, (ROWS, 1), 0)
    rows = ((local >> 7) * PROW + prow) * NB + (local & 127)
    rows = chase(rows, piv_row_ref, range(PANELS - 1, -1, -1))
    origin_ref[...] = jnp.broadcast_to(rows, (ROWS, NB))


def place_of(origin):
    unit = (origin >> 2) & 31
    return (unit << 5) + 16 + ((origin >> 7) << 2) + (origin & 3)


def moved_rows(origin, gathered, kept):
    lane = lax.broadcasted_iota(jnp.int32, (ROWS, 1024), 1)
    onehot = jnp.where(lane == jnp.where(origin < TOP, place_of(origin), -1), 1.0, 0.0).astype(BF)
    return jnp.where(origin < TOP, select_rows(onehot, gathered), kept)


def column_kernel(origin_ref, gathered_ref, a_ref, out_ref):
    origin = origin_ref[:, :1]
    for unit in range(PROW):
        out_ref[unit * 16 : unit * 16 + 16, :] = gathered_ref[unit * 32 : unit * 32 + 16, :]
    out_ref[TOP:, :] = moved_rows(origin, gathered_ref[...], a_ref[:, :NB])


def exchange_first(picked, top):
    sent = jnp.concatenate([picked.reshape(PROW, 16, NB), top.reshape(PROW, 4, NB)], axis=1)
    got = lax.all_to_all(sent, "prow", 0, 0)
    chunk = jnp.concatenate([jnp.sum(got[:, :16], axis=0), got[:4, 16:].reshape(16, NB)], axis=0)
    sent = jnp.broadcast_to(chunk[None], (PROW, 32, NB))
    return lax.all_to_all(sent, "prow", 0, 0).reshape(PROW * 32, NB)


def exchange_rest(picked, top):
    sent = jnp.concatenate([picked.reshape(4, NB, REST), top.reshape(4, 32, REST)], axis=1)
    got = lax.all_to_all(sent, "prow", 0, 0, axis_index_groups=X_GROUPS)
    sent = jnp.concatenate(
        [jnp.sum(got[:, :NB], axis=0).reshape(8, 16, REST), got[0, NB:].reshape(8, 4, REST)], axis=1
    )
    got = lax.all_to_all(sent, "prow", 0, 0, axis_index_groups=Z_GROUPS)
    chunk = jnp.concatenate([jnp.sum(got[:, :16], axis=0), got[:4, 16:].reshape(16, REST)], axis=0)
    got = lax.all_to_all(
        jnp.broadcast_to(chunk[None], (8, 32, REST)), "prow", 0, 0, axis_index_groups=Z_GROUPS
    )
    got = got.reshape(256, REST)
    got = lax.all_to_all(
        jnp.broadcast_to(got[None], (4, 256, REST)), "prow", 0, 0, axis_index_groups=X_GROUPS
    )
    return got.reshape(PROW * 32, REST)


def spread_start(own):
    up = lax.ppermute(own, "pcol", [(q, q + 4) for q in range(4)])
    down = lax.ppermute(own, "pcol", [(q, q + 12) for q in range(4)])
    return up, down


def spread_columns(own, pcol):
    return spread_rest(own, *spread_start(own), pcol)


def spread_rest(own, up, down, pcol):
    near = jnp.where(pcol < 4, own, jnp.where(pcol < 8, up, down))
    half = near.shape[0] // 2
    left = lax.ppermute(near[:half], "pcol", [(q + 4, q + 8) for q in range(4)])
    right = lax.ppermute(near[half:], "pcol", [(q + 12, q + 8) for q in range(4)])
    far = (pcol >= 8) & (pcol < 12)
    near = jnp.where(far, jnp.concatenate([left, right], axis=0), near)
    return [near] + [lax.ppermute(near, "pcol", [(q, q ^ n) for q in range(PCOL)]) for n in (1, 2, 3)]


def lane_sum(mask, value):
    return jnp.sum(jnp.where(mask, value, 0.0), axis=1, keepdims=True)


def sub_sum(mask, value):
    return jnp.sum(jnp.where(mask, value, 0.0), axis=0, keepdims=True).astype(jnp.int32)


def iota(shape, axis):
    return lax.broadcasted_iota(jnp.int32, shape, axis)


def ranks(masks):
    count = len(masks)
    padded = -(-count // 8) * 8
    rows = [jnp.where(mask, 1.0, 0.0) for mask in masks]
    rows = rows + [jnp.zeros((1, NB), F32)] * (padded - count)
    before = jnp.where(iota((NB, NB), 0) < iota((NB, NB), 1), 1.0, 0.0).astype(BF)
    found = mm(jnp.concatenate(rows, axis=0).astype(BF), before)
    return [found[n : n + 1, :] for n in range(count)]


def slots(mask, rank, value, capacity):
    row = iota((capacity, NB), 0).astype(F32)
    return lane_sum(mask & (rank == row), value + 1.0).astype(jnp.int32) - 1


def onehot_of(column, width):
    return jnp.where(iota((column.shape[0], width), 1) == column, 1.0, 0.0).astype(BF)


def plan_kernel(
    pivots_ref, a_ref, send_ref, leave0_ref, leave1_ref, leave2_ref, leave3_ref, block_ref, plan_ref,
    over_ref, source_ref, target_ref,
):
    prow = lax.axis_index("prow")
    x = prow >> 3
    z = prow & 7
    sub = iota((NB, NB), 0)
    lane = iota((NB, NB), 1)
    subf = sub.astype(F32)
    lane_row = iota((1, NB), 1)
    piv_row = [pivots_ref[m : m + 1, :] for m in range(PANELS)]
    piv_col = []
    for m in range(PANELS):
        piv_col.append(lane_sum(sub == lane, piv_row[m].astype(F32)).astype(jnp.int32))

    def met(m, rows):
        return sub_sum(piv_col[m] == rows, subf + float(m * NB + 1))

    source = []
    target = []
    for k in range(PANELS):
        rows = piv_row[k]
        for m in range(k - 1, -1, -1):
            hit = met(m, rows)
            rows = jnp.where(hit > 0, hit - 1, rows)
        source.append(rows)
        source_ref[k : k + 1, :] = rows
        rows = lane_row + k * NB
        for m in range(PANELS):
            if m == k:
                rows = jnp.where(rows == lane_row + k * NB, piv_row[k], rows)
                continue
            hit = met(m, rows)
            moved = jnp.where(hit > 0, hit - 1, rows)
            if m > k:
                look = sub_sum(sub + m * NB == rows, piv_col[m].astype(F32))
                moved = jnp.where(look > 0, look, moved)
            rows = moved
        target.append(rows)
        target_ref[k : k + 1, :] = rows

    def local_of(rows):
        return ((rows >> 12) << 7) | (rows & 127)

    def owner_of(rows):
        return (rows >> 7) & 31

    masks = [owner_of(source[k]) == prow for k in range(PANELS)]
    order = ranks(masks)
    chosen = [
        slots(masks[k], order[k], local_of(source[k]).astype(F32), 16) for k in range(PANELS)
    ]
    send_ref[...] = select_rows(onehot_of(jnp.concatenate(chosen, axis=0), ROWS), a_ref[...])
    mine = target_ref[pl.ds(prow & 3, 1), :]
    leaves = (mine >= TOP) & (prow < PANELS)
    masks = [leaves & (((mine >> 10) & 3) == n) for n in range(4)]
    order = ranks(masks)
    lanef = lane_row.astype(F32)
    chosen = [slots(masks[n], order[n], lanef, 48) for n in range(4)]
    leaving = select_rows(onehot_of(jnp.concatenate(chosen, axis=0), NB), a_ref[:NB, :])
    block_ref[...] = a_ref[:, :NB]
    for n, ref in enumerate((leave0_ref, leave1_ref, leave2_ref, leave3_ref)):
        ref[...] = leaving[48 * n : 48 * n + 48]

    panel = source_ref[pl.ds(x, 1), :]
    panel_z = (panel >> 7) & 7
    panel_x = (panel >> 10) & 3
    here = panel_z == z
    masks = [here & (panel_x == n) for n in range(4)] + [here]
    order = ranks(masks)
    spot = jnp.zeros((1, NB), F32)
    for n in range(4):
        spot = spot + jnp.where(masks[n], order[n] + 16.0 * n, 0.0)
    wide = lambda column: jnp.broadcast_to(column, (column.shape[0], NB))
    plan_ref[0:32, :] = wide(slots(here, order[4], spot, 32))
    other = target_ref[pl.ds(z & 3, 1), :]
    along = (other >= TOP) & (z < PANELS) & (((other >> 10) & 3) == x)
    masks = [along & (((other >> 7) & 7) == n) for n in range(8)] + [along]
    order = ranks(masks)
    for n in range(8):
        plan_ref[32 + 16 * n : 48 + 16 * n, :] = wide(slots(masks[n], order[n], order[8], 16))
    zf = panel_z.astype(F32)
    zcol = lane_sum(sub == lane, zf)
    ahead = lane_sum((zf == zcol) & (lane < sub), 1.0)
    plan_ref[160:288, :] = wide((zcol * 32.0 + ahead).astype(jnp.int32))
    masks = [(target[k] >= TOP) & (owner_of(target[k]) == prow) for k in range(PANELS)]
    order = ranks(masks)
    row = iota((ROWS, NB), 0)
    total = jnp.zeros((ROWS, 1), F32)
    for k in range(PANELS):
        total = total + lane_sum(masks[k] & (local_of(target[k]) == row), order[k] + (16.0 * k + 1.0))
    plan_ref[288:544, :] = wide(total.astype(jnp.int32) - 1)
    unit = iota((PROW, NB), 0)
    over = jnp.zeros((PROW, 1), F32)
    for k in range(PANELS):
        leaves = target[k] >= TOP
        for mask, cap in (
            (owner_of(source[k]) == unit, 16.0),
            (((source[k] >> 7) & 7) == unit, 32.0),
            (leaves & (((target[k] >> 10) & 3) == unit), 48.0),
            (leaves & (owner_of(target[k]) == unit), 16.0),
        ):
            over = jnp.maximum(over, lane_sum(mask, 1.0) - cap)
    over = jnp.max(over, axis=0, keepdims=True)
    over_ref[...] = jnp.broadcast_to(over, (8, NB)).astype(jnp.int32)


def turn_kernel(plan_ref, got_ref, first_ref, rest_ref):
    rows = select_rows(onehot_of(plan_ref[0:32, :1], 64), got_ref[...])
    for n in range(8):
        first_ref[n] = rows[:, :NB]
    rest_ref[...] = rows[:, NB:]


def join_kernel(plan_ref, rows_ref, leave0_ref, leave1_ref, leave2_ref, leave3_ref, send_ref):
    held = leave1_ref[...] + leave2_ref[...] + leave3_ref[...]
    held = jnp.where(lax.axis_index("prow") < 8, leave0_ref[...], held)
    sent = select_rows(onehot_of(plan_ref[32:160, :1], 48), held)
    for n in range(8):
        for c in range(REST // NB):
            send_ref[n, 32 * c : 32 * c + 32, :] = rows_ref[:, c * NB : c * NB + NB]
        for c in range(COLS // NB):
            spot = 160 + 16 * c
            send_ref[n, spot : spot + 16, :] = sent[16 * n : 16 * n + 16, c * NB : c * NB + NB]


def lead_kernel(plan_ref, got_ref, lead_ref):
    lead_ref[...] = select_rows(onehot_of(plan_ref[160:288, :1], 256), got_ref[...])


def pivot_part(got_ref, c):
    return jnp.concatenate([got_ref[n, 32 * c : 32 * c + 32, :] for n in range(8)], axis=0)


def moved_part(got_ref, c):
    spot = 160 + 16 * c
    return jnp.concatenate([got_ref[n, spot : spot + 16, :] for n in range(4)], axis=0)


def panel_kernel(plan_ref, lead_ref, got_ref, block_ref, *refs):
    blocks, (send_ref, rows_ref, full_ref, sems) = refs[:4], refs[4:]
    panel = lax.axis_index("prow") >> 3
    got = jnp.concatenate([pivot_part(got_ref, c) for c in range(REST // NB)], axis=1)
    full_ref[:, :NB] = lead_ref[...]
    full_ref[:, NB:COLS] = select_rows(onehot_of(plan_ref[160:288, :1], 256), got)

    def store(index, value):
        @pl.when(index != panel)
        def _():
            spot = COLS // NB + jnp.where(index < panel, index, index - 1)
            full_ref[:, lane_block(spot)] = value

    put_columns(blocks, slice(0, NB), store)
    copies = [
        pltpu.make_async_copy(full_ref, send_ref.at[n], sems.at[n]) for n in range(4)
    ]
    for copy in copies:
        copy.start()
    slot = plan_ref[288:544, :1]
    moved = select_rows(onehot_of(slot, 64), moved_part(got_ref, 0))
    rows_ref[...] = jnp.where(slot >= 0, moved, block_ref[...])
    for copy in copies:
        copy.wait()


def put_columns(block_refs, rows, store):
    kind = lax.axis_index("pcol") & 3
    for n, ref in enumerate(block_refs):
        store(kind ^ n, ref[rows, :])


def lane_block(index):
    return pl.ds(pl.multiple_of(index * NB, NB), NB)


def own_rows_kernel(plan_ref, rows_ref, got_ref, a_ref, out_ref):
    slot = plan_ref[288:544, :1]
    moved = jnp.concatenate([moved_part(got_ref, c) for c in range(1, COLS // NB)], axis=1)
    moved = select_rows(onehot_of(slot, 64), moved)
    out_ref[:, :NB] = rows_ref[...]
    out_ref[:, NB:] = jnp.where(slot >= 0, moved, a_ref[:, NB:])


def factor_kernel(
    top_ref, right_ref, lower_ref, upper_ref, left0_ref, left1_ref, left2_ref, left3_ref,
    result_ref, z_ref, y_ref, m_ref, u_ref, d_ref, out_ref, sems,
):
    prow = lax.axis_index("prow")
    pcol = lax.axis_index("pcol")
    fetches = []
    for n, ref in enumerate((left0_ref, left1_ref, left2_ref, left3_ref)):
        target = z_ref.at[TOP : TOP + ROWS, lane_block((pcol & 3) ^ n)]
        fetches.append(pltpu.make_async_copy(ref, target, sems.at[n]))
    fetches.append(pltpu.make_async_copy(right_ref, out_ref, sems.at[4]))
    for fetch in fetches:
        fetch.start()
    for k in range(PANELS):
        rows = slice(k * NB, k * NB + NB)
        for spot in range(PANELS - 1):
            block = spot if spot < k else spot + 1
            z_ref[rows, block * NB : block * NB + NB] = top_ref[
                rows, COLS + spot * NB : COLS + spot * NB + NB
            ]
    for k in range(PANELS):
        s = k * NB
        e = s + NB
        before = top_ref if k == 0 else y_ref
        lh, ll = split2(lower_ref[k])
        l3 = jnp.concatenate([lh, ll, lh], axis=1)
        if e < TOP:
            bh, bl = split2(z_ref[s:e, e:])
            corner = mm(l3, jnp.concatenate([bh, bh, bl], axis=0))
            z_ref[s:e, e:] = corner
            uh, ul = split2(corner)
            corner3 = jnp.concatenate([uh, uh, ul], axis=0)
        d_ref[s:e, :] = before[s:e, :NB]
        bh, bl = split2(before[s:e, :COLS])
        upper_rows = mm(l3, jnp.concatenate([bh, bh, bl], axis=0))
        y_ref[s:e, :] = upper_rows
        uh, ul = split2(upper_rows)
        u3 = jnp.concatenate([uh, uh, ul], axis=0)
        u_ref[3 * s : 3 * e, :] = u3
        if k == 0:
            for fetch in fetches[:4]:
                fetch.wait()
        multipliers = dot3(z_ref[e:, s:e], upper_ref[k])
        z_ref[e:, s:e] = multipliers
        mh, ml = split2(multipliers)
        m3 = jnp.concatenate([mh, ml, mh], axis=1)
        m_ref[:, 3 * s : 3 * e] = m3[TOP - e :]
        if e < TOP:
            z_ref[e:, e:] = z_ref[e:, e:] - mm(m3, corner3)
            y_ref[e:TOP, :] = before[e:TOP, :COLS] - mm(m3[: TOP - e], u3)
    fetches[4].wait()
    out_ref[...] = out_ref[...] - mm(m_ref[...], u_ref[...])
    panel_cols = lane_block(pcol & 3)
    top_rows = pl.ds(pl.multiple_of((prow & 3) * NB, NB), NB)

    @pl.when(pcol < PANELS)
    def _():
        out_ref[:, :NB] = z_ref[TOP:, panel_cols]

    @pl.when(prow < PANELS)
    def _():
        out_ref[:NB, :] = y_ref[top_rows, :]

    @pl.when((prow < PANELS) & (pcol < PANELS))
    def _():
        out_ref[:NB, :NB] = jnp.where(
            prow == pcol, d_ref[top_rows, :], z_ref[top_rows, panel_cols]
        )

    copy = pltpu.make_async_copy(out_ref, result_ref, sems.at[5])
    copy.start()
    copy.wait()


def kernel_call(body, shapes, scratch=(), out=None, limit=None):
    def call(*args):
        return pl.pallas_call(
            body,
            in_specs=[VMEM] * len(args),
            out_specs=out or [VMEM] * len(shapes),
            out_shape=[jax.ShapeDtypeStruct(shape, kind) for shape, kind in shapes],
            scratch_shapes=list(scratch),
            compiler_params=pltpu.CompilerParams(vmem_limit_bytes=limit or KERNEL_VMEM),
        )(*args)

    return call


def factor(top, right, lower_inverse, upper_inverse, *left):
    right, *left = [
        pltpu.with_memory_space_constraint(value, pltpu.HBM) for value in (right, *left)
    ]
    args = (top, right, lower_inverse, upper_inverse, *left)
    result = pl.pallas_call(
        factor_kernel,
        in_specs=[VMEM, HBM, VMEM, VMEM] + [HBM] * 4,
        out_specs=HBM,
        out_shape=jax.ShapeDtypeStruct((ROWS, COLS), F32),
        scratch_shapes=[
            pltpu.VMEM((TOP + ROWS, TOP), F32),
            pltpu.VMEM((TOP, COLS), F32),
            pltpu.VMEM((ROWS, 3 * TOP), BF),
            pltpu.VMEM((3 * TOP, COLS), BF),
            pltpu.VMEM((TOP, NB), F32),
            pltpu.VMEM((ROWS, COLS), F32),
            pltpu.SemaphoreType.DMA((6,)),
        ],
        compiler_params=pltpu.CompilerParams(vmem_limit_bytes=FACTOR_VMEM),
    )(*args)
    return pltpu.with_memory_space_constraint(result, pltpu.HBM)


def along(value, groups):
    return lax.all_to_all(value, "prow", 0, 0, axis_index_groups=groups)


def slotted(send, leaving, block, plan, matrix, lower_inverse, upper_inverse):
    pcol = lax.axis_index("pcol")
    got = along(send.reshape(4, 16, COLS), X_GROUPS)
    held = [leaving[0]]
    for n in range(1, 4):
        pairs = [(k, 8 * n + k) for k in range(PANELS)]
        held.append(lax.ppermute(leaving[n], "prow", pairs))
    first, rest = kernel_call(turn_kernel, [((8, 32, NB), F32), ((32, REST), F32)])(
        plan, got.reshape(64, COLS)
    )
    first = along(first, Z_GROUPS)
    (rest,) = kernel_call(join_kernel, [((8, 256, NB), F32)])(plan, rest, *held)
    rest = along(rest, Z_GROUPS)
    (lead,) = kernel_call(lead_kernel, [((NB, NB), F32)])(plan, first.reshape(256, NB))
    ends = spread_start(lead)
    late = spread_rest(lead, *ends, pcol)
    send, rows = kernel_call(
        panel_kernel,
        [((4, NB, WIDE - NB), F32), ((ROWS, NB), F32)],
        [pltpu.VMEM((NB, WIDE - NB), F32), pltpu.SemaphoreType.DMA((4,))],
        [HBM, VMEM],
        60 << 20,
    )(plan, lead, rest, block, *late)
    top = along(send, X_GROUPS).reshape(TOP, WIDE - NB)
    ends = spread_start(rows)
    left = spread_rest(rows, *ends, pcol)
    (right,) = kernel_call(own_rows_kernel, [((ROWS, COLS), F32)])(plan, rows, rest, matrix)
    return factor(top, right, lower_inverse, upper_inverse, *left)


def dense_rows_kernel(
    origin_ref, gathered_ref, a_ref, own_ref, block0_ref, block1_ref, block2_ref, block3_ref,
    top_ref, right_ref,
):
    def store_corner(index, value):
        for k in range(PANELS):

            @pl.when(index != k)
            def _():
                spot = lane_block(COLS // NB + jnp.where(index < k, index, index - 1))
                top_ref[k * NB : k * NB + NB, spot] = value[k * NB : k * NB + NB]

    put_columns((block0_ref, block1_ref, block2_ref, block3_ref), slice(0, TOP), store_corner)
    top_ref[:, :NB] = own_ref[:TOP, :]
    right_ref[:, :NB] = own_ref[TOP:, :]
    for unit in range(PROW):
        top_ref[unit * 16 : unit * 16 + 16, NB:COLS] = gathered_ref[unit * 32 : unit * 32 + 16, :]
    origin = origin_ref[:, :1]

    @pl.loop(0, REST // NB)
    def _(c):
        right_ref[:, lane_block(c + 1)] = moved_rows(
            origin, gathered_ref[:, lane_block(c)], a_ref[:, lane_block(c + 1)]
        )


def dense(pivots, matrix, lower_inverse, upper_inverse):
    prow = lax.axis_index("prow")
    pcol = lax.axis_index("pcol")
    place = jnp.stack([prow, pcol]).astype(jnp.int32)
    picked_first, picked_rest, origin = pl.pallas_call(
        pick_kernel,
        in_specs=[SMEM, VMEM, VMEM, VMEM],
        out_specs=[VMEM] * 3,
        out_shape=[
            jax.ShapeDtypeStruct((TOP, NB), F32),
            jax.ShapeDtypeStruct((TOP, REST), F32),
            jax.ShapeDtypeStruct((ROWS, NB), jnp.int32),
        ],
    )(place, pivots.reshape(PANELS, NB), pivots.reshape(TOP, 1), matrix)
    gathered_first = exchange_first(picked_first, matrix[:NB, :NB])
    (own,) = kernel_call(column_kernel, [((TOP + ROWS, NB), F32)])(origin, gathered_first, matrix)
    blocks = spread_columns(own, pcol)
    gathered_rest = exchange_rest(picked_rest, matrix[:NB, NB:])
    top, right = kernel_call(
        dense_rows_kernel, [((TOP, WIDE - NB), F32), ((ROWS, COLS), F32)]
    )(origin, gathered_rest, matrix, own, *blocks)
    left = [block[TOP:] for block in blocks]
    return factor(top, right, lower_inverse, upper_inverse, *left)


def per_device(matrix, pivots, lower_inverse, upper_inverse):
    send, *leaving, block, plan, over = kernel_call(
        plan_kernel,
        [((64, COLS), F32)]
        + [((48, COLS), F32)] * 4
        + [((ROWS, NB), F32), ((544, NB), jnp.int32), ((8, NB), jnp.int32)],
        [pltpu.VMEM((8, NB), jnp.int32), pltpu.VMEM((8, NB), jnp.int32)],
    )(pivots.reshape(PANELS, NB), matrix)
    return lax.cond(
        over[0, 0] <= 0,
        lambda: slotted(send, leaving, block, plan, matrix, lower_inverse, upper_inverse),
        lambda: dense(pivots, matrix, lower_inverse, upper_inverse),
    )


def solution(mesh):
    in_specs = (P("prow", "pcol"), P(), P(), P())
    out_specs = P("prow", "pcol")
    return jax.shard_map(
        per_device, mesh=mesh, in_specs=in_specs, out_specs=out_specs, check_vma=False
    )
```
